32 devices in a mesh: leaf: 8 (over y, x, core), probe: 4 (over z).
Axes of the slice: x: 2, y: 2, z: 4, core: 2. Of those that a mesh axis runs over, the one named last changes fastest.
Arguments:
- leaf_blocks: float32 [8192, 1024], P('leaf'), may hold values from -0.1875 to 0.1875
- block_mask: int32 [8, 8, 8], P('leaf'), may hold values 0 or 1
- row_factor_stack: float32 [3, 8192, 128], P(None, 'leaf'), may hold values from -0.5 to 0.5
- column_factor_stack: float32 [3, 8192, 128], P(None, 'leaf'), may hold values from -0.0625 to 0.0625
- probes: float32 [8192, 1024], P('leaf', 'probe'), may hold values from -6 to 6
Outputs:
- applied: float32 [8192, 1024], P('leaf', 'probe')
- probe_gram: float32 [1024, 1024], P('leaf', 'probe')
The draws below stay inside these ranges and needn't reach their ends.
All inputs are finite; a program needn't handle non-finite values. No bound on the sum of `block_mask` on one device may be relied on, other than what follows from the above.
Results may differ from the reference program's by a relative error of at most 0.0001.
Values sent between devices are 32-bit elements; how exact they have to be, the bound alone decides.
A program may use at most 64 MiB of HBM per device.

```python
import jax
import jax.numpy as jnp
from jax import lax

LEAF_PTS = 1024
MB = 8
RANK = 128
PROBES = 1024
LEVELS = 3
POINTS = 8192
N_LEAF = 8


def touch_ends(drawn, key, smallest, high):
    longest = drawn.shape.index(max(drawn.shape))
    spots = []
    for shift in (0, 1):
        where = [jax.random.randint(jax.random.fold_in(key, axis), (), 0, length) for axis, length in enumerate(drawn.shape)]
        where[longest] = (where[longest] + shift) % drawn.shape[longest]
        spots.append(tuple(where))
    return drawn.at[spots[0]].set(smallest).at[spots[1]].set(high)


def block_scale(key, dims, shards, least, largest):
    loudness, own = 1.0, jax.random.fold_in(key, 6)
    for dim, blocks in shards:
        steps = jnp.exp(jax.random.uniform(jax.random.fold_in(own, dim), (blocks,), jnp.float32, least / len(shards), largest / len(shards)))
        loudness = loudness * jnp.repeat(steps, dims[dim] // blocks).reshape([-1 if axis == dim else 1 for axis in range(len(dims))])
    return loudness


def normal_values(key, dims, deviation, bound, cuts=(), kind=jnp.bfloat16):
    values = jax.random.normal(key, dims, jnp.float32) * deviation
    if len(cuts) > 0:
        values = block_scale(key, dims, cuts, -0.22, 0.18) * values
    return jnp.clip(values, min=-bound, max=bound).astype(kind)


def setup_inputs(seed: int = 0) -> dict:
    keys = jax.random.split(jax.random.key(seed), 6)
    leaf_blocks = normal_values(keys[0], (POINTS, LEAF_PTS), LEAF_PTS ** -0.5, 0.1875, ((0, 8),), jnp.float32)
    block_mask = touch_ends((jax.random.randint(keys[1], (N_LEAF, MB, MB), 0, 4) < 3).astype(jnp.int32), jax.random.fold_in(keys[1], 1), 0, 1)
    row_factor_stack = normal_values(keys[2], (LEVELS, POINTS, RANK), RANK ** -0.5, 0.5, ((1, 8),), jnp.float32)
    column_factor_stack = normal_values(keys[3], (LEVELS, POINTS, RANK), POINTS ** -0.5, 0.0625, ((1, 8),), jnp.float32)
    probes = normal_values(keys[4], (POINTS, PROBES), 1.0, 6.0, ((0, 8), (1, 4)), jnp.float32)
    return {"leaf_blocks": leaf_blocks, "block_mask": block_mask, "row_factor_stack": row_factor_stack, "column_factor_stack": column_factor_stack, "probes": probes}


def leaf_product(inputs):
    block, weights, columns = inputs
    block_span_width = LEAF_PTS // MB
    spread = jnp.repeat(jnp.repeat(weights.astype(jnp.float32), block_span_width, 0), block_span_width, 1)
    return jnp.dot(block * spread, columns, precision=lax.Precision.HIGHEST, preferred_element_type=jnp.float32)


def reference(leaf_blocks, block_mask, row_factor_stack, column_factor_stack, probes):
    block_list = leaf_blocks.reshape(N_LEAF, LEAF_PTS, LEAF_PTS)
    columns = probes.reshape(N_LEAF, LEAF_PTS, PROBES)
    applied = lax.map(leaf_product, (block_list, block_mask, columns)).reshape(POINTS, PROBES)
    for level in range(LEVELS):
        width = LEAF_PTS * 2 ** level
        cluster_groups = POINTS // width
        grouped = probes.reshape(cluster_groups, width, PROBES)
        right_part = column_factor_stack[level].reshape(cluster_groups, width, RANK)
        probe_projected = jnp.einsum("bsr,bsp->brp", right_part, grouped, precision=lax.Precision.HIGHEST)
        swapped = probe_projected.reshape(cluster_groups // 2, 2, RANK, PROBES)[:, ::-1].reshape(cluster_groups, RANK, PROBES)
        left_part = row_factor_stack[level].reshape(cluster_groups, width, RANK)
        applied = applied + jnp.einsum("bsr,brp->bsp", left_part, swapped, precision=lax.Precision.HIGHEST).reshape(POINTS, PROBES)
    probe_gram = jnp.dot(applied.T, applied, precision=lax.Precision.HIGHEST, preferred_element_type=jnp.float32) / POINTS
    return applied, probe_gram
```

```python
import functools

import jax
import jax.numpy as jnp
from jax import lax
from jax.experimental import pallas as pl
from jax.experimental.pallas import tpu as pltpu
from jax.sharding import PartitionSpec as P

MESH = pl.DeviceIdType.MESH
CONTRACT_ROWS = (((0,), (0,)), ((), ()))
PLAIN = (((1,), (0,)), ((), ()))


def split(value):
    high = value.astype(jnp.bfloat16)
    return high, (value - high.astype(jnp.float32)).astype(jnp.bfloat16)


def dot3(left, right, dims):
    (lh, ll), (rh, rl) = left, right
    dot = functools.partial(lax.dot_general, dimension_numbers=dims, preferred_element_type=jnp.float32)
    return dot(lh, rh) + (dot(lh, rl) + dot(ll, rh))


def ring_kernel(
    n_leaf, n_probe, pieces,
    mask, block_hbm, row_hbm, col_hbm, probe_hbm, app_hbm, gram_ref,
    block, row, col, probe, probe_h, probe_l, own, swap, sib_h, sib_l,
    app, app_h, app_l, got, part, shares, total, extra, turned, kept_h, kept_l,
    load_sem, out_sem, swap_send, swap_recv, right_send, right_recv, left_send, left_recv,
    share_send, share_recv, extra_send, extra_recv,
):
    depth, rank = row.shape[0], row.shape[2]
    points, width = app.shape
    side = mask.shape[1]
    span = points // side
    half = points // 2
    piece = half // pieces
    leaf, z = lax.axis_index("leaf"), lax.axis_index("probe")
    slab = n_probe * width // n_leaf
    fan = n_leaf // n_probe
    a, b = leaf // fan, leaf % fan
    last = n_probe - 1
    ends = n_probe > 2

    loads = [
        pltpu.make_async_copy(source, target, load_sem.at[i])
        for i, (source, target) in enumerate(
            ((probe_hbm, probe), (col_hbm, col), (block_hbm, block), (row_hbm, row))
        )
    ]
    loads[0].start()
    loads[1].start()

    barrier = pltpu.get_barrier_semaphore()

    @pl.loop(1, n_leaf)
    def _(k):
        pl.semaphore_signal(
            barrier, inc=1, device_id={"leaf": (leaf + k) % n_leaf, "probe": z}, device_id_type=MESH
        )

    @pl.when(z > 0)
    def _():
        pl.semaphore_signal(barrier, inc=1, device_id={"leaf": leaf, "probe": z - 1}, device_id_type=MESH)

    @pl.when(z < last)
    def _():
        pl.semaphore_signal(barrier, inc=1, device_id={"leaf": leaf, "probe": z + 1}, device_id_type=MESH)

    @pl.when(a != z)
    def _():
        @pl.loop(0, fan)
        def _(c):
            pl.semaphore_signal(
                barrier, inc=1, device_id={"leaf": z * fan + c, "probe": a}, device_id_type=MESH
            )

    loads[0].wait()
    ph, plo = split(probe[...])
    probe_h[...] = ph
    probe_l[...] = plo
    loads[1].wait()
    loads[2].start()
    loads[3].start()
    columns = jnp.concatenate([col[level] for level in range(depth)], axis=1)
    own[...] = dot3(split(columns), (probe_h[...], probe_l[...]), CONTRACT_ROWS).reshape(own.shape)

    peers = n_leaf - 1 + jnp.where(z > 0, 1, 0) + jnp.where(z < last, 1, 0) + jnp.where(a != z, fan, 0)
    pl.semaphore_wait(barrier, peers)

    def exchange(step):
        away = 2**step
        other = leaf + (1 - 2 * ((leaf // away) % 2)) * away
        start = sum(depth - s for s in range(step))
        return start, pltpu.make_async_remote_copy(
            src_ref=own.at[pl.ds(step, depth - step)],
            dst_ref=swap.at[pl.ds(start, depth - step)],
            send_sem=swap_send.at[step],
            recv_sem=swap_recv.at[step],
            device_id={"leaf": other, "probe": z},
            device_id_type=MESH,
        )

    def near(which):
        @pl.loop(0, side // 2)
        def _(i):
            line = which * (side // 2) + i
            rows = pl.ds(pl.multiple_of(line * span, span), span)
            strips = [
                block[rows, j * span : (j + 1) * span] * mask[0, line, j].astype(jnp.float32)
                for j in range(side)
            ]
            into = pl.ds(pl.multiple_of(i * span, span), span)
            kept_h[into, :], kept_l[into, :] = split(jnp.concatenate(strips, axis=1))

        app[which * half : (which + 1) * half, :] = dot3(
            (kept_h[...], kept_l[...]), (probe_h[...], probe_l[...]), PLAIN
        )

    for step in range(depth):
        start, copy = exchange(step)
        copy.start()
        if step == 0:
            loads[2].wait()
        for which in range(2):
            if step == min(which, depth - 1):
                near(which)
        copy.wait()
        sib_h[step * rank : (step + 1) * rank, :], sib_l[step * rank : (step + 1) * rank, :] = split(
            swap[start]
        )
        for level in range(step + 1, depth):
            own[level] = own[level] + swap[start + level - step]

    def ship(source, to, slot, begin, send, recv):
        rows = pl.ds(pl.multiple_of(begin, piece), piece)
        return pltpu.make_async_remote_copy(
            src_ref=source.at[rows] if source is app else source.at[slot, rows],
            dst_ref=got.at[slot, rows],
            send_sem=send.at[slot, begin // piece],
            recv_sem=recv.at[slot, begin // piece],
            device_id={"leaf": leaf, "probe": to},
            device_id_type=MESH,
        )

    def rightward(source, slot, begin):
        return ship(source, jnp.minimum(z + 1, last), slot, begin, right_send, right_recv)

    def leftward(source, slot, begin):
        return ship(source, jnp.maximum(z - 1, 0), slot, begin, left_send, left_recv)

    loads[3].wait()
    sends_right = (z < last - 1) if ends else (z < last)
    sends_left = (z > 1) if ends else (z > 0)

    def far(which):
        rows = slice(which * half, (which + 1) * half)
        factors = jnp.concatenate([row[level, rows, :] for level in range(depth)], axis=1)
        value = app[rows, :] + dot3(split(factors), (sib_h[...], sib_l[...]), PLAIN)
        app[rows, :] = value
        app_h[rows, :], app_l[rows, :] = split(value)

    far(0)

    @pl.when(sends_right)
    def _():
        @pl.loop(0, pieces)
        def _(c):
            rightward(app, z, c * piece).start()

    far(1)

    @pl.when(sends_left)
    def _():
        @pl.loop(0, pieces)
        def _(c):
            leftward(app, z, half + c * piece).start()

    if ends:
        @pl.loop(0, pieces)
        def _(c):
            @pl.when(z == 0)
            def _():
                rightward(app, z, half + c * piece).start()

            @pl.when(z == last)
            def _():
                leftward(app, z, c * piece).start()

    keep = pltpu.make_async_copy(app, app_hbm, out_sem)
    keep.start()

    def gram(slot, source, begin, fresh):
        into = pl.ds(pl.multiple_of(slot * width, width), width)
        rows = pl.ds(pl.multiple_of(begin, half), half)
        here = (app_h[rows, :], app_l[rows, :])
        there = here if source is None else split(source[slot, rows, :])
        value = dot3(there, here, CONTRACT_ROWS)
        part[into, :] = value if fresh else part[into, :] + value

    def share(k):
        to = (leaf + k) % n_leaf
        return pltpu.make_async_remote_copy(
            src_ref=part.at[pl.ds(pl.multiple_of(to * slab, slab), slab)],
            dst_ref=shares.at[k],
            send_sem=share_send.at[k],
            recv_sem=share_recv.at[k],
            device_id={"leaf": to, "probe": z},
            device_id_type=MESH,
        )

    def give(slot):
        @pl.loop(0, fan)
        def _(c):
            to = slot * fan + c

            @pl.when(to != leaf)
            def _():
                share((to - leaf + n_leaf) % n_leaf).start()

    part[...] = jnp.zeros_like(part)

    @pl.loop(0, 2)
    def _(h):
        gram(z, None, h * half, False)

    give(z)

    @pl.loop(1, n_probe)
    def _(d):
        from_left = (z - d >= 0) & ((z < last) | (d > 1) | (not ends))
        from_right = (z + d <= last) & ((z > 0) | (d > 1) | (not ends))
        low_slot, high_slot = jnp.maximum(z - d, 0), jnp.minimum(z + d, last)

        @pl.loop(0, pieces)
        def _(c):
            up, low = c * piece, half + c * piece

            @pl.when(from_left)
            def _():
                rightward(got, low_slot, up).wait_recv()

                @pl.when(z < last)
                def _():
                    rightward(got, low_slot, up).start()

            @pl.when(from_right)
            def _():
                leftward(got, high_slot, low).wait_recv()

                @pl.when(z > 0)
                def _():
                    leftward(got, high_slot, low).start()

        @pl.loop(0, 2)
        def _(h):
            @pl.when(jnp.where(h == 0, from_left, from_right))
            def _():
                slot = jnp.where(h == 0, low_slot, high_slot)
                gram(slot, got, h * half, False)
                whole = (d > 1) | jnp.where(h == 0, z != 1, z != last - 1) | (not ends)

                @pl.when(whole)
                def _():
                    give(slot)

    if ends:
        at_low, at_high = z == 1, z == last - 1

        @pl.loop(0, pieces)
        def _(c):
            @pl.when(at_low)
            def _():
                rightward(got, z - 1, half + c * piece).wait_recv()

            @pl.when(at_high)
            def _():
                leftward(got, z + 1, c * piece).wait_recv()

        @pl.loop(0, 2)
        def _(h):
            @pl.when(jnp.where(h == 0, at_high, at_low))
            def _():
                slot = jnp.where(h == 0, jnp.minimum(z + 1, last), jnp.maximum(z - 1, 0))
                gram(slot, got, h * half, False)
                give(slot)

    total[...] = part[pl.ds(pl.multiple_of(leaf * slab, slab), slab), :]

    def holds(slot):
        return (not ends) | (((z > 0) | (slot != 1)) & ((z < last) | (slot != last - 1)))

    @pl.when(holds(a))
    def _():
        @pl.loop(1, n_leaf)
        def _(k):
            share(k).wait_recv()
            total[...] = total[...] + shares[k]

    scale = 1.0 / (points * n_leaf)

    tile = extra.shape[1]

    def trade(c, at):
        return pltpu.make_async_remote_copy(
            src_ref=total if tile == width else total.at[:, pl.ds(pl.multiple_of(c * tile, tile), tile)],
            dst_ref=extra.at[pl.ds(pl.multiple_of(at * slab, slab), slab)],
            send_sem=extra_send.at[c],
            recv_sem=extra_recv.at[at],
            device_id={"leaf": z * fan + c, "probe": a},
            device_id_type=MESH,
        )

    @pl.when(a != z)
    def _():
        @pl.loop(0, fan)
        def _(c):
            trade(c, b).start()

        @pl.loop(0, fan)
        def _(c):
            trade(c, c).wait_recv()

        turned[...] = extra[...].T
        skip = 0 if tile == slab else pl.multiple_of(b * slab, slab)
        gram_ref[...] = (total[...] + turned[pl.ds(skip, slab), :]) * scale

        @pl.loop(0, fan)
        def _(c):
            trade(c, b).wait_send()

    @pl.when(a == z)
    def _():
        gram_ref[...] = total[...] * scale

    @pl.loop(0, pieces)
    def _(c):
        up, low = c * piece, half + c * piece

        @pl.when(sends_right)
        def _():
            rightward(app, z, up).wait_send()

        @pl.when(sends_left)
        def _():
            leftward(app, z, low).wait_send()

        if ends:

            @pl.when(z == 0)
            def _():
                rightward(app, z, low).wait_send()

            @pl.when(z == last)
            def _():
                leftward(app, z, up).wait_send()

        @pl.loop(1, n_probe)
        def _(d):
            @pl.when((z - d >= 0) & (z < last))
            def _():
                rightward(got, jnp.maximum(z - d, 0), up).wait_send()

            @pl.when((z + d <= last) & (z > 0))
            def _():
                leftward(got, jnp.minimum(z + d, last), low).wait_send()

    @pl.loop(1, n_leaf)
    def _(k):
        @pl.when(holds(((leaf + k) % n_leaf) // fan))
        def _():
            share(k).wait_send()

    keep.wait()


def ring(n_leaf, n_probe, leaf_blocks, block_mask, row_factor_stack, column_factor_stack, probes):
    depth, points, rank = row_factor_stack.shape
    width = probes.shape[1]
    slab = n_probe * width // n_leaf
    fan = n_leaf // n_probe
    pieces = 4
    tile = slab if slab % 128 == 0 else width
    f32, bf16 = jnp.float32, jnp.bfloat16
    dma = pltpu.SemaphoreType.DMA
    hbm = pl.BlockSpec(memory_space=pltpu.HBM)
    return pl.pallas_call(
        functools.partial(ring_kernel, n_leaf, n_probe, pieces),
        out_shape=(
            jax.ShapeDtypeStruct((points, width), f32),
            jax.ShapeDtypeStruct((slab, width), f32),
        ),
        in_specs=[pl.BlockSpec(memory_space=pltpu.SMEM), hbm, hbm, hbm, hbm],
        out_specs=(hbm, pl.BlockSpec(memory_space=pltpu.VMEM)),
        scratch_shapes=[
            pltpu.VMEM((points, points), f32),
            pltpu.VMEM((depth, points, rank), f32),
            pltpu.VMEM((depth, points, rank), f32),
            pltpu.VMEM((points, width), f32),
            pltpu.VMEM((points, width), bf16),
            pltpu.VMEM((points, width), bf16),
            pltpu.VMEM((depth, rank, width), f32),
            pltpu.VMEM((depth * (depth + 1) // 2, rank, width), f32),
            pltpu.VMEM((depth * rank, width), bf16),
            pltpu.VMEM((depth * rank, width), bf16),
            pltpu.VMEM((points, width), f32),
            pltpu.VMEM((points, width), bf16),
            pltpu.VMEM((points, width), bf16),
            pltpu.VMEM((n_probe, points, width), f32),
            pltpu.VMEM((n_probe * width, width), f32),
            pltpu.VMEM((n_leaf, slab, width), f32),
            pltpu.VMEM((slab, width), f32),
            pltpu.VMEM((width, tile), f32),
            pltpu.VMEM((tile, width), f32),
            pltpu.VMEM((points // 2, points), bf16),
            pltpu.VMEM((points // 2, points), bf16),
            dma((4,)),
            dma,
            dma((depth,)),
            dma((depth,)),
            dma((n_probe, 2 * pieces)),
            dma((n_probe, 2 * pieces)),
            dma((n_probe, 2 * pieces)),
            dma((n_probe, 2 * pieces)),
            dma((n_leaf,)),
            dma((n_leaf,)),
            dma((fan,)),
            dma((fan,)),
        ],
        compiler_params=pltpu.CompilerParams(
            collective_id=0, has_side_effects=True, vmem_limit_bytes=67043328
        ),
    )(block_mask, leaf_blocks, row_factor_stack, column_factor_stack, probes)


def hub_kernel(
    n_leaf, n_probe, parts,
    mask, block_hbm, row_hbm, col_hbm, probe_hbm, app_hbm, gram_ref,
    block, row, col, probe, probe_h, probe_l, block_h, block_l, row_h, row_l,
    own, pair_in, pair_sum, group_in, sib, sib_h, sib_l, app, app_h, app_l, near_other,
    got_probe, got_sib, got_turned, turned, pairs, arrived, summed, straight, crossed, diag, shares,
    load_sem, out_sem, pair_send, pair_recv, group_send, group_recv, half_send, half_recv,
    probe_send, probe_recv, sib_send, sib_recv, turned_send, turned_recv,
    part_send, part_recv, straight_send, straight_recv, crossed_send, crossed_recv, share_send, share_recv,
):
    depth, rank = row.shape[0], row.shape[2]
    points, width = app.shape
    side = mask.shape[1]
    span = points // side
    half = points // 2
    leaf, z = lax.axis_index("leaf"), lax.axis_index("probe")
    slab = n_probe * width // n_leaf
    fan = n_leaf // n_probe
    chunk = width // parts
    last = n_probe - 1
    h = n_probe // 2
    teams = n_leaf // 2
    split_rank = rank // 2
    flow = leaf % 2
    team = leaf // 2
    mate = leaf + 1 - 2 * flow
    a, b = leaf // fan, leaf % fan

    def along(direction, position):
        return jnp.where(direction == 0, position, last - position)

    q = along(flow, z)
    is_hub = q == h
    hub = along(flow, h)

    def remote(src, dst, send, recv, to_leaf, to_z):
        return pltpu.make_async_remote_copy(
            src_ref=src, dst_ref=dst, send_sem=send, recv_sem=recv,
            device_id={"leaf": to_leaf, "probe": to_z}, device_id_type=MESH,
        )

    loads = [
        pltpu.make_async_copy(source, target, load_sem.at[i])
        for i, (source, target) in enumerate(
            ((probe_hbm, probe), (col_hbm, col), (block_hbm, block), (row_hbm, row))
        )
    ]
    loads[0].start()
    loads[1].start()

    barrier = pltpu.get_barrier_semaphore()
    everyone = n_leaf * n_probe
    me = leaf * n_probe + z

    @pl.loop(1, everyone)
    def _(k):
        to = (me + k) % everyone
        pl.semaphore_signal(
            barrier, inc=1, device_id={"leaf": to // n_probe, "probe": to % n_probe}, device_id_type=MESH
        )

    loads[2].start()
    loads[3].start()
    loads[0].wait()
    ph, plo = split(probe[...])
    probe_h[...] = ph
    probe_l[...] = plo
    loads[1].wait()
    columns = jnp.concatenate([col[level] for level in range(depth)], axis=1)
    own[...] = dot3(split(columns), (probe_h[...], probe_l[...]), CONTRACT_ROWS).reshape(own.shape)
    pl.semaphore_wait(barrier, everyone - 1)

    sides = [k for k in range(n_probe) if abs(k - h) == 1]
    distant = [k for k in range(n_probe) if abs(k - h) > 1]
    is_side = jnp.abs(q - h) == 1
    place = jnp.where(q > h, 1, 0)

    def give_probe(slot):
        return remote(probe, got_probe.at[slot], probe_send, probe_recv.at[slot], leaf, hub)

    @pl.when(is_side)
    def _():
        give_probe(place).start()

    first_level = remote(own.at[0], sib.at[0], pair_send.at[0], pair_recv.at[0], mate, z)
    upper_levels = remote(
        own.at[pl.ds(1, depth - 1), pl.ds(pl.multiple_of((1 - flow) * split_rank, split_rank), split_rank)],
        pair_in, pair_send.at[1], pair_recv.at[1], mate, z,
    )
    upper_levels.start()
    first_level.start()
    mine = pl.ds(pl.multiple_of(flow * split_rank, split_rank), split_rank)

    def to_group(level, k):
        members = 2 ** (level - 1)
        base = leaf - leaf % 2**level + (1 - 2 * ((leaf // 2**level) % 2)) * 2**level
        from_slot = members - 1 + (leaf % 2**level) // 2
        return remote(
            pair_sum.at[level - 1], group_in.at[from_slot],
            group_send.at[members - 1 + k], group_recv.at[from_slot], base + 2 * k + flow, z,
        )

    def from_group(level, k):
        members = 2 ** (level - 1)
        return remote(
            pair_sum.at[level - 1], group_in.at[members - 1 + k],
            group_send.at[members - 1 + k], group_recv.at[members - 1 + k], mate, z,
        )

    upper_levels.wait_recv()
    for level in range(1, depth):
        pair_sum[level - 1] = own[level, mine, :] + pair_in[level - 1]
    for level in reversed(range(1, depth)):
        @pl.loop(0, 2 ** (level - 1))
        def _(k):
            to_group(level, k).start()

    loads[2].wait()

    @pl.loop(0, side)
    def _(line):
        rows = pl.ds(pl.multiple_of(line * span, span), span)
        strips = [
            block[rows, j * span : (j + 1) * span] * mask[0, line, j].astype(jnp.float32)
            for j in range(side)
        ]
        block_h[rows, :], block_l[rows, :] = split(jnp.concatenate(strips, axis=1))

    def near(target):
        @pl.loop(0, 2)
        def _(i):
            rows = pl.ds(pl.multiple_of(i * half, half), half)
            target[rows, :] = dot3(
                (block_h[rows, :], block_l[rows, :]), (probe_h[...], probe_l[...]), PLAIN
            )

    near(app)
    loads[3].wait()
    for level in range(depth):
        row_h[:, level * rank : (level + 1) * rank], row_l[:, level * rank : (level + 1) * rank] = split(row[level])

    for level in range(1, depth):
        @pl.loop(0, 2 ** (level - 1))
        def _(k):
            from_group(level, k).wait_recv()

        begin = 2 ** (level - 1) - 1
        value = group_in[begin]
        for k in range(1, 2 ** (level - 1)):
            value = value + group_in[begin + k]
        sib[level, mine, :] = value

    half_copy = remote(
        sib.at[pl.ds(1, depth - 1), mine], sib.at[pl.ds(1, depth - 1), mine], half_send, half_recv, mate, z
    )
    half_copy.start()
    first_level.wait_recv()
    half_copy.wait_recv()

    def give_sib(slot):
        return remote(sib, got_sib.at[slot], sib_send, sib_recv.at[slot], leaf, hub)

    @pl.when(is_side)
    def _():
        give_sib(place).start()

    def far(source, base, target, slot):
        flat = source[...].reshape(depth * rank, width)
        sib_h[...], sib_l[...] = split(flat)

        @pl.loop(0, 2)
        def _(i):
            rows = pl.ds(pl.multiple_of(i * half, half), half)
            value = base[rows, :] + dot3((row_h[rows, :], row_l[rows, :]), (sib_h[...], sib_l[...]), PLAIN)
            if target is not None:
                target[rows, :] = value
            app_h[slot, rows, :], app_l[slot, rows, :] = split(value)

    far(sib, app, app, h)
    keep = pltpu.make_async_copy(app, app_hbm, out_sem)
    keep.start()

    def rows_of(c):
        return pl.ds(pl.multiple_of(c * chunk, chunk), chunk)

    def give_turned(c):
        return remote(
            turned.at[rows_of(c)], got_turned.at[rows_of(c)], turned_send.at[c], turned_recv.at[c], leaf, hub
        )

    @pl.when(q == 0)
    def _():
        per = 128 // chunk
        for strip in range(width // 128):
            lanes = slice(strip * 128, (strip + 1) * 128)
            turned[lanes, :] = app[:, lanes].T
            for c in range(strip * per, (strip + 1) * per):
                give_turned(c).start()

    diag[...] = dot3((app_h[h], app_l[h]), (app_h[h], app_l[h]), CONTRACT_ROWS)

    def share(k):
        to = z * fan + k
        return remote(
            diag.at[pl.ds(pl.multiple_of(k * slab, slab), slab)], shares.at[leaf],
            share_send.at[k], share_recv.at[leaf], to, z,
        )

    @pl.loop(0, fan)
    def _(k):
        @pl.when(z * fan + k != leaf)
        def _():
            share(k).start()

    order = [(i, j) for j in range(n_probe) for i in range(j)]

    def part_copy(i, j, c, k):
        pid = order.index((i, j))
        return remote(
            pairs.at[pid, rows_of(c), pl.ds(pl.multiple_of(k * slab, slab), slab)],
            arrived.at[i, team, rows_of(c)],
            part_send.at[pid, c, k], part_recv.at[i, team, c], along(flow, j) * fan + k, z,
        )

    def give_part(i, j, c):
        @pl.loop(0, fan)
        def _(k):
            local = along(flow, j) * fan + k == leaf

            @pl.when(local)
            def _():
                arrived[i, team, rows_of(c), :] = pairs[
                    order.index((i, j)), rows_of(c), pl.ds(pl.multiple_of(k * slab, slab), slab)
                ]

            @pl.when(jnp.logical_not(local))
            def _():
                part_copy(i, j, c, k).start()

    @pl.when(is_hub)
    def _():
        for slot, k in enumerate(sides):
            give_probe(slot).wait_recv()
            ph, plo = split(got_probe[slot])
            probe_h[...] = ph
            probe_l[...] = plo
            near(near_other.at[slot])
        for slot, k in enumerate(sides):
            give_sib(slot).wait_recv()
            far(got_sib.at[slot], near_other.at[slot], None, k)
        for i, j in order:
            if i > 0:
                pairs[order.index((i, j))] = dot3(
                    (app_h[i], app_l[i]), (app_h[j], app_l[j]), CONTRACT_ROWS
                )

                @pl.loop(0, parts)
                def _(c):
                    give_part(i, j, c)

    def late(c):
        @pl.when(is_hub)
        def _():
            give_turned(c).wait_recv()
            piece = split(got_turned[rows_of(c), :])
            for j in range(1, n_probe):
                pairs[order.index((0, j)), rows_of(c), :] = dot3(piece, (app_h[j], app_l[j]), PLAIN)
                give_part(0, j, c)

    current = jnp.where(z == h, 0, 1)
    collects = (z == h) | (z == last - h)
    position = along(current, a)

    def arrival(i, m, c):
        return remote(
            arrived.at[i, m, rows_of(c)], arrived.at[i, m, rows_of(c)],
            part_send.at[0, c, 0], part_recv.at[i, m, c], mate, z,
        )

    lanes_here = pl.ds(pl.multiple_of(b * slab, slab), slab)
    per_slab = slab // chunk

    def send_crossed(i, c):
        return remote(
            summed.at[i, rows_of(c)], crossed.at[rows_of(c)],
            crossed_send.at[i, c], crossed_recv.at[c], leaf, along(current, i),
        )

    def send_straight(i, c):
        return remote(
            summed.at[i, rows_of(c)], straight.at[rows_of(c % per_slab), lanes_here],
            straight_send.at[i, c], straight_recv.at[c % per_slab, b],
            along(current, i) * fan + c // per_slab, a,
        )

    def collect(i, c):
        @pl.when(collects & (i < position))
        def _():
            for m in range(teams):
                @pl.when(2 * m + current != leaf)
                def _():
                    arrival(i, m, c).wait_recv()

            value = arrived[i, 0, rows_of(c), :]
            for m in range(1, teams):
                value = value + arrived[i, m, rows_of(c), :]
            summed[i, rows_of(c), :] = value
            if i == h:
                crossed[rows_of(c), :] = value
            else:
                send_crossed(i, c).start()
            send_straight(i, c).start()

    for c in range(parts - 1):
        late(c)
    for i in range(1, n_probe - 1):
        @pl.loop(0, parts)
        def _(c):
            collect(i, c)

    @pl.loop(0, parts - 2)
    def _(c):
        collect(0, c)

    late(parts - 1)

    @pl.loop(parts - 2, parts)
    def _(c):
        collect(0, c)

    scale = 1.0 / (points * n_leaf)

    @pl.when(a == z)
    def _():
        shares[leaf] = diag[pl.ds(pl.multiple_of(b * slab, slab), slab), :]

        @pl.loop(1, n_leaf)
        def _(k):
            other = (leaf + k) % n_leaf
            remote(
                shares.at[other], shares.at[other], share_send.at[0], share_recv.at[other], mate, z
            ).wait_recv()

        value = shares[0]
        for k in range(1, n_leaf):
            value = value + shares[k]
        gram_ref[...] = value * scale

    @pl.when(a != z)
    def _():
        back = jnp.where(z < a, 0, 1)

        @pl.when(along(back, h) != z)
        def _():
            @pl.loop(0, parts)
            def _(c):
                remote(
                    summed.at[0, rows_of(c)], crossed.at[rows_of(c)],
                    crossed_send.at[0, c], crossed_recv.at[c], mate, z,
                ).wait_recv()

        @pl.loop(0, per_slab * fan)
        def _(n):
            c, k = n // fan, n % fan
            remote(
                summed.at[0, rows_of(c)], straight.at[rows_of(c), pl.ds(pl.multiple_of(k * slab, slab), slab)],
                straight_send.at[0, c], straight_recv.at[c, k], mate, z,
            ).wait_recv()

        gram_ref[...] = (straight[...] + crossed[...].T) * scale

    first_level.wait_send()
    upper_levels.wait_send()
    half_copy.wait_send()
    for level in range(1, depth):
        @pl.loop(0, 2 ** (level - 1))
        def _(k):
            to_group(level, k).wait_send()

    @pl.when(is_side)
    def _():
        give_probe(place).wait_send()
        give_sib(place).wait_send()

    @pl.when(q == 0)
    def _():
        @pl.loop(0, parts)
        def _(c):
            give_turned(c).wait_send()

    @pl.loop(0, fan)
    def _(k):
        @pl.when(z * fan + k != leaf)
        def _():
            share(k).wait_send()

    @pl.when(is_hub)
    def _():
        for i, j in order:
            @pl.loop(0, parts * fan)
            def _(n):
                c, k = n // fan, n % fan

                @pl.when(along(flow, j) * fan + k != leaf)
                def _():
                    part_copy(i, j, c, k).wait_send()

    for i in range(n_probe - 1):
        @pl.when(collects & (i < position))
        def _():
            @pl.loop(0, parts)
            def _(c):
                if i != h:
                    send_crossed(i, c).wait_send()
                send_straight(i, c).wait_send()

    keep.wait()


def hub_local(n_leaf, n_probe, leaf_blocks, block_mask, row_factor_stack, column_factor_stack, probes):
    depth, points, rank = row_factor_stack.shape
    width = probes.shape[1]
    slab = n_probe * width // n_leaf
    fan = n_leaf // n_probe
    parts = 2 * width // slab
    teams = n_leaf // 2
    count = n_probe * (n_probe - 1) // 2
    f32, bf16 = jnp.float32, jnp.bfloat16
    dma = pltpu.SemaphoreType.DMA
    hbm = pl.BlockSpec(memory_space=pltpu.HBM)
    groups = 2 ** (depth - 1) - 1
    return pl.pallas_call(
        functools.partial(hub_kernel, n_leaf, n_probe, parts),
        out_shape=(
            jax.ShapeDtypeStruct((points, width), f32),
            jax.ShapeDtypeStruct((slab, width), f32),
        ),
        in_specs=[pl.BlockSpec(memory_space=pltpu.SMEM), hbm, hbm, hbm, hbm],
        out_specs=(hbm, pl.BlockSpec(memory_space=pltpu.VMEM)),
        scratch_shapes=[
            pltpu.VMEM((points, points), f32),
            pltpu.VMEM((depth, points, rank), f32),
            pltpu.VMEM((depth, points, rank), f32),
            pltpu.VMEM((points, width), f32),
            pltpu.VMEM((points, width), bf16),
            pltpu.VMEM((points, width), bf16),
            pltpu.VMEM((points, points), bf16),
            pltpu.VMEM((points, points), bf16),
            pltpu.VMEM((points, depth * rank), bf16),
            pltpu.VMEM((points, depth * rank), bf16),
            pltpu.VMEM((depth, rank, width), f32),
            pltpu.VMEM((depth - 1, rank // 2, width), f32),
            pltpu.VMEM((depth - 1, rank // 2, width), f32),
            pltpu.VMEM((groups, rank // 2, width), f32),
            pltpu.VMEM((depth, rank, width), f32),
            pltpu.VMEM((depth * rank, width), bf16),
            pltpu.VMEM((depth * rank, width), bf16),
            pltpu.VMEM((points, width), f32),
            pltpu.VMEM((n_probe, points, width), bf16),
            pltpu.VMEM((n_probe, points, width), bf16),
            pltpu.VMEM((2, points, width), f32),
            pltpu.VMEM((2, points, width), f32),
            pltpu.VMEM((2, depth, rank, width), f32),
            pltpu.VMEM((width, points), f32),
            pltpu.VMEM((width, points), f32),
            pltpu.VMEM((count, width, width), f32),
            pltpu.VMEM((n_probe - 1, teams, width, slab), f32),
            pltpu.VMEM((n_probe - 1, width, slab), f32),
            pltpu.VMEM((slab, width), f32),
            pltpu.VMEM((width, slab), f32),
            pltpu.VMEM((width, width), f32),
            pltpu.VMEM((n_leaf, slab, width), f32),
            dma((4,)),
            dma,
            dma((2,)),
            dma((2,)),
            dma((groups,)),
            dma((groups,)),
            dma,
            dma,
            dma,
            dma((2,)),
            dma,
            dma((2,)),
            dma((parts,)),
            dma((parts,)),
            dma((count, parts, fan)),
            dma((n_probe - 1, teams, parts)),
            dma((n_probe - 1, parts)),
            dma((2, fan)),
            dma((n_probe - 1, parts)),
            dma((parts,)),
            dma((fan,)),
            dma((n_leaf,)),
        ],
        compiler_params=pltpu.CompilerParams(
            collective_id=0, has_side_effects=True, vmem_limit_bytes=67043328
        ),
    )(block_mask, leaf_blocks, row_factor_stack, column_factor_stack, probes)


def local(n_leaf, n_probe, *arrays):
    width = arrays[-1].shape[1]
    whole_lanes = (n_probe * width) % (128 * n_leaf) == 0
    if n_probe == 4 and n_leaf == 2 * n_probe and whole_lanes:
        return hub_local(n_leaf, n_probe, *arrays)
    return ring(n_leaf, n_probe, *arrays)


def solution(mesh):
    return jax.shard_map(
        functools.partial(local, mesh.shape["leaf"], mesh.shape["probe"]),
        mesh=mesh,
        in_specs=(
            P("leaf", None),
            P("leaf", None, None),
            P(None, "leaf", None),
            P(None, "leaf", None),
            P("leaf", "probe"),
        ),
        out_specs=(P("leaf", "probe"), P("leaf", "probe")),
        check_vma=False,
    )
```

```python
import functools

import jax
import jax.numpy as jnp
from jax import lax
from jax.experimental import pallas as pl
from jax.experimental.pallas import tpu as pltpu
from jax.sharding import PartitionSpec as P

MESH = pl.DeviceIdType.MESH
CONTRACT_ROWS = (((0,), (0,)), ((), ()))
PLAIN = (((1,), (0,)), ((), ()))


def split(value):
    high = value.astype(jnp.bfloat16)
    return high, (value - high.astype(jnp.float32)).astype(jnp.bfloat16)


def dot3(left, right, dims):
    (lh, ll), (rh, rl) = left, right
    dot = functools.partial(lax.dot_general, dimension_numbers=dims, preferred_element_type=jnp.float32)
    return dot(lh, rh) + (dot(lh, rl) + dot(ll, rh))


def ring_kernel(
    n_leaf, n_probe, pieces,
    mask, block_hbm, row_hbm, col_hbm, probe_hbm, app_hbm, gram_ref,
    block, row, col, probe, probe_h, probe_l, own, swap, sib_h, sib_l,
    app, app_h, app_l, got, part, shares, total, extra, turned, kept_h, kept_l,
    load_sem, out_sem, swap_send, swap_recv, right_send, right_recv, left_send, left_recv,
    share_send, share_recv, extra_send, extra_recv,
):
    depth, rank = row.shape[0], row.shape[2]
    points, width = app.shape
    side = mask.shape[1]
    span = points // side
    half = points // 2
    piece = half // pieces
    leaf, z = lax.axis_index("leaf"), lax.axis_index("probe")
    slab = n_probe * width // n_leaf
    fan = n_leaf // n_probe
    a, b = leaf // fan, leaf % fan
    last = n_probe - 1
    ends = n_probe > 2

    loads = [
        pltpu.make_async_copy(source, target, load_sem.at[i])
        for i, (source, target) in enumerate(
            ((probe_hbm, probe), (col_hbm, col), (block_hbm, block), (row_hbm, row))
        )
    ]
    loads[0].start()
    loads[1].start()

    barrier = pltpu.get_barrier_semaphore()

    @pl.loop(1, n_leaf)
    def _(k):
        pl.semaphore_signal(
            barrier, inc=1, device_id={"leaf": (leaf + k) % n_leaf, "probe": z}, device_id_type=MESH
        )

    @pl.when(z > 0)
    def _():
        pl.semaphore_signal(barrier, inc=1, device_id={"leaf": leaf, "probe": z - 1}, device_id_type=MESH)

    @pl.when(z < last)
    def _():
        pl.semaphore_signal(barrier, inc=1, device_id={"leaf": leaf, "probe": z + 1}, device_id_type=MESH)

    @pl.when(a != z)
    def _():
        @pl.loop(0, fan)
        def _(c):
            pl.semaphore_signal(
                barrier, inc=1, device_id={"leaf": z * fan + c, "probe": a}, device_id_type=MESH
            )

    loads[0].wait()
    ph, plo = split(probe[...])
    probe_h[...] = ph
    probe_l[...] = plo
    loads[1].wait()
    loads[2].start()
    loads[3].start()
    columns = jnp.concatenate([col[level] for level in range(depth)], axis=1)
    own[...] = dot3(split(columns), (probe_h[...], probe_l[...]), CONTRACT_ROWS).reshape(own.shape)

    peers = n_leaf - 1 + jnp.where(z > 0, 1, 0) + jnp.where(z < last, 1, 0) + jnp.where(a != z, fan, 0)
    pl.semaphore_wait(barrier, peers)

    def exchange(step):
        away = 2**step
        other = leaf + (1 - 2 * ((leaf // away) % 2)) * away
        start = sum(depth - s for s in range(step))
        return start, pltpu.make_async_remote_copy(
            src_ref=own.at[pl.ds(step, depth - step)],
            dst_ref=swap.at[pl.ds(start, depth - step)],
            send_sem=swap_send.at[step],
            recv_sem=swap_recv.at[step],
            device_id={"leaf": other, "probe": z},
            device_id_type=MESH,
        )

    def near(which):
        @pl.loop(0, side // 2)
        def _(i):
            line = which * (side // 2) + i
            rows = pl.ds(pl.multiple_of(line * span, span), span)
            strips = [
                block[rows, j * span : (j + 1) * span] * mask[0, line, j].astype(jnp.float32)
                for j in range(side)
            ]
            into = pl.ds(pl.multiple_of(i * span, span), span)
            kept_h[into, :], kept_l[into, :] = split(jnp.concatenate(strips, axis=1))

        app[which * half : (which + 1) * half, :] = dot3(
            (kept_h[...], kept_l[...]), (probe_h[...], probe_l[...]), PLAIN
        )

    for step in range(depth):
        start, copy = exchange(step)
        copy.start()
        if step == 0:
            loads[2].wait()
        for which in range(2):
            if step == min(which, depth - 1):
                near(which)
        copy.wait()
        sib_h[step * rank : (step + 1) * rank, :], sib_l[step * rank : (step + 1) * rank, :] = split(
            swap[start]
        )
        for level in range(step + 1, depth):
            own[level] = own[level] + swap[start + level - step]

    def ship(source, to, slot, begin, send, recv):
        rows = pl.ds(pl.multiple_of(begin, piece), piece)
        return pltpu.make_async_remote_copy(
            src_ref=source.at[rows] if source is app else source.at[slot, rows],
            dst_ref=got.at[slot, rows],
            send_sem=send.at[slot, begin // piece],
            recv_sem=recv.at[slot, begin // piece],
            device_id={"leaf": leaf, "probe": to},
            device_id_type=MESH,
        )

    def rightward(source, slot, begin):
        return ship(source, jnp.minimum(z + 1, last), slot, begin, right_send, right_recv)

    def leftward(source, slot, begin):
        return ship(source, jnp.maximum(z - 1, 0), slot, begin, left_send, left_recv)

    loads[3].wait()
    sends_right = (z < last - 1) if ends else (z < last)
    sends_left = (z > 1) if ends else (z > 0)

    def far(which):
        rows = slice(which * half, (which + 1) * half)
        factors = jnp.concatenate([row[level, rows, :] for level in range(depth)], axis=1)
        value = app[rows, :] + dot3(split(factors), (sib_h[...], sib_l[...]), PLAIN)
        app[rows, :] = value
        app_h[rows, :], app_l[rows, :] = split(value)

    far(0)

    @pl.when(sends_right)
    def _():
        @pl.loop(0, pieces)
        def _(c):
            rightward(app, z, c * piece).start()

    far(1)

    @pl.when(sends_left)
    def _():
        @pl.loop(0, pieces)
        def _(c):
            leftward(app, z, half + c * piece).start()

    if ends:
        @pl.loop(0, pieces)
        def _(c):
            @pl.when(z == 0)
            def _():
                rightward(app, z, half + c * piece).start()

            @pl.when(z == last)
            def _():
                leftward(app, z, c * piece).start()

    keep = pltpu.make_async_copy(app, app_hbm, out_sem)
    keep.start()

    def gram(slot, source, begin, fresh):
        into = pl.ds(pl.multiple_of(slot * width, width), width)
        rows = pl.ds(pl.multiple_of(begin, half), half)
        here = (app_h[rows, :], app_l[rows, :])
        there = here if source is None else split(source[slot, rows, :])
        value = dot3(there, here, CONTRACT_ROWS)
        part[into, :] = value if fresh else part[into, :] + value

    def share(k):
        to = (leaf + k) % n_leaf
        return pltpu.make_async_remote_copy(
            src_ref=part.at[pl.ds(pl.multiple_of(to * slab, slab), slab)],
            dst_ref=shares.at[k],
            send_sem=share_send.at[k],
            recv_sem=share_recv.at[k],
            device_id={"leaf": to, "probe": z},
            device_id_type=MESH,
        )

    def give(slot):
        @pl.loop(0, fan)
        def _(c):
            to = slot * fan + c

            @pl.when(to != leaf)
            def _():
                share((to - leaf + n_leaf) % n_leaf).start()

    part[...] = jnp.zeros_like(part)

    @pl.loop(0, 2)
    def _(h):
        gram(z, None, h * half, False)

    give(z)

    @pl.loop(1, n_probe)
    def _(d):
        from_left = (z - d >= 0) & ((z < last) | (d > 1) | (not ends))
        from_right = (z + d <= last) & ((z > 0) | (d > 1) | (not ends))
        low_slot, high_slot = jnp.maximum(z - d, 0), jnp.minimum(z + d, last)

        @pl.loop(0, pieces)
        def _(c):
            up, low = c * piece, half + c * piece

            @pl.when(from_left)
            def _():
                rightward(got, low_slot, up).wait_recv()

                @pl.when(z < last)
                def _():
                    rightward(got, low_slot, up).start()

            @pl.when(from_right)
            def _():
                leftward(got, high_slot, low).wait_recv()

                @pl.when(z > 0)
                def _():
                    leftward(got, high_slot, low).start()

        @pl.loop(0, 2)
        def _(h):
            @pl.when(jnp.where(h == 0, from_left, from_right))
            def _():
                slot = jnp.where(h == 0, low_slot, high_slot)
                gram(slot, got, h * half, False)
                whole = (d > 1) | jnp.where(h == 0, z != 1, z != last - 1) | (not ends)

                @pl.when(whole)
                def _():
                    give(slot)

    if ends:
        at_low, at_high = z == 1, z == last - 1

        @pl.loop(0, pieces)
        def _(c):
            @pl.when(at_low)
            def _():
                rightward(got, z - 1, half + c * piece).wait_recv()

            @pl.when(at_high)
            def _():
                leftward(got, z + 1, c * piece).wait_recv()

        @pl.loop(0, 2)
        def _(h):
            @pl.when(jnp.where(h == 0, at_high, at_low))
            def _():
                slot = jnp.where(h == 0, jnp.minimum(z + 1, last), jnp.maximum(z - 1, 0))
                gram(slot, got, h * half, False)
                give(slot)

    total[...] = part[pl.ds(pl.multiple_of(leaf * slab, slab), slab), :]

    def holds(slot):
        return (not ends) | (((z > 0) | (slot != 1)) & ((z < last) | (slot != last - 1)))

    @pl.when(holds(a))
    def _():
        @pl.loop(1, n_leaf)
        def _(k):
            share(k).wait_recv()
            total[...] = total[...] + shares[k]

    scale = 1.0 / (points * n_leaf)

    tile = extra.shape[1]

    def trade(c, at):
        return pltpu.make_async_remote_copy(
            src_ref=total if tile == width else total.at[:, pl.ds(pl.multiple_of(c * tile, tile), tile)],
            dst_ref=extra.at[pl.ds(pl.multiple_of(at * slab, slab), slab)],
            send_sem=extra_send.at[c],
            recv_sem=extra_recv.at[at],
            device_id={"leaf": z * fan + c, "probe": a},
            device_id_type=MESH,
        )

    @pl.when(a != z)
    def _():
        @pl.loop(0, fan)
        def _(c):
            trade(c, b).start()

        @pl.loop(0, fan)
        def _(c):
            trade(c, c).wait_recv()

        turned[...] = extra[...].T
        skip = 0 if tile == slab else pl.multiple_of(b * slab, slab)
        gram_ref[...] = (total[...] + turned[pl.ds(skip, slab), :]) * scale

        @pl.loop(0, fan)
        def _(c):
            trade(c, b).wait_send()

    @pl.when(a == z)
    def _():
        gram_ref[...] = total[...] * scale

    @pl.loop(0, pieces)
    def _(c):
        up, low = c * piece, half + c * piece

        @pl.when(sends_right)
        def _():
            rightward(app, z, up).wait_send()

        @pl.when(sends_left)
        def _():
            leftward(app, z, low).wait_send()

        if ends:

            @pl.when(z == 0)
            def _():
                rightward(app, z, low).wait_send()

            @pl.when(z == last)
            def _():
                leftward(app, z, up).wait_send()

        @pl.loop(1, n_probe)
        def _(d):
            @pl.when((z - d >= 0) & (z < last))
            def _():
                rightward(got, jnp.maximum(z - d, 0), up).wait_send()

            @pl.when((z + d <= last) & (z > 0))
            def _():
                leftward(got, jnp.minimum(z + d, last), low).wait_send()

    @pl.loop(1, n_leaf)
    def _(k):
        @pl.when(holds(((leaf + k) % n_leaf) // fan))
        def _():
            share(k).wait_send()

    keep.wait()


def ring(n_leaf, n_probe, leaf_blocks, block_mask, row_factor_stack, column_factor_stack, probes):
    depth, points, rank = row_factor_stack.shape
    width = probes.shape[1]
    slab = n_probe * width // n_leaf
    fan = n_leaf // n_probe
    pieces = 4
    tile = slab if slab % 128 == 0 else width
    f32, bf16 = jnp.float32, jnp.bfloat16
    dma = pltpu.SemaphoreType.DMA
    hbm = pl.BlockSpec(memory_space=pltpu.HBM)
    return pl.pallas_call(
        functools.partial(ring_kernel, n_leaf, n_probe, pieces),
        out_shape=(
            jax.ShapeDtypeStruct((points, width), f32),
            jax.ShapeDtypeStruct((slab, width), f32),
        ),
        in_specs=[pl.BlockSpec(memory_space=pltpu.SMEM), hbm, hbm, hbm, hbm],
        out_specs=(hbm, pl.BlockSpec(memory_space=pltpu.VMEM)),
        scratch_shapes=[
            pltpu.VMEM((points, points), f32),
            pltpu.VMEM((depth, points, rank), f32),
            pltpu.VMEM((depth, points, rank), f32),
            pltpu.VMEM((points, width), f32),
            pltpu.VMEM((points, width), bf16),
            pltpu.VMEM((points, width), bf16),
            pltpu.VMEM((depth, rank, width), f32),
            pltpu.VMEM((depth * (depth + 1) // 2, rank, width), f32),
            pltpu.VMEM((depth * rank, width), bf16),
            pltpu.VMEM((depth * rank, width), bf16),
            pltpu.VMEM((points, width), f32),
            pltpu.VMEM((points, width), bf16),
            pltpu.VMEM((points, width), bf16),
            pltpu.VMEM((n_probe, points, width), f32),
            pltpu.VMEM((n_probe * width, width), f32),
            pltpu.VMEM((n_leaf, slab, width), f32),
            pltpu.VMEM((slab, width), f32),
            pltpu.VMEM((width, tile), f32),
            pltpu.VMEM((tile, width), f32),
            pltpu.VMEM((points // 2, points), bf16),
            pltpu.VMEM((points // 2, points), bf16),
            dma((4,)),
            dma,
            dma((depth,)),
            dma((depth,)),
            dma((n_probe, 2 * pieces)),
            dma((n_probe, 2 * pieces)),
            dma((n_probe, 2 * pieces)),
            dma((n_probe, 2 * pieces)),
            dma((n_leaf,)),
            dma((n_leaf,)),
            dma((fan,)),
            dma((fan,)),
        ],
        compiler_params=pltpu.CompilerParams(
            collective_id=0, has_side_effects=True, vmem_limit_bytes=67043328
        ),
    )(block_mask, leaf_blocks, row_factor_stack, column_factor_stack, probes)


def hub_kernel(
    n_leaf, n_probe, parts,
    mask_hbm, block_hbm, row_hbm, col_hbm, probe_hbm, app_hbm, gram_ref,
    mask, block, row, col, probe, probe_h, probe_l, block_h, block_l, row_h, row_l,
    own, pair_in, pair_sum, group_in, sib, sib_h, sib_l, app, app_h, app_l, near_other,
    got_probe, got_sib, got_turned, turned, pairs, arrived, summed, straight, crossed, diag, diag_in, diag_sum, shares,
    load_sem, out_sem, pair_send, pair_recv, group_send, group_recv, half_send, half_recv,
    probe_send, probe_recv, sib_send, sib_recv, turned_send, turned_recv,
    part_send, part_recv, straight_send, straight_recv, crossed_send, crossed_recv, swap_send, swap_recv, share_send, share_recv, ready, go,
):
    depth, rank = row.shape[0], row.shape[2]
    points, width = app.shape
    side = mask.shape[1]
    span = points // side
    half = points // 2
    leaf, z = lax.axis_index("leaf"), lax.axis_index("probe")
    slab = n_probe * width // n_leaf
    fan = n_leaf // n_probe
    chunk = width // parts
    last = n_probe - 1
    h = n_probe // 2
    teams = n_leaf // 2
    split_rank = rank // 2
    flow = leaf % 2
    team = leaf // 2
    mate = leaf + 1 - 2 * flow
    a, b = leaf // fan, leaf % fan

    def along(direction, position):
        return jnp.where(direction == 0, position, last - position)

    q = along(flow, z)
    is_hub = q == h
    hub = along(flow, h)

    def remote(src, dst, send, recv, to_leaf, to_z):
        return pltpu.make_async_remote_copy(
            src_ref=src, dst_ref=dst, send_sem=send, recv_sem=recv,
            device_id={"leaf": to_leaf, "probe": to_z}, device_id_type=MESH,
        )

    loads = [
        pltpu.make_async_copy(source, target, load_sem.at[i])
        for i, (source, target) in enumerate(
            ((probe_hbm, probe), (col_hbm, col), (block_hbm, block), (row_hbm, row), (mask_hbm, mask))
        )
    ]
    loads[0].start()
    loads[1].start()

    barrier = pltpu.get_barrier_semaphore()

    @pl.loop(1, n_leaf)
    def _(k):
        pl.semaphore_signal(
            barrier, inc=1, device_id={"leaf": (leaf + k) % n_leaf, "probe": z}, device_id_type=MESH
        )

    @pl.loop(0, n_probe)
    def _(k):
        @pl.when((k != z) & (jnp.abs(k - z) < last))
        def _():
            pl.semaphore_signal(barrier, inc=1, device_id={"leaf": leaf, "probe": k}, device_id_type=MESH)

    pl.semaphore_wait(barrier, n_leaf - 1 + last - jnp.where((z == 0) | (z == last), 1, 0))

    sides = [k for k in range(n_probe) if abs(k - h) == 1]
    distant = [k for k in range(n_probe) if abs(k - h) > 1]
    is_side = jnp.abs(q - h) == 1
    place = jnp.where(q > h, 1, 0)

    def give_probe(slot):
        return remote(probe_hbm, got_probe.at[slot], probe_send, probe_recv.at[slot], leaf, hub)

    @pl.when(is_side)
    def _():
        give_probe(place).start()

    loads[0].wait()
    ph, plo = split(probe[...])
    probe_h[...] = ph
    probe_l[...] = plo
    loads[1].wait()
    loads[4].start()
    loads[2].start()
    loads[3].start()
    columns = jnp.concatenate([col[level] for level in range(depth)], axis=1)
    own[...] = dot3(split(columns), (probe_h[...], probe_l[...]), CONTRACT_ROWS).reshape(own.shape)

    @pl.loop(1, n_leaf)
    def _(k):
        pl.semaphore_signal(
            ready, inc=1, device_id={"leaf": (leaf + k) % n_leaf, "probe": z}, device_id_type=MESH
        )

    first_level = remote(own.at[0], sib.at[0], pair_send.at[0], pair_recv.at[0], mate, z)
    upper_levels = remote(
        own.at[pl.ds(1, depth - 1), pl.ds(pl.multiple_of((1 - flow) * split_rank, split_rank), split_rank)],
        pair_in, pair_send.at[1], pair_recv.at[1], mate, z,
    )
    upper_levels.start()
    first_level.start()
    mine = pl.ds(pl.multiple_of(flow * split_rank, split_rank), split_rank)

    def to_group(level, k):
        members = 2 ** (level - 1)
        base = leaf - leaf % 2**level + (1 - 2 * ((leaf // 2**level) % 2)) * 2**level
        from_slot = members - 1 + (leaf % 2**level) // 2
        return remote(
            pair_sum.at[level - 1], group_in.at[from_slot],
            group_send.at[members - 1 + k], group_recv.at[from_slot], base + 2 * k + flow, z,
        )

    def from_group(level, k):
        members = 2 ** (level - 1)
        return remote(
            pair_sum.at[level - 1], group_in.at[members - 1 + k],
            group_send.at[members - 1 + k], group_recv.at[members - 1 + k], mate, z,
        )

    upper_levels.wait_recv()
    for level in range(1, depth):
        pair_sum[level - 1] = own[level, mine, :] + pair_in[level - 1]
    for level in reversed(range(1, depth)):
        @pl.loop(0, 2 ** (level - 1))
        def _(k):
            to_group(level, k).start()

    loads[4].wait()
    loads[2].wait()

    @pl.loop(0, side)
    def _(line):
        rows = pl.ds(pl.multiple_of(line * span, span), span)
        strips = [
            block[rows, j * span : (j + 1) * span] * mask[0, line, j].astype(jnp.float32)
            for j in range(side)
        ]
        block_h[rows, :], block_l[rows, :] = split(jnp.concatenate(strips, axis=1))

    def near(target):
        @pl.loop(0, 2)
        def _(i):
            rows = pl.ds(pl.multiple_of(i * half, half), half)
            target[rows, :] = dot3(
                (block_h[rows, :], block_l[rows, :]), (probe_h[...], probe_l[...]), PLAIN
            )

    near(app)
    loads[3].wait()
    for level in range(depth):
        row_h[:, level * rank : (level + 1) * rank], row_l[:, level * rank : (level + 1) * rank] = split(row[level])

    for level in range(1, depth):
        @pl.loop(0, 2 ** (level - 1))
        def _(k):
            from_group(level, k).wait_recv()

        begin = 2 ** (level - 1) - 1
        value = group_in[begin]
        for k in range(1, 2 ** (level - 1)):
            value = value + group_in[begin + k]
        sib[level, mine, :] = value

    half_copy = remote(
        sib.at[pl.ds(1, depth - 1), mine], sib.at[pl.ds(1, depth - 1), mine], half_send, half_recv, mate, z
    )
    half_copy.start()
    first_level.wait_recv()
    half_copy.wait_recv()

    def give_sib(slot):
        return remote(sib, got_sib.at[slot], sib_send, sib_recv.at[slot], leaf, hub)

    @pl.when(is_side)
    def _():
        give_sib(place).start()

    def far(source, base, target, slot):
        flat = source[...].reshape(depth * rank, width)
        sib_h[...], sib_l[...] = split(flat)

        @pl.loop(0, 2)
        def _(i):
            rows = pl.ds(pl.multiple_of(i * half, half), half)
            value = base[rows, :] + dot3((row_h[rows, :], row_l[rows, :]), (sib_h[...], sib_l[...]), PLAIN)
            if target is not None:
                target[rows, :] = value
            app_h[slot, rows, :], app_l[slot, rows, :] = split(value)

    far(sib, app, app, h)
    keep = pltpu.make_async_copy(app, app_hbm, out_sem)
    keep.start()

    def rows_of(c):
        return pl.ds(pl.multiple_of(c * chunk, chunk), chunk)

    def give_turned(c):
        return remote(
            turned.at[rows_of(c)], got_turned.at[rows_of(c)], turned_send.at[c], turned_recv.at[c], leaf, hub
        )

    @pl.when(q == 0)
    def _():
        per = 128 // chunk
        for strip in range(width // 128):
            lanes = slice(strip * 128, (strip + 1) * 128)
            turned[lanes, :] = app[:, lanes].T
            if strip == 0:
                give_turned(0).start()

    diag[...] = dot3((app_h[h], app_l[h]), (app_h[h], app_l[h]), CONTRACT_ROWS)

    def slab_of(k):
        return pl.ds(pl.multiple_of(k * slab, slab), slab)

    swap = remote(diag.at[slab_of(1 - flow)], diag_in, swap_send, swap_recv, mate, z)
    swap.start()
    share = remote(diag_sum, shares.at[team], share_send, share_recv.at[team], z * fan + flow, z)

    def give_share():
        swap.wait_recv()
        diag_sum[...] = diag[slab_of(flow), :] + diag_in[...]

        @pl.when(a != z)
        def _():
            share.start()

    order = [(i, j) for j in range(n_probe) for i in range(j)]
    seat = {(i, j): 1 if (i, j) == (1, last) else j for i, j in order}

    def part_copy(i, j, c, k):
        pid = order.index((i, j))
        return remote(
            pairs.at[pid, rows_of(c), pl.ds(pl.multiple_of(k * slab, slab), slab)],
            arrived.at[i, team, rows_of(c)],
            part_send.at[pid, c, k], part_recv.at[i, team, c], along(flow, seat[i, j]) * fan + k, z,
        )

    def give_part(i, j, c):
        @pl.loop(0, fan)
        def _(k):
            local = along(flow, seat[i, j]) * fan + k == leaf

            @pl.when(local)
            def _():
                arrived[i, team, rows_of(c), :] = pairs[
                    order.index((i, j)), rows_of(c), pl.ds(pl.multiple_of(k * slab, slab), slab)
                ]

            @pl.when(jnp.logical_not(local))
            def _():
                part_copy(i, j, c, k).start()

    give_share()

    @pl.when(is_side)
    def _():
        give_sib(place).wait_send()

        @pl.when(q < h)
        def _():
            pl.semaphore_signal(go, inc=1, device_id={"leaf": leaf, "probe": along(flow, 0)}, device_id_type=MESH)

        @pl.when(q > h)
        def _():
            pl.semaphore_signal(go, inc=1, device_id={"leaf": mate, "probe": z}, device_id_type=MESH)

    @pl.when(q == 0)
    def _():
        pl.semaphore_wait(go, 2)

        @pl.loop(1, parts)
        def _(c):
            give_turned(c).start()

    @pl.when(is_hub)
    def _():
        for slot, k in enumerate(sides):
            give_probe(slot).wait_recv()
            ph, plo = split(got_probe[slot])
            probe_h[...] = ph
            probe_l[...] = plo
            near(near_other.at[slot])
        for slot, k in enumerate(sides):
            give_sib(slot).wait_recv()
            far(got_sib.at[slot], near_other.at[slot], None, k)
        for i, j in order:
            if i > 0:
                pairs[order.index((i, j))] = dot3(
                    (app_h[i], app_l[i]), (app_h[j], app_l[j]), CONTRACT_ROWS
                )

                @pl.loop(0, parts)
                def _(c):
                    give_part(i, j, c)

    def late(c):
        @pl.when(is_hub)
        def _():
            give_turned(c).wait_recv()
            high, low = split(got_turned[rows_of(c), :])
            stacked = jnp.concatenate([high, low], axis=0)
            dot = functools.partial(lax.dot_general, dimension_numbers=PLAIN, preferred_element_type=jnp.float32)
            for j in range(1, n_probe):
                both = dot(stacked, app_h[j])
                pairs[order.index((0, j)), rows_of(c), :] = both[:chunk] + (dot(high, app_l[j]) + both[chunk:])
                give_part(0, j, c)

    current = jnp.where(z == h, 0, 1)
    collects = (z == h) | (z == last - h)
    position = along(current, a)

    def arrival(i, m, c):
        return remote(
            arrived.at[i, m, rows_of(c)], arrived.at[i, m, rows_of(c)],
            part_send.at[0, c, 0], part_recv.at[i, m, c], mate, z,
        )

    lanes_here = pl.ds(pl.multiple_of(b * slab, slab), slab)
    per_slab = slab // chunk

    def holds(i):
        match = [j for j in range(n_probe) if (i, j) in seat]
        found = jnp.bool_(False)
        partner = position
        for j in match:
            found = found | (position == seat[i, j])
            if seat[i, j] != j:
                partner = jnp.where(position == seat[i, j], j, partner)
        return collects & found, along(current, partner)

    def send_crossed(i, c):
        return remote(
            summed.at[i, rows_of(c)], crossed.at[rows_of(c)],
            crossed_send.at[i, c], crossed_recv.at[c], holds(i)[1] * fan + b, along(current, i),
        )

    def send_straight(i, c):
        return remote(
            summed.at[i, rows_of(c)], straight.at[rows_of(c % per_slab), lanes_here],
            straight_send.at[i, c], straight_recv.at[c % per_slab, b],
            along(current, i) * fan + c // per_slab, holds(i)[1],
        )

    def collect(i, c):
        @pl.when(holds(i)[0])
        def _():
            for m in range(teams):
                @pl.when(2 * m + current != leaf)
                def _():
                    arrival(i, m, c).wait_recv()

            value = arrived[i, 0, rows_of(c), :]
            for m in range(1, teams):
                value = value + arrived[i, m, rows_of(c), :]
            summed[i, rows_of(c), :] = value
            if i == h:
                crossed[rows_of(c), :] = value
            else:
                send_crossed(i, c).start()
            send_straight(i, c).start()

    @pl.loop(0, parts - 1)
    def _(c):
        late(c)

    pl.semaphore_wait(ready, n_leaf - 1)
    for i in range(1, n_probe - 1):
        @pl.loop(0, parts)
        def _(c):
            collect(i, c)

    @pl.loop(0, parts - 2)
    def _(c):
        collect(0, c)

    late(parts - 1)

    @pl.loop(parts - 2, parts)
    def _(c):
        collect(0, c)

    scale = 1.0 / (points * n_leaf)

    @pl.when(a == z)
    def _():
        shares[team] = diag_sum[...]

        @pl.loop(1, teams)
        def _(k):
            other = (team + k) % teams
            remote(diag_sum, shares.at[other], share_send, share_recv.at[other], mate, z).wait_recv()

        value = shares[0]
        for k in range(1, teams):
            value = value + shares[k]
        gram_ref[...] = value * scale

    @pl.when(a != z)
    def _():
        back = jnp.where(z < a, 0, 1)

        @pl.when(along(back, h) != z)
        def _():
            @pl.loop(0, parts)
            def _(c):
                remote(
                    summed.at[0, rows_of(c)], crossed.at[rows_of(c)],
                    crossed_send.at[0, c], crossed_recv.at[c], mate, z,
                ).wait_recv()

        @pl.loop(0, per_slab * fan)
        def _(n):
            c, k = n // fan, n % fan
            remote(
                summed.at[0, rows_of(c)], straight.at[rows_of(c), pl.ds(pl.multiple_of(k * slab, slab), slab)],
                straight_send.at[0, c], straight_recv.at[c, k], mate, z,
            ).wait_recv()

        gram_ref[...] = (straight[...] + crossed[...].T) * scale

    first_level.wait_send()
    upper_levels.wait_send()
    half_copy.wait_send()
    for level in range(1, depth):
        @pl.loop(0, 2 ** (level - 1))
        def _(k):
            to_group(level, k).wait_send()

    @pl.when(is_side)
    def _():
        give_probe(place).wait_send()

    @pl.when(q == 0)
    def _():
        @pl.loop(0, parts)
        def _(c):
            give_turned(c).wait_send()

    swap.wait_send()

    @pl.when(a != z)
    def _():
        share.wait_send()

    @pl.when(is_hub)
    def _():
        for i, j in order:
            @pl.loop(0, parts * fan)
            def _(n):
                c, k = n // fan, n % fan

                @pl.when(along(flow, seat[i, j]) * fan + k != leaf)
                def _():
                    part_copy(i, j, c, k).wait_send()

    for i in range(n_probe - 1):
        @pl.when(holds(i)[0])
        def _():
            @pl.loop(0, parts)
            def _(c):
                if i != h:
                    send_crossed(i, c).wait_send()
                send_straight(i, c).wait_send()

    keep.wait()


def hub_local(n_leaf, n_probe, leaf_blocks, block_mask, row_factor_stack, column_factor_stack, probes):
    depth, points, rank = row_factor_stack.shape
    width = probes.shape[1]
    slab = n_probe * width // n_leaf
    fan = n_leaf // n_probe
    parts = 2 * width // slab
    teams = n_leaf // 2
    count = n_probe * (n_probe - 1) // 2
    f32, bf16 = jnp.float32, jnp.bfloat16
    dma = pltpu.SemaphoreType.DMA
    hbm = pl.BlockSpec(memory_space=pltpu.HBM)
    groups = 2 ** (depth - 1) - 1
    return pl.pallas_call(
        functools.partial(hub_kernel, n_leaf, n_probe, parts),
        out_shape=(
            jax.ShapeDtypeStruct((points, width), f32),
            jax.ShapeDtypeStruct((slab, width), f32),
        ),
        in_specs=[hbm] * 5,
        out_specs=(hbm, pl.BlockSpec(memory_space=pltpu.VMEM)),
        scratch_shapes=[
            pltpu.SMEM(block_mask.shape, block_mask.dtype),
            pltpu.VMEM((points, points), f32),
            pltpu.VMEM((depth, points, rank), f32),
            pltpu.VMEM((depth, points, rank), f32),
            pltpu.VMEM((points, width), f32),
            pltpu.VMEM((points, width), bf16),
            pltpu.VMEM((points, width), bf16),
            pltpu.VMEM((points, points), bf16),
            pltpu.VMEM((points, points), bf16),
            pltpu.VMEM((points, depth * rank), bf16),
            pltpu.VMEM((points, depth * rank), bf16),
            pltpu.VMEM((depth, rank, width), f32),
            pltpu.VMEM((depth - 1, rank // 2, width), f32),
            pltpu.VMEM((depth - 1, rank // 2, width), f32),
            pltpu.VMEM((groups, rank // 2, width), f32),
            pltpu.VMEM((depth, rank, width), f32),
            pltpu.VMEM((depth * rank, width), bf16),
            pltpu.VMEM((depth * rank, width), bf16),
            pltpu.VMEM((points, width), f32),
            pltpu.VMEM((n_probe, points, width), bf16),
            pltpu.VMEM((n_probe, points, width), bf16),
            pltpu.VMEM((2, points, width), f32),
            pltpu.VMEM((2, points, width), f32),
            pltpu.VMEM((2, depth, rank, width), f32),
            pltpu.VMEM((width, points), f32),
            pltpu.VMEM((width, points), f32),
            pltpu.VMEM((count, width, width), f32),
            pltpu.VMEM((n_probe - 1, teams, width, slab), f32),
            pltpu.VMEM((n_probe - 1, width, slab), f32),
            pltpu.VMEM((slab, width), f32),
            pltpu.VMEM((width, slab), f32),
            pltpu.VMEM((width, width), f32),
            pltpu.VMEM((slab, width), f32),
            pltpu.VMEM((slab, width), f32),
            pltpu.VMEM((teams, slab, width), f32),
            dma((5,)),
            dma,
            dma((2,)),
            dma((2,)),
            dma((groups,)),
            dma((groups,)),
            dma,
            dma,
            dma,
            dma((2,)),
            dma,
            dma((2,)),
            dma((parts,)),
            dma((parts,)),
            dma((count, parts, fan)),
            dma((n_probe - 1, teams, parts)),
            dma((n_probe - 1, parts)),
            dma((2, fan)),
            dma((n_probe - 1, parts)),
            dma((parts,)),
            dma,
            dma,
            dma,
            dma((teams,)),
            pltpu.SemaphoreType.REGULAR,
            pltpu.SemaphoreType.REGULAR,
        ],
        compiler_params=pltpu.CompilerParams(
            collective_id=0, has_side_effects=True, vmem_limit_bytes=67043328
        ),
    )(block_mask, leaf_blocks, row_factor_stack, column_factor_stack, probes)


def local(n_leaf, n_probe, *arrays):
    width = arrays[-1].shape[1]
    whole_lanes = (n_probe * width) % (128 * n_leaf) == 0
    if n_probe == 4 and n_leaf == 2 * n_probe and whole_lanes:
        return hub_local(n_leaf, n_probe, *arrays)
    return ring(n_leaf, n_probe, *arrays)


def solution(mesh):
    return jax.shard_map(
        functools.partial(local, mesh.shape["leaf"], mesh.shape["probe"]),
        mesh=mesh,
        in_specs=(
            P("leaf", None),
            P("leaf", None, None),
            P(None, "leaf", None),
            P(None, "leaf", None),
            P("leaf", "probe"),
        ),
        out_specs=(P("leaf", "probe"), P("leaf", "probe")),
        check_vma=False,
    )
```

```python
import functools

import jax
import jax.numpy as jnp
from jax import lax
from jax.experimental import pallas as pl
from jax.experimental.pallas import tpu as pltpu
from jax.sharding import PartitionSpec as P

MESH = pl.DeviceIdType.MESH
CONTRACT_ROWS = (((0,), (0,)), ((), ()))
PLAIN = (((1,), (0,)), ((), ()))


def split(value):
    high = value.astype(jnp.bfloat16)
    return high, (value - high.astype(jnp.float32)).astype(jnp.bfloat16)


def dot3(left, right, dims):
    (lh, ll), (rh, rl) = left, right
    dot = functools.partial(lax.dot_general, dimension_numbers=dims, preferred_element_type=jnp.float32)
    return dot(lh, rh) + (dot(lh, rl) + dot(ll, rh))


def ring_kernel(
    n_leaf, n_probe, pieces,
    mask, block_hbm, row_hbm, col_hbm, probe_hbm, app_hbm, gram_ref,
    block, row, col, probe, probe_h, probe_l, own, swap, sib_h, sib_l,
    app, app_h, app_l, got, part, shares, total, extra, turned, kept_h, kept_l,
    load_sem, out_sem, swap_send, swap_recv, right_send, right_recv, left_send, left_recv,
    share_send, share_recv, extra_send, extra_recv,
):
    depth, rank = row.shape[0], row.shape[2]
    points, width = app.shape
    side = mask.shape[1]
    span = points // side
    half = points // 2
    piece = half // pieces
    leaf, z = lax.axis_index("leaf"), lax.axis_index("probe")
    slab = n_probe * width // n_leaf
    fan = n_leaf // n_probe
    a, b = leaf // fan, leaf % fan
    last = n_probe - 1
    ends = n_probe > 2

    loads = [
        pltpu.make_async_copy(source, target, load_sem.at[i])
        for i, (source, target) in enumerate(
            ((probe_hbm, probe), (col_hbm, col), (block_hbm, block), (row_hbm, row))
        )
    ]
    loads[0].start()
    loads[1].start()

    barrier = pltpu.get_barrier_semaphore()

    @pl.loop(1, n_leaf)
    def _(k):
        pl.semaphore_signal(
            barrier, inc=1, device_id={"leaf": (leaf + k) % n_leaf, "probe": z}, device_id_type=MESH
        )

    @pl.when(z > 0)
    def _():
        pl.semaphore_signal(barrier, inc=1, device_id={"leaf": leaf, "probe": z - 1}, device_id_type=MESH)

    @pl.when(z < last)
    def _():
        pl.semaphore_signal(barrier, inc=1, device_id={"leaf": leaf, "probe": z + 1}, device_id_type=MESH)

    @pl.when(a != z)
    def _():
        @pl.loop(0, fan)
        def _(c):
            pl.semaphore_signal(
                barrier, inc=1, device_id={"leaf": z * fan + c, "probe": a}, device_id_type=MESH
            )

    loads[0].wait()
    ph, plo = split(probe[...])
    probe_h[...] = ph
    probe_l[...] = plo
    loads[1].wait()
    loads[2].start()
    loads[3].start()
    columns = jnp.concatenate([col[level] for level in range(depth)], axis=1)
    own[...] = dot3(split(columns), (probe_h[...], probe_l[...]), CONTRACT_ROWS).reshape(own.shape)

    peers = n_leaf - 1 + jnp.where(z > 0, 1, 0) + jnp.where(z < last, 1, 0) + jnp.where(a != z, fan, 0)
    pl.semaphore_wait(barrier, peers)

    def exchange(step):
        away = 2**step
        other = leaf + (1 - 2 * ((leaf // away) % 2)) * away
        start = sum(depth - s for s in range(step))
        return start, pltpu.make_async_remote_copy(
            src_ref=own.at[pl.ds(step, depth - step)],
            dst_ref=swap.at[pl.ds(start, depth - step)],
            send_sem=swap_send.at[step],
            recv_sem=swap_recv.at[step],
            device_id={"leaf": other, "probe": z},
            device_id_type=MESH,
        )

    def near(which):
        @pl.loop(0, side // 2)
        def _(i):
            line = which * (side // 2) + i
            rows = pl.ds(pl.multiple_of(line * span, span), span)
            strips = [
                block[rows, j * span : (j + 1) * span] * mask[0, line, j].astype(jnp.float32)
                for j in range(side)
            ]
            into = pl.ds(pl.multiple_of(i * span, span), span)
            kept_h[into, :], kept_l[into, :] = split(jnp.concatenate(strips, axis=1))

        app[which * half : (which + 1) * half, :] = dot3(
            (kept_h[...], kept_l[...]), (probe_h[...], probe_l[...]), PLAIN
        )

    for step in range(depth):
        start, copy = exchange(step)
        copy.start()
        if step == 0:
            loads[2].wait()
        for which in range(2):
            if step == min(which, depth - 1):
                near(which)
        copy.wait()
        sib_h[step * rank : (step + 1) * rank, :], sib_l[step * rank : (step + 1) * rank, :] = split(
            swap[start]
        )
        for level in range(step + 1, depth):
            own[level] = own[level] + swap[start + level - step]

    def ship(source, to, slot, begin, send, recv):
        rows = pl.ds(pl.multiple_of(begin, piece), piece)
        return pltpu.make_async_remote_copy(
            src_ref=source.at[rows] if source is app else source.at[slot, rows],
            dst_ref=got.at[slot, rows],
            send_sem=send.at[slot, begin // piece],
            recv_sem=recv.at[slot, begin // piece],
            device_id={"leaf": leaf, "probe": to},
            device_id_type=MESH,
        )

    def rightward(source, slot, begin):
        return ship(source, jnp.minimum(z + 1, last), slot, begin, right_send, right_recv)

    def leftward(source, slot, begin):
        return ship(source, jnp.maximum(z - 1, 0), slot, begin, left_send, left_recv)

    loads[3].wait()
    sends_right = (z < last - 1) if ends else (z < last)
    sends_left = (z > 1) if ends else (z > 0)

    def far(which):
        rows = slice(which * half, (which + 1) * half)
        factors = jnp.concatenate([row[level, rows, :] for level in range(depth)], axis=1)
        value = app[rows, :] + dot3(split(factors), (sib_h[...], sib_l[...]), PLAIN)
        app[rows, :] = value
        app_h[rows, :], app_l[rows, :] = split(value)

    far(0)

    @pl.when(sends_right)
    def _():
        @pl.loop(0, pieces)
        def _(c):
            rightward(app, z, c * piece).start()

    far(1)

    @pl.when(sends_left)
    def _():
        @pl.loop(0, pieces)
        def _(c):
            leftward(app, z, half + c * piece).start()

    if ends:
        @pl.loop(0, pieces)
        def _(c):
            @pl.when(z == 0)
            def _():
                rightward(app, z, half + c * piece).start()

            @pl.when(z == last)
            def _():
                leftward(app, z, c * piece).start()

    keep = pltpu.make_async_copy(app, app_hbm, out_sem)
    keep.start()

    def gram(slot, source, begin, fresh):
        into = pl.ds(pl.multiple_of(slot * width, width), width)
        rows = pl.ds(pl.multiple_of(begin, half), half)
        here = (app_h[rows, :], app_l[rows, :])
        there = here if source is None else split(source[slot, rows, :])
        value = dot3(there, here, CONTRACT_ROWS)
        part[into, :] = value if fresh else part[into, :] + value

    def share(k):
        to = (leaf + k) % n_leaf
        return pltpu.make_async_remote_copy(
            src_ref=part.at[pl.ds(pl.multiple_of(to * slab, slab), slab)],
            dst_ref=shares.at[k],
            send_sem=share_send.at[k],
            recv_sem=share_recv.at[k],
            device_id={"leaf": to, "probe": z},
            device_id_type=MESH,
        )

    def give(slot):
        @pl.loop(0, fan)
        def _(c):
            to = slot * fan + c

            @pl.when(to != leaf)
            def _():
                share((to - leaf + n_leaf) % n_leaf).start()

    part[...] = jnp.zeros_like(part)

    @pl.loop(0, 2)
    def _(h):
        gram(z, None, h * half, False)

    give(z)

    @pl.loop(1, n_probe)
    def _(d):
        from_left = (z - d >= 0) & ((z < last) | (d > 1) | (not ends))
        from_right = (z + d <= last) & ((z > 0) | (d > 1) | (not ends))
        low_slot, high_slot = jnp.maximum(z - d, 0), jnp.minimum(z + d, last)

        @pl.loop(0, pieces)
        def _(c):
            up, low = c * piece, half + c * piece

            @pl.when(from_left)
            def _():
                rightward(got, low_slot, up).wait_recv()

                @pl.when(z < last)
                def _():
                    rightward(got, low_slot, up).start()

            @pl.when(from_right)
            def _():
                leftward(got, high_slot, low).wait_recv()

                @pl.when(z > 0)
                def _():
                    leftward(got, high_slot, low).start()

        @pl.loop(0, 2)
        def _(h):
            @pl.when(jnp.where(h == 0, from_left, from_right))
            def _():
                slot = jnp.where(h == 0, low_slot, high_slot)
                gram(slot, got, h * half, False)
                whole = (d > 1) | jnp.where(h == 0, z != 1, z != last - 1) | (not ends)

                @pl.when(whole)
                def _():
                    give(slot)

    if ends:
        at_low, at_high = z == 1, z == last - 1

        @pl.loop(0, pieces)
        def _(c):
            @pl.when(at_low)
            def _():
                rightward(got, z - 1, half + c * piece).wait_recv()

            @pl.when(at_high)
            def _():
                leftward(got, z + 1, c * piece).wait_recv()

        @pl.loop(0, 2)
        def _(h):
            @pl.when(jnp.where(h == 0, at_high, at_low))
            def _():
                slot = jnp.where(h == 0, jnp.minimum(z + 1, last), jnp.maximum(z - 1, 0))
                gram(slot, got, h * half, False)
                give(slot)

    total[...] = part[pl.ds(pl.multiple_of(leaf * slab, slab), slab), :]

    def holds(slot):
        return (not ends) | (((z > 0) | (slot != 1)) & ((z < last) | (slot != last - 1)))

    @pl.when(holds(a))
    def _():
        @pl.loop(1, n_leaf)
        def _(k):
            share(k).wait_recv()
            total[...] = total[...] + shares[k]

    scale = 1.0 / (points * n_leaf)

    tile = extra.shape[1]

    def trade(c, at):
        return pltpu.make_async_remote_copy(
            src_ref=total if tile == width else total.at[:, pl.ds(pl.multiple_of(c * tile, tile), tile)],
            dst_ref=extra.at[pl.ds(pl.multiple_of(at * slab, slab), slab)],
            send_sem=extra_send.at[c],
            recv_sem=extra_recv.at[at],
            device_id={"leaf": z * fan + c, "probe": a},
            device_id_type=MESH,
        )

    @pl.when(a != z)
    def _():
        @pl.loop(0, fan)
        def _(c):
            trade(c, b).start()

        @pl.loop(0, fan)
        def _(c):
            trade(c, c).wait_recv()

        turned[...] = extra[...].T
        skip = 0 if tile == slab else pl.multiple_of(b * slab, slab)
        gram_ref[...] = (total[...] + turned[pl.ds(skip, slab), :]) * scale

        @pl.loop(0, fan)
        def _(c):
            trade(c, b).wait_send()

    @pl.when(a == z)
    def _():
        gram_ref[...] = total[...] * scale

    @pl.loop(0, pieces)
    def _(c):
        up, low = c * piece, half + c * piece

        @pl.when(sends_right)
        def _():
            rightward(app, z, up).wait_send()

        @pl.when(sends_left)
        def _():
            leftward(app, z, low).wait_send()

        if ends:

            @pl.when(z == 0)
            def _():
                rightward(app, z, low).wait_send()

            @pl.when(z == last)
            def _():
                leftward(app, z, up).wait_send()

        @pl.loop(1, n_probe)
        def _(d):
            @pl.when((z - d >= 0) & (z < last))
            def _():
                rightward(got, jnp.maximum(z - d, 0), up).wait_send()

            @pl.when((z + d <= last) & (z > 0))
            def _():
                leftward(got, jnp.minimum(z + d, last), low).wait_send()

    @pl.loop(1, n_leaf)
    def _(k):
        @pl.when(holds(((leaf + k) % n_leaf) // fan))
        def _():
            share(k).wait_send()

    keep.wait()


def ring(n_leaf, n_probe, leaf_blocks, block_mask, row_factor_stack, column_factor_stack, probes):
    depth, points, rank = row_factor_stack.shape
    width = probes.shape[1]
    slab = n_probe * width // n_leaf
    fan = n_leaf // n_probe
    pieces = 4
    tile = slab if slab % 128 == 0 else width
    f32, bf16 = jnp.float32, jnp.bfloat16
    dma = pltpu.SemaphoreType.DMA
    hbm = pl.BlockSpec(memory_space=pltpu.HBM)
    return pl.pallas_call(
        functools.partial(ring_kernel, n_leaf, n_probe, pieces),
        out_shape=(
            jax.ShapeDtypeStruct((points, width), f32),
            jax.ShapeDtypeStruct((slab, width), f32),
        ),
        in_specs=[pl.BlockSpec(memory_space=pltpu.SMEM), hbm, hbm, hbm, hbm],
        out_specs=(hbm, pl.BlockSpec(memory_space=pltpu.VMEM)),
        scratch_shapes=[
            pltpu.VMEM((points, points), f32),
            pltpu.VMEM((depth, points, rank), f32),
            pltpu.VMEM((depth, points, rank), f32),
            pltpu.VMEM((points, width), f32),
            pltpu.VMEM((points, width), bf16),
            pltpu.VMEM((points, width), bf16),
            pltpu.VMEM((depth, rank, width), f32),
            pltpu.VMEM((depth * (depth + 1) // 2, rank, width), f32),
            pltpu.VMEM((depth * rank, width), bf16),
            pltpu.VMEM((depth * rank, width), bf16),
            pltpu.VMEM((points, width), f32),
            pltpu.VMEM((points, width), bf16),
            pltpu.VMEM((points, width), bf16),
            pltpu.VMEM((n_probe, points, width), f32),
            pltpu.VMEM((n_probe * width, width), f32),
            pltpu.VMEM((n_leaf, slab, width), f32),
            pltpu.VMEM((slab, width), f32),
            pltpu.VMEM((width, tile), f32),
            pltpu.VMEM((tile, width), f32),
            pltpu.VMEM((points // 2, points), bf16),
            pltpu.VMEM((points // 2, points), bf16),
            dma((4,)),
            dma,
            dma((depth,)),
            dma((depth,)),
            dma((n_probe, 2 * pieces)),
            dma((n_probe, 2 * pieces)),
            dma((n_probe, 2 * pieces)),
            dma((n_probe, 2 * pieces)),
            dma((n_leaf,)),
            dma((n_leaf,)),
            dma((fan,)),
            dma((fan,)),
        ],
        compiler_params=pltpu.CompilerParams(
            collective_id=0, has_side_effects=True, vmem_limit_bytes=67043328
        ),
    )(block_mask, leaf_blocks, row_factor_stack, column_factor_stack, probes)


def hub_kernel(
    n_leaf, n_probe, parts,
    mask_hbm, block_hbm, row_hbm, col_hbm, probe_hbm, app, gram_ref,
    mask, block, row, col, probe, probe_h, probe_l, block_h, block_l, row_h, row_l,
    own, pair_in, pair_sum, group_in, sib, sib_h, sib_l, app_h, app_l, near_other,
    got_probe, got_sib, got_turned, turned, pairs, arrived, summed, straight, crossed, diag, diag_in, diag_sum, shares,
    load_sem, pair_send, pair_recv, group_send, group_recv, half_send, half_recv,
    probe_send, probe_recv, sib_send, sib_recv, turned_send, turned_recv,
    part_send, part_recv, straight_send, straight_recv, crossed_send, crossed_recv, swap_send, swap_recv, share_send, share_recv, ready, go,
):
    depth, rank = row.shape[0], row.shape[2]
    points, width = app.shape
    side = mask.shape[1]
    span = points // side
    half = points // 2
    leaf, z = lax.axis_index("leaf"), lax.axis_index("probe")
    slab = n_probe * width // n_leaf
    fan = n_leaf // n_probe
    chunk = width // parts
    last = n_probe - 1
    h = n_probe // 2
    teams = n_leaf // 2
    split_rank = rank // 2
    flow = leaf % 2
    team = leaf // 2
    mate = leaf + 1 - 2 * flow
    a, b = leaf // fan, leaf % fan

    def along(direction, position):
        return jnp.where(direction == 0, position, last - position)

    q = along(flow, z)
    is_hub = q == h
    hub = along(flow, h)

    def remote(src, dst, send, recv, to_leaf, to_z):
        return pltpu.make_async_remote_copy(
            src_ref=src, dst_ref=dst, send_sem=send, recv_sem=recv,
            device_id={"leaf": to_leaf, "probe": to_z}, device_id_type=MESH,
        )

    loads = [
        pltpu.make_async_copy(source, target, load_sem.at[i])
        for i, (source, target) in enumerate(
            ((probe_hbm, probe), (col_hbm, col), (block_hbm, block), (row_hbm, row), (mask_hbm, mask))
        )
    ]
    loads[0].start()
    loads[1].start()

    barrier = pltpu.get_barrier_semaphore()

    @pl.loop(1, n_leaf)
    def _(k):
        pl.semaphore_signal(
            barrier, inc=1, device_id={"leaf": (leaf + k) % n_leaf, "probe": z}, device_id_type=MESH
        )

    @pl.loop(0, n_probe)
    def _(k):
        @pl.when((k != z) & (jnp.abs(k - z) < last))
        def _():
            pl.semaphore_signal(barrier, inc=1, device_id={"leaf": leaf, "probe": k}, device_id_type=MESH)

    pl.semaphore_wait(barrier, n_leaf - 1 + last - jnp.where((z == 0) | (z == last), 1, 0))

    sides = [k for k in range(n_probe) if abs(k - h) == 1]
    distant = [k for k in range(n_probe) if abs(k - h) > 1]
    is_side = jnp.abs(q - h) == 1
    place = jnp.where(q > h, 1, 0)

    def give_probe(slot):
        return remote(probe_hbm, got_probe.at[slot], probe_send, probe_recv.at[slot], leaf, hub)

    @pl.when(is_side)
    def _():
        give_probe(place).start()

    loads[0].wait()
    ph, plo = split(probe[...])
    probe_h[...] = ph
    probe_l[...] = plo
    loads[1].wait()
    loads[4].start()
    loads[2].start()
    loads[3].start()
    columns = jnp.concatenate([col[level] for level in range(depth)], axis=1)
    own[...] = dot3(split(columns), (probe_h[...], probe_l[...]), CONTRACT_ROWS).reshape(own.shape)

    @pl.loop(1, n_leaf)
    def _(k):
        pl.semaphore_signal(
            ready, inc=1, device_id={"leaf": (leaf + k) % n_leaf, "probe": z}, device_id_type=MESH
        )

    first_level = remote(own.at[0], sib.at[0], pair_send.at[0], pair_recv.at[0], mate, z)
    upper_levels = remote(
        own.at[pl.ds(1, depth - 1), pl.ds(pl.multiple_of((1 - flow) * split_rank, split_rank), split_rank)],
        pair_in, pair_send.at[1], pair_recv.at[1], mate, z,
    )
    upper_levels.start()
    first_level.start()
    mine = pl.ds(pl.multiple_of(flow * split_rank, split_rank), split_rank)

    def to_group(level, k):
        members = 2 ** (level - 1)
        base = leaf - leaf % 2**level + (1 - 2 * ((leaf // 2**level) % 2)) * 2**level
        from_slot = members - 1 + (leaf % 2**level) // 2
        return remote(
            pair_sum.at[level - 1], group_in.at[from_slot],
            group_send.at[members - 1 + k], group_recv.at[from_slot], base + 2 * k + flow, z,
        )

    def from_group(level, k):
        members = 2 ** (level - 1)
        return remote(
            pair_sum.at[level - 1], group_in.at[members - 1 + k],
            group_send.at[members - 1 + k], group_recv.at[members - 1 + k], mate, z,
        )

    upper_levels.wait_recv()
    for level in range(1, depth):
        pair_sum[level - 1] = own[level, mine, :] + pair_in[level - 1]
    for level in reversed(range(1, depth)):
        @pl.loop(0, 2 ** (level - 1))
        def _(k):
            to_group(level, k).start()

    loads[4].wait()
    loads[2].wait()

    @pl.loop(0, side)
    def _(line):
        rows = pl.ds(pl.multiple_of(line * span, span), span)
        strips = [
            block[rows, j * span : (j + 1) * span] * mask[0, line, j].astype(jnp.float32)
            for j in range(side)
        ]
        block_h[rows, :], block_l[rows, :] = split(jnp.concatenate(strips, axis=1))

    def near(target):
        @pl.loop(0, 2)
        def _(i):
            rows = pl.ds(pl.multiple_of(i * half, half), half)
            target[rows, :] = dot3(
                (block_h[rows, :], block_l[rows, :]), (probe_h[...], probe_l[...]), PLAIN
            )

    near(app)
    loads[3].wait()
    for level in range(depth):
        row_h[:, level * rank : (level + 1) * rank], row_l[:, level * rank : (level + 1) * rank] = split(row[level])

    for level in range(1, depth):
        @pl.loop(0, 2 ** (level - 1))
        def _(k):
            from_group(level, k).wait_recv()

        begin = 2 ** (level - 1) - 1
        value = group_in[begin]
        for k in range(1, 2 ** (level - 1)):
            value = value + group_in[begin + k]
        sib[level, mine, :] = value

    half_copy = remote(
        sib.at[pl.ds(1, depth - 1), mine], sib.at[pl.ds(1, depth - 1), mine], half_send, half_recv, mate, z
    )
    half_copy.start()
    first_level.wait_recv()
    half_copy.wait_recv()

    def give_sib(slot, level):
        return remote(
            sib.at[level], got_sib.at[slot, level], sib_send.at[level], sib_recv.at[slot, level], leaf, hub
        )

    @pl.when(is_side)
    def _():
        for level in range(depth):
            give_sib(place, level).start()

    def far(source, base, target, slot):
        flat = source[...].reshape(depth * rank, width)
        sib_h[...], sib_l[...] = split(flat)

        @pl.loop(0, 2)
        def _(i):
            rows = pl.ds(pl.multiple_of(i * half, half), half)
            value = base[rows, :] + dot3((row_h[rows, :], row_l[rows, :]), (sib_h[...], sib_l[...]), PLAIN)
            if target is not None:
                target[rows, :] = value
            app_h[slot, rows, :], app_l[slot, rows, :] = split(value)

    far(sib, app, app, h)

    def rows_of(c):
        return pl.ds(pl.multiple_of(c * chunk, chunk), chunk)

    def give_turned(c):
        return remote(
            turned.at[rows_of(c)], got_turned.at[rows_of(c)], turned_send.at[c], turned_recv.at[c], leaf, hub
        )

    @pl.when(q == 0)
    def _():
        per = 128 // chunk
        for strip in range(width // 128):
            lanes = slice(strip * 128, (strip + 1) * 128)
            turned[lanes, :] = app[:, lanes].T

    diag[...] = dot3((app_h[h], app_l[h]), (app_h[h], app_l[h]), CONTRACT_ROWS)

    def slab_of(k):
        return pl.ds(pl.multiple_of(k * slab, slab), slab)

    swap = remote(diag.at[slab_of(1 - flow)], diag_in, swap_send, swap_recv, mate, z)
    swap.start()
    share = remote(diag_sum, shares.at[team], share_send, share_recv.at[team], z * fan + flow, z)

    def give_share():
        swap.wait_recv()
        diag_sum[...] = diag[slab_of(flow), :] + diag_in[...]

        @pl.when(a != z)
        def _():
            share.start()

    order = [(i, j) for j in range(n_probe) for i in range(j)]
    seat = {(i, j): 1 if (i, j) == (1, last) else j for i, j in order}

    def part_copy(i, j, c):
        pid = order.index((i, j))
        return remote(
            pairs.at[pid, rows_of(c)], arrived.at[i, team, rows_of(c)],
            part_send.at[pid, c], part_recv.at[i, team, c], along(flow, seat[i, j]) * fan + 1 - flow, z,
        )

    give_share()

    @pl.when(is_side)
    def _():
        for level in range(depth):
            give_sib(place, level).wait_send()

        @pl.when(q < h)
        def _():
            pl.semaphore_signal(go, inc=1, device_id={"leaf": leaf, "probe": along(flow, 0)}, device_id_type=MESH)

        @pl.when(q > h)
        def _():
            pl.semaphore_signal(go, inc=1, device_id={"leaf": mate, "probe": z}, device_id_type=MESH)

    @pl.when(q == 0)
    def _():
        pl.semaphore_wait(go, 2)

        @pl.loop(0, parts)
        def _(c):
            give_turned(c).start()

    @pl.when(is_hub)
    def _():
        for slot, k in enumerate(sides):
            give_probe(slot).wait_recv()
            ph, plo = split(got_probe[slot])
            probe_h[...] = ph
            probe_l[...] = plo
            near(near_other.at[slot])

        def pair(i, j):
            pairs[order.index((i, j))] = dot3((app_h[i], app_l[i]), (app_h[j], app_l[j]), CONTRACT_ROWS)

            @pl.loop(0, parts)
            def _(c):
                part_copy(i, j, c).start()

        for slot, k in enumerate(sides):
            for level in range(depth):
                give_sib(slot, level).wait_recv()
            far(got_sib.at[slot], near_other.at[slot], None, k)
            pair(min(k, h), max(k, h))
        pair(*sides)

    def late(c):
        @pl.when(is_hub)
        def _():
            give_turned(c).wait_recv()
            high, low = split(got_turned[rows_of(c), :])
            stacked = jnp.concatenate([high, low], axis=0)
            dot = functools.partial(lax.dot_general, dimension_numbers=PLAIN, preferred_element_type=jnp.float32)
            for j in range(1, n_probe):
                both = dot(stacked, app_h[j])
                pairs[order.index((0, j)), rows_of(c), :] = both[:chunk] + (dot(high, app_l[j]) + both[chunk:])
                part_copy(0, j, c).start()

    current = 1 - flow
    collects = z == along(current, h)
    position = along(current, a)

    def arrival(i, m, c):
        return remote(
            arrived.at[i, m, rows_of(c)], arrived.at[i, m, rows_of(c)],
            part_send.at[0, c], part_recv.at[i, m, c], mate, z,
        )

    per_slab = slab // chunk

    def holds(i):
        match = [j for j in range(n_probe) if (i, j) in seat]
        found = jnp.bool_(False)
        partner = position
        for j in match:
            found = found | (position == seat[i, j])
            if seat[i, j] != j:
                partner = jnp.where(position == seat[i, j], j, partner)
        return collects & found, along(current, partner)

    def send_crossed(i, c, k):
        return remote(
            summed.at[i, rows_of(c), k * slab : (k + 1) * slab], crossed.at[rows_of(c)],
            crossed_send.at[i, c, k], crossed_recv.at[c], holds(i)[1] * fan + k, along(current, i),
        )

    def send_straight(i, c):
        return remote(
            summed.at[i, rows_of(c)], straight.at[rows_of(c % per_slab)],
            straight_send.at[i, c], straight_recv.at[c % per_slab],
            along(current, i) * fan + c // per_slab, holds(i)[1],
        )

    def collect(i, c):
        @pl.when(holds(i)[0])
        def _():
            for m in range(teams):
                arrival(i, m, c).wait_recv()
            value = arrived[i, 0, rows_of(c), :]
            for m in range(1, teams):
                value = value + arrived[i, m, rows_of(c), :]
            summed[i, rows_of(c), :] = value
            send_straight(i, c).start()
            for k in range(fan):
                if i == h:

                    @pl.when(flow == k)
                    def _():
                        crossed[rows_of(c), :] = value[:, k * slab : (k + 1) * slab]

                    @pl.when(flow != k)
                    def _():
                        send_crossed(i, c, k).start()

                else:
                    send_crossed(i, c, k).start()

    def collect_all(i, begin, end):
        @pl.loop(begin, end)
        def _(c):
            collect(i, c)

    def cross(i):
        @pl.when(holds(i)[0])
        def _():
            @pl.loop(0, parts)
            def _(c):
                for k in range(fan):
                    send_crossed(i, c, k).start()

    @pl.loop(0, parts)
    def _(c):
        late(c)

    pl.semaphore_wait(ready, n_leaf - 1)
    for i in range(1, n_probe - 1):
        collect_all(i, 0, parts)
    collect_all(0, 0, parts - 2)
    collect_all(0, parts - 2, parts)

    scale = 1.0 / (points * n_leaf)

    @pl.when(a == z)
    def _():
        shares[team] = diag_sum[...]

        @pl.loop(1, teams)
        def _(k):
            other = (team + k) % teams
            remote(diag_sum, shares.at[other], share_send, share_recv.at[other], mate, z).wait_recv()

        value = shares[0]
        for k in range(1, teams):
            value = value + shares[k]
        gram_ref[...] = value * scale

    @pl.when(a != z)
    def _():
        back = jnp.where(z < a, 0, 1)

        @pl.when((along(back, h) != z) | (flow == back))
        def _():
            @pl.loop(0, parts)
            def _(c):
                remote(
                    summed.at[0, rows_of(c), 0:slab], crossed.at[rows_of(c)],
                    crossed_send.at[0, c, 0], crossed_recv.at[c], mate, z,
                ).wait_recv()

        @pl.loop(0, per_slab)
        def _(c):
            remote(
                summed.at[0, rows_of(c)], straight.at[rows_of(c)],
                straight_send.at[0, c], straight_recv.at[c], mate, z,
            ).wait_recv()

        gram_ref[...] = (straight[...] + crossed[...].T) * scale

    first_level.wait_send()
    upper_levels.wait_send()
    half_copy.wait_send()
    for level in range(1, depth):
        @pl.loop(0, 2 ** (level - 1))
        def _(k):
            to_group(level, k).wait_send()

    @pl.when(is_side)
    def _():
        give_probe(place).wait_send()

    @pl.when(q == 0)
    def _():
        @pl.loop(0, parts)
        def _(c):
            give_turned(c).wait_send()

    swap.wait_send()

    @pl.when(a != z)
    def _():
        share.wait_send()

    @pl.when(is_hub)
    def _():
        for i, j in order:

            @pl.loop(0, parts)
            def _(c):
                part_copy(i, j, c).wait_send()

    for i in range(n_probe - 1):

        @pl.when(holds(i)[0])
        def _():
            @pl.loop(0, parts)
            def _(c):
                send_straight(i, c).wait_send()
                for k in range(fan):
                    if i == h:

                        @pl.when(flow != k)
                        def _():
                            send_crossed(i, c, k).wait_send()

                    else:
                        send_crossed(i, c, k).wait_send()


def hub_local(n_leaf, n_probe, leaf_blocks, block_mask, row_factor_stack, column_factor_stack, probes):
    depth, points, rank = row_factor_stack.shape
    width = probes.shape[1]
    slab = n_probe * width // n_leaf
    fan = n_leaf // n_probe
    parts = 2 * width // slab
    teams = n_leaf // 2
    count = n_probe * (n_probe - 1) // 2
    f32, bf16 = jnp.float32, jnp.bfloat16
    dma = pltpu.SemaphoreType.DMA
    hbm = pl.BlockSpec(memory_space=pltpu.HBM)
    groups = 2 ** (depth - 1) - 1
    return pl.pallas_call(
        functools.partial(hub_kernel, n_leaf, n_probe, parts),
        out_shape=(
            pltpu.VMEM((points, width), f32),
            pltpu.VMEM((slab, width), f32),
        ),
        in_specs=[hbm] * 5,
        out_specs=(pl.BlockSpec(memory_space=pltpu.VMEM), pl.BlockSpec(memory_space=pltpu.VMEM)),
        scratch_shapes=[
            pltpu.SMEM(block_mask.shape, block_mask.dtype),
            pltpu.VMEM((points, points), f32),
            pltpu.VMEM((depth, points, rank), f32),
            pltpu.VMEM((depth, points, rank), f32),
            pltpu.VMEM((points, width), f32),
            pltpu.VMEM((points, width), bf16),
            pltpu.VMEM((points, width), bf16),
            pltpu.VMEM((points, points), bf16),
            pltpu.VMEM((points, points), bf16),
            pltpu.VMEM((points, depth * rank), bf16),
            pltpu.VMEM((points, depth * rank), bf16),
            pltpu.VMEM((depth, rank, width), f32),
            pltpu.VMEM((depth - 1, rank // 2, width), f32),
            pltpu.VMEM((depth - 1, rank // 2, width), f32),
            pltpu.VMEM((groups, rank // 2, width), f32),
            pltpu.VMEM((depth, rank, width), f32),
            pltpu.VMEM((depth * rank, width), bf16),
            pltpu.VMEM((depth * rank, width), bf16),
            pltpu.VMEM((n_probe, points, width), bf16),
            pltpu.VMEM((n_probe, points, width), bf16),
            pltpu.VMEM((2, points, width), f32),
            pltpu.VMEM((2, points, width), f32),
            pltpu.VMEM((2, depth, rank, width), f32),
            pltpu.VMEM((width, points), f32),
            pltpu.VMEM((width, points), f32),
            pltpu.VMEM((count, width, width), f32),
            pltpu.VMEM((n_probe - 1, teams, width, width), f32),
            pltpu.VMEM((n_probe - 1, width, width), f32),
            pltpu.VMEM((slab, width), f32),
            pltpu.VMEM((width, slab), f32),
            pltpu.VMEM((width, width), f32),
            pltpu.VMEM((slab, width), f32),
            pltpu.VMEM((slab, width), f32),
            pltpu.VMEM((teams, slab, width), f32),
            dma((5,)),
            dma((2,)),
            dma((2,)),
            dma((groups,)),
            dma((groups,)),
            dma,
            dma,
            dma,
            dma((2,)),
            dma((depth,)),
            dma((2, depth)),
            dma((parts,)),
            dma((parts,)),
            dma((count, parts)),
            dma((n_probe - 1, teams, parts)),
            dma((n_probe - 1, parts)),
            dma((slab * parts // width,)),
            dma((n_probe - 1, parts, fan)),
            dma((parts,)),
            dma,
            dma,
            dma,
            dma((teams,)),
            pltpu.SemaphoreType.REGULAR,
            pltpu.SemaphoreType.REGULAR,
        ],
        compiler_params=pltpu.CompilerParams(
            collective_id=0, has_side_effects=True, vmem_limit_bytes=56 * 2**20
        ),
    )(block_mask, leaf_blocks, row_factor_stack, column_factor_stack, probes)


def local(n_leaf, n_probe, *arrays):
    width = arrays[-1].shape[1]
    whole_lanes = (n_probe * width) % (128 * n_leaf) == 0
    if n_probe == 4 and n_leaf == 2 * n_probe and whole_lanes:
        return hub_local(n_leaf, n_probe, *arrays)
    return ring(n_leaf, n_probe, *arrays)


def solution(mesh):
    return jax.shard_map(
        functools.partial(local, mesh.shape["leaf"], mesh.shape["probe"]),
        mesh=mesh,
        in_specs=(
            P("leaf", None),
            P("leaf", None, None),
            P(None, "leaf", None),
            P(None, "leaf", None),
            P("leaf", "probe"),
        ),
        out_specs=(P("leaf", "probe"), P("leaf", "probe")),
        check_vma=False,
    )
```

```python
import functools

import jax
import jax.numpy as jnp
from jax import lax
from jax.experimental import pallas as pl
from jax.experimental.pallas import tpu as pltpu
from jax.sharding import PartitionSpec as P

MESH = pl.DeviceIdType.MESH
CONTRACT_ROWS = (((0,), (0,)), ((), ()))
PLAIN = (((1,), (0,)), ((), ()))


def split(value):
    high = value.astype(jnp.bfloat16)
    return high, (value - high.astype(jnp.float32)).astype(jnp.bfloat16)


def dot3(left, right, dims):
    (lh, ll), (rh, rl) = left, right
    dot = functools.partial(lax.dot_general, dimension_numbers=dims, preferred_element_type=jnp.float32)
    return dot(lh, rh) + (dot(lh, rl) + dot(ll, rh))


def ring_kernel(
    n_leaf, n_probe, pieces,
    mask, block_hbm, row_hbm, col_hbm, probe_hbm, app_hbm, gram_ref,
    block, row, col, probe, probe_h, probe_l, own, swap, sib_h, sib_l,
    app, app_h, app_l, got, part, shares, total, extra, turned, kept_h, kept_l,
    load_sem, out_sem, swap_send, swap_recv, right_send, right_recv, left_send, left_recv,
    share_send, share_recv, extra_send, extra_recv,
):
    depth, rank = row.shape[0], row.shape[2]
    points, width = app.shape
    side = mask.shape[1]
    span = points // side
    half = points // 2
    piece = half // pieces
    leaf, z = lax.axis_index("leaf"), lax.axis_index("probe")
    slab = n_probe * width // n_leaf
    fan = n_leaf // n_probe
    a, b = leaf // fan, leaf % fan
    last = n_probe - 1
    ends = n_probe > 2

    loads = [
        pltpu.make_async_copy(source, target, load_sem.at[i])
        for i, (source, target) in enumerate(
            ((probe_hbm, probe), (col_hbm, col), (block_hbm, block), (row_hbm, row))
        )
    ]
    loads[0].start()
    loads[1].start()

    barrier = pltpu.get_barrier_semaphore()

    @pl.loop(1, n_leaf)
    def _(k):
        pl.semaphore_signal(
            barrier, inc=1, device_id={"leaf": (leaf + k) % n_leaf, "probe": z}, device_id_type=MESH
        )

    @pl.when(z > 0)
    def _():
        pl.semaphore_signal(barrier, inc=1, device_id={"leaf": leaf, "probe": z - 1}, device_id_type=MESH)

    @pl.when(z < last)
    def _():
        pl.semaphore_signal(barrier, inc=1, device_id={"leaf": leaf, "probe": z + 1}, device_id_type=MESH)

    @pl.when(a != z)
    def _():
        @pl.loop(0, fan)
        def _(c):
            pl.semaphore_signal(
                barrier, inc=1, device_id={"leaf": z * fan + c, "probe": a}, device_id_type=MESH
            )

    loads[0].wait()
    ph, plo = split(probe[...])
    probe_h[...] = ph
    probe_l[...] = plo
    loads[1].wait()
    loads[2].start()
    loads[3].start()
    columns = jnp.concatenate([col[level] for level in range(depth)], axis=1)
    own[...] = dot3(split(columns), (probe_h[...], probe_l[...]), CONTRACT_ROWS).reshape(own.shape)

    peers = n_leaf - 1 + jnp.where(z > 0, 1, 0) + jnp.where(z < last, 1, 0) + jnp.where(a != z, fan, 0)
    pl.semaphore_wait(barrier, peers)

    def exchange(step):
        away = 2**step
        other = leaf + (1 - 2 * ((leaf // away) % 2)) * away
        start = sum(depth - s for s in range(step))
        return start, pltpu.make_async_remote_copy(
            src_ref=own.at[pl.ds(step, depth - step)],
            dst_ref=swap.at[pl.ds(start, depth - step)],
            send_sem=swap_send.at[step],
            recv_sem=swap_recv.at[step],
            device_id={"leaf": other, "probe": z},
            device_id_type=MESH,
        )

    def near(which):
        @pl.loop(0, side // 2)
        def _(i):
            line = which * (side // 2) + i
            rows = pl.ds(pl.multiple_of(line * span, span), span)
            strips = [
                block[rows, j * span : (j + 1) * span] * mask[0, line, j].astype(jnp.float32)
                for j in range(side)
            ]
            into = pl.ds(pl.multiple_of(i * span, span), span)
            kept_h[into, :], kept_l[into, :] = split(jnp.concatenate(strips, axis=1))

        app[which * half : (which + 1) * half, :] = dot3(
            (kept_h[...], kept_l[...]), (probe_h[...], probe_l[...]), PLAIN
        )

    for step in range(depth):
        start, copy = exchange(step)
        copy.start()
        if step == 0:
            loads[2].wait()
        for which in range(2):
            if step == min(which, depth - 1):
                near(which)
        copy.wait()
        sib_h[step * rank : (step + 1) * rank, :], sib_l[step * rank : (step + 1) * rank, :] = split(
            swap[start]
        )
        for level in range(step + 1, depth):
            own[level] = own[level] + swap[start + level - step]

    def ship(source, to, slot, begin, send, recv):
        rows = pl.ds(pl.multiple_of(begin, piece), piece)
        return pltpu.make_async_remote_copy(
            src_ref=source.at[rows] if source is app else source.at[slot, rows],
            dst_ref=got.at[slot, rows],
            send_sem=send.at[slot, begin // piece],
            recv_sem=recv.at[slot, begin // piece],
            device_id={"leaf": leaf, "probe": to},
            device_id_type=MESH,
        )

    def rightward(source, slot, begin):
        return ship(source, jnp.minimum(z + 1, last), slot, begin, right_send, right_recv)

    def leftward(source, slot, begin):
        return ship(source, jnp.maximum(z - 1, 0), slot, begin, left_send, left_recv)

    loads[3].wait()
    sends_right = (z < last - 1) if ends else (z < last)
    sends_left = (z > 1) if ends else (z > 0)

    def far(which):
        rows = slice(which * half, (which + 1) * half)
        factors = jnp.concatenate([row[level, rows, :] for level in range(depth)], axis=1)
        value = app[rows, :] + dot3(split(factors), (sib_h[...], sib_l[...]), PLAIN)
        app[rows, :] = value
        app_h[rows, :], app_l[rows, :] = split(value)

    far(0)

    @pl.when(sends_right)
    def _():
        @pl.loop(0, pieces)
        def _(c):
            rightward(app, z, c * piece).start()

    far(1)

    @pl.when(sends_left)
    def _():
        @pl.loop(0, pieces)
        def _(c):
            leftward(app, z, half + c * piece).start()

    if ends:
        @pl.loop(0, pieces)
        def _(c):
            @pl.when(z == 0)
            def _():
                rightward(app, z, half + c * piece).start()

            @pl.when(z == last)
            def _():
                leftward(app, z, c * piece).start()

    keep = pltpu.make_async_copy(app, app_hbm, out_sem)
    keep.start()

    def gram(slot, source, begin, fresh):
        into = pl.ds(pl.multiple_of(slot * width, width), width)
        rows = pl.ds(pl.multiple_of(begin, half), half)
        here = (app_h[rows, :], app_l[rows, :])
        there = here if source is None else split(source[slot, rows, :])
        value = dot3(there, here, CONTRACT_ROWS)
        part[into, :] = value if fresh else part[into, :] + value

    def share(k):
        to = (leaf + k) % n_leaf
        return pltpu.make_async_remote_copy(
            src_ref=part.at[pl.ds(pl.multiple_of(to * slab, slab), slab)],
            dst_ref=shares.at[k],
            send_sem=share_send.at[k],
            recv_sem=share_recv.at[k],
            device_id={"leaf": to, "probe": z},
            device_id_type=MESH,
        )

    def give(slot):
        @pl.loop(0, fan)
        def _(c):
            to = slot * fan + c

            @pl.when(to != leaf)
            def _():
                share((to - leaf + n_leaf) % n_leaf).start()

    part[...] = jnp.zeros_like(part)

    @pl.loop(0, 2)
    def _(h):
        gram(z, None, h * half, False)

    give(z)

    @pl.loop(1, n_probe)
    def _(d):
        from_left = (z - d >= 0) & ((z < last) | (d > 1) | (not ends))
        from_right = (z + d <= last) & ((z > 0) | (d > 1) | (not ends))
        low_slot, high_slot = jnp.maximum(z - d, 0), jnp.minimum(z + d, last)

        @pl.loop(0, pieces)
        def _(c):
            up, low = c * piece, half + c * piece

            @pl.when(from_left)
            def _():
                rightward(got, low_slot, up).wait_recv()

                @pl.when(z < last)
                def _():
                    rightward(got, low_slot, up).start()

            @pl.when(from_right)
            def _():
                leftward(got, high_slot, low).wait_recv()

                @pl.when(z > 0)
                def _():
                    leftward(got, high_slot, low).start()

        @pl.loop(0, 2)
        def _(h):
            @pl.when(jnp.where(h == 0, from_left, from_right))
            def _():
                slot = jnp.where(h == 0, low_slot, high_slot)
                gram(slot, got, h * half, False)
                whole = (d > 1) | jnp.where(h == 0, z != 1, z != last - 1) | (not ends)

                @pl.when(whole)
                def _():
                    give(slot)

    if ends:
        at_low, at_high = z == 1, z == last - 1

        @pl.loop(0, pieces)
        def _(c):
            @pl.when(at_low)
            def _():
                rightward(got, z - 1, half + c * piece).wait_recv()

            @pl.when(at_high)
            def _():
                leftward(got, z + 1, c * piece).wait_recv()

        @pl.loop(0, 2)
        def _(h):
            @pl.when(jnp.where(h == 0, at_high, at_low))
            def _():
                slot = jnp.where(h == 0, jnp.minimum(z + 1, last), jnp.maximum(z - 1, 0))
                gram(slot, got, h * half, False)
                give(slot)

    total[...] = part[pl.ds(pl.multiple_of(leaf * slab, slab), slab), :]

    def holds(slot):
        return (not ends) | (((z > 0) | (slot != 1)) & ((z < last) | (slot != last - 1)))

    @pl.when(holds(a))
    def _():
        @pl.loop(1, n_leaf)
        def _(k):
            share(k).wait_recv()
            total[...] = total[...] + shares[k]

    scale = 1.0 / (points * n_leaf)

    tile = extra.shape[1]

    def trade(c, at):
        return pltpu.make_async_remote_copy(
            src_ref=total if tile == width else total.at[:, pl.ds(pl.multiple_of(c * tile, tile), tile)],
            dst_ref=extra.at[pl.ds(pl.multiple_of(at * slab, slab), slab)],
            send_sem=extra_send.at[c],
            recv_sem=extra_recv.at[at],
            device_id={"leaf": z * fan + c, "probe": a},
            device_id_type=MESH,
        )

    @pl.when(a != z)
    def _():
        @pl.loop(0, fan)
        def _(c):
            trade(c, b).start()

        @pl.loop(0, fan)
        def _(c):
            trade(c, c).wait_recv()

        turned[...] = extra[...].T
        skip = 0 if tile == slab else pl.multiple_of(b * slab, slab)
        gram_ref[...] = (total[...] + turned[pl.ds(skip, slab), :]) * scale

        @pl.loop(0, fan)
        def _(c):
            trade(c, b).wait_send()

    @pl.when(a == z)
    def _():
        gram_ref[...] = total[...] * scale

    @pl.loop(0, pieces)
    def _(c):
        up, low = c * piece, half + c * piece

        @pl.when(sends_right)
        def _():
            rightward(app, z, up).wait_send()

        @pl.when(sends_left)
        def _():
            leftward(app, z, low).wait_send()

        if ends:

            @pl.when(z == 0)
            def _():
                rightward(app, z, low).wait_send()

            @pl.when(z == last)
            def _():
                leftward(app, z, up).wait_send()

        @pl.loop(1, n_probe)
        def _(d):
            @pl.when((z - d >= 0) & (z < last))
            def _():
                rightward(got, jnp.maximum(z - d, 0), up).wait_send()

            @pl.when((z + d <= last) & (z > 0))
            def _():
                leftward(got, jnp.minimum(z + d, last), low).wait_send()

    @pl.loop(1, n_leaf)
    def _(k):
        @pl.when(holds(((leaf + k) % n_leaf) // fan))
        def _():
            share(k).wait_send()

    keep.wait()


def ring(n_leaf, n_probe, leaf_blocks, block_mask, row_factor_stack, column_factor_stack, probes):
    depth, points, rank = row_factor_stack.shape
    width = probes.shape[1]
    slab = n_probe * width // n_leaf
    fan = n_leaf // n_probe
    pieces = 4
    tile = slab if slab % 128 == 0 else width
    f32, bf16 = jnp.float32, jnp.bfloat16
    dma = pltpu.SemaphoreType.DMA
    hbm = pl.BlockSpec(memory_space=pltpu.HBM)
    return pl.pallas_call(
        functools.partial(ring_kernel, n_leaf, n_probe, pieces),
        out_shape=(
            jax.ShapeDtypeStruct((points, width), f32),
            jax.ShapeDtypeStruct((slab, width), f32),
        ),
        in_specs=[pl.BlockSpec(memory_space=pltpu.SMEM), hbm, hbm, hbm, hbm],
        out_specs=(hbm, pl.BlockSpec(memory_space=pltpu.VMEM)),
        scratch_shapes=[
            pltpu.VMEM((points, points), f32),
            pltpu.VMEM((depth, points, rank), f32),
            pltpu.VMEM((depth, points, rank), f32),
            pltpu.VMEM((points, width), f32),
            pltpu.VMEM((points, width), bf16),
            pltpu.VMEM((points, width), bf16),
            pltpu.VMEM((depth, rank, width), f32),
            pltpu.VMEM((depth * (depth + 1) // 2, rank, width), f32),
            pltpu.VMEM((depth * rank, width), bf16),
            pltpu.VMEM((depth * rank, width), bf16),
            pltpu.VMEM((points, width), f32),
            pltpu.VMEM((points, width), bf16),
            pltpu.VMEM((points, width), bf16),
            pltpu.VMEM((n_probe, points, width), f32),
            pltpu.VMEM((n_probe * width, width), f32),
            pltpu.VMEM((n_leaf, slab, width), f32),
            pltpu.VMEM((slab, width), f32),
            pltpu.VMEM((width, tile), f32),
            pltpu.VMEM((tile, width), f32),
            pltpu.VMEM((points // 2, points), bf16),
            pltpu.VMEM((points // 2, points), bf16),
            dma((4,)),
            dma,
            dma((depth,)),
            dma((depth,)),
            dma((n_probe, 2 * pieces)),
            dma((n_probe, 2 * pieces)),
            dma((n_probe, 2 * pieces)),
            dma((n_probe, 2 * pieces)),
            dma((n_leaf,)),
            dma((n_leaf,)),
            dma((fan,)),
            dma((fan,)),
        ],
        compiler_params=pltpu.CompilerParams(
            collective_id=0, has_side_effects=True, vmem_limit_bytes=67043328
        ),
    )(block_mask, leaf_blocks, row_factor_stack, column_factor_stack, probes)


def hub_kernel(
    n_leaf, n_probe, parts,
    mask_hbm, block_hbm, row_hbm, col_hbm, probe_hbm, app, gram_ref,
    mask, block, row, col, probe, probe_h, probe_l, block_h, block_l, row_h, row_l,
    own, pair_in, pair_sum, group_in, sib, sib_h, sib_l, app_h, app_l, near_other,
    got_probe, got_sib, got_turned, turned, pairs, arrived, summed, straight, crossed, diag, diag_in, diag_sum, shares,
    load_sem, pair_send, pair_recv, group_send, group_recv, half_send, half_recv,
    probe_send, probe_recv, sib_send, sib_recv, turned_send, turned_recv,
    part_send, part_recv, straight_send, straight_recv, crossed_send, crossed_recv, swap_send, swap_recv, share_send, share_recv, ready, go,
):
    depth, rank = row.shape[0], row.shape[2]
    points, width = app.shape
    side = mask.shape[1]
    span = points // side
    half = points // 2
    leaf, z = lax.axis_index("leaf"), lax.axis_index("probe")
    slab = n_probe * width // n_leaf
    fan = n_leaf // n_probe
    chunk = width // parts
    last = n_probe - 1
    h = n_probe // 2
    teams = n_leaf // 2
    split_rank = rank // 2
    flow = leaf % 2
    team = leaf // 2
    mate = leaf + 1 - 2 * flow
    a, b = leaf // fan, leaf % fan

    def along(direction, position):
        return jnp.where(direction == 0, position, last - position)

    q = along(flow, z)
    is_hub = q == h
    hub = along(flow, h)

    def remote(src, dst, send, recv, to_leaf, to_z):
        return pltpu.make_async_remote_copy(
            src_ref=src, dst_ref=dst, send_sem=send, recv_sem=recv,
            device_id={"leaf": to_leaf, "probe": to_z}, device_id_type=MESH,
        )

    loads = [
        pltpu.make_async_copy(source, target, load_sem.at[i])
        for i, (source, target) in enumerate(
            ((probe_hbm, probe), (col_hbm, col), (block_hbm, block), (row_hbm, row), (mask_hbm, mask))
        )
    ]
    loads[0].start()
    loads[1].start()

    barrier = pltpu.get_barrier_semaphore()

    @pl.loop(1, n_leaf)
    def _(k):
        pl.semaphore_signal(
            barrier, inc=1, device_id={"leaf": (leaf + k) % n_leaf, "probe": z}, device_id_type=MESH
        )

    @pl.loop(0, n_probe)
    def _(k):
        @pl.when((k != z) & (jnp.abs(k - z) < last))
        def _():
            pl.semaphore_signal(barrier, inc=1, device_id={"leaf": leaf, "probe": k}, device_id_type=MESH)

    pl.semaphore_wait(barrier, n_leaf - 1 + last - jnp.where((z == 0) | (z == last), 1, 0))

    sides = [k for k in range(n_probe) if abs(k - h) == 1]
    distant = [k for k in range(n_probe) if abs(k - h) > 1]
    is_side = jnp.abs(q - h) == 1
    place = jnp.where(q > h, 1, 0)

    def give_probe(slot):
        return remote(probe_hbm, got_probe.at[slot], probe_send, probe_recv.at[slot], leaf, hub)

    @pl.when(is_side)
    def _():
        give_probe(place).start()

    loads[0].wait()
    ph, plo = split(probe[...])
    probe_h[...] = ph
    probe_l[...] = plo
    loads[1].wait()
    loads[4].start()
    loads[2].start()
    loads[3].start()
    columns = jnp.concatenate([col[level] for level in range(depth)], axis=1)
    own[...] = dot3(split(columns), (probe_h[...], probe_l[...]), CONTRACT_ROWS).reshape(own.shape)

    @pl.loop(1, n_leaf)
    def _(k):
        pl.semaphore_signal(
            ready, inc=1, device_id={"leaf": (leaf + k) % n_leaf, "probe": z}, device_id_type=MESH
        )

    first_level = remote(own.at[0], sib.at[0], pair_send.at[0], pair_recv.at[0], mate, z)
    upper_levels = remote(
        own.at[pl.ds(1, depth - 1), pl.ds(pl.multiple_of((1 - flow) * split_rank, split_rank), split_rank)],
        pair_in, pair_send.at[1], pair_recv.at[1], mate, z,
    )
    upper_levels.start()
    first_level.start()
    mine = pl.ds(pl.multiple_of(flow * split_rank, split_rank), split_rank)

    def to_group(level, k):
        members = 2 ** (level - 1)
        base = leaf - leaf % 2**level + (1 - 2 * ((leaf // 2**level) % 2)) * 2**level
        from_slot = members - 1 + (leaf % 2**level) // 2
        return remote(
            pair_sum.at[level - 1], group_in.at[from_slot],
            group_send.at[members - 1 + k], group_recv.at[from_slot], base + 2 * k + flow, z,
        )

    def from_group(level, k):
        members = 2 ** (level - 1)
        return remote(
            pair_sum.at[level - 1], group_in.at[members - 1 + k],
            group_send.at[members - 1 + k], group_recv.at[members - 1 + k], mate, z,
        )

    upper_levels.wait_recv()
    for level in range(1, depth):
        pair_sum[level - 1] = own[level, mine, :] + pair_in[level - 1]
    for level in reversed(range(1, depth)):
        @pl.loop(0, 2 ** (level - 1))
        def _(k):
            to_group(level, k).start()

    loads[4].wait()
    loads[2].wait()

    @pl.loop(0, side)
    def _(line):
        rows = pl.ds(pl.multiple_of(line * span, span), span)
        strips = [
            block[rows, j * span : (j + 1) * span] * mask[0, line, j].astype(jnp.float32)
            for j in range(side)
        ]
        block_h[rows, :], block_l[rows, :] = split(jnp.concatenate(strips, axis=1))

    def near(target):
        @pl.loop(0, 2)
        def _(i):
            rows = pl.ds(pl.multiple_of(i * half, half), half)
            target[rows, :] = dot3(
                (block_h[rows, :], block_l[rows, :]), (probe_h[...], probe_l[...]), PLAIN
            )

    near(app)
    loads[3].wait()
    for level in range(depth):
        row_h[:, level * rank : (level + 1) * rank], row_l[:, level * rank : (level + 1) * rank] = split(row[level])

    for level in range(1, depth):
        @pl.loop(0, 2 ** (level - 1))
        def _(k):
            from_group(level, k).wait_recv()

        begin = 2 ** (level - 1) - 1
        value = group_in[begin]
        for k in range(1, 2 ** (level - 1)):
            value = value + group_in[begin + k]
        sib[level, mine, :] = value

    half_copy = remote(
        sib.at[pl.ds(1, depth - 1), mine], sib.at[pl.ds(1, depth - 1), mine], half_send, half_recv, mate, z
    )
    half_copy.start()
    first_level.wait_recv()
    half_copy.wait_recv()

    def give_sib(slot, level):
        return remote(
            sib.at[level], got_sib.at[slot, level], sib_send.at[level], sib_recv.at[slot, level], leaf, hub
        )

    @pl.when(is_side)
    def _():
        for level in range(depth):
            give_sib(place, level).start()

    def far(source, base, target, slot):
        flat = source[...].reshape(depth * rank, width)
        sib_h[...], sib_l[...] = split(flat)

        @pl.loop(0, 2)
        def _(i):
            rows = pl.ds(pl.multiple_of(i * half, half), half)
            value = base[rows, :] + dot3((row_h[rows, :], row_l[rows, :]), (sib_h[...], sib_l[...]), PLAIN)
            if target is not None:
                target[rows, :] = value
            app_h[slot, rows, :], app_l[slot, rows, :] = split(value)

    far(sib, app, app, h)

    def rows_of(c):
        return pl.ds(pl.multiple_of(c * chunk, chunk), chunk)

    def give_turned(c):
        return remote(
            turned.at[rows_of(c)], got_turned.at[rows_of(c)], turned_send.at[c], turned_recv.at[c], leaf, hub
        )

    @pl.when(q == 0)
    def _():
        per = 128 // chunk
        for strip in range(width // 128):
            lanes = slice(strip * 128, (strip + 1) * 128)
            turned[lanes, :] = app[:, lanes].T

    diag[...] = dot3((app_h[h], app_l[h]), (app_h[h], app_l[h]), CONTRACT_ROWS)

    def slab_of(k):
        return pl.ds(pl.multiple_of(k * slab, slab), slab)

    swap = remote(diag.at[slab_of(1 - flow)], diag_in, swap_send, swap_recv, mate, z)
    swap.start()
    share = remote(diag_sum, shares.at[team], share_send, share_recv.at[team], z * fan + flow, z)

    def give_share():
        swap.wait_recv()
        diag_sum[...] = diag[slab_of(flow), :] + diag_in[...]

        @pl.when(a != z)
        def _():
            share.start()

    order = [(i, j) for j in range(n_probe) for i in range(j)]
    seat = {(i, j): i if j == i + 1 else j for i, j in order}

    def part_copy(i, j, c):
        pid = order.index((i, j))
        return remote(
            pairs.at[pid, rows_of(c)], arrived.at[i, team, rows_of(c)],
            part_send.at[pid, c], part_recv.at[i, team, c], along(flow, seat[i, j]) * fan + 1 - flow, z,
        )

    give_share()

    @pl.when(is_side)
    def _():
        for level in range(depth):
            give_sib(place, level).wait_send()

        @pl.when(q < h)
        def _():
            pl.semaphore_signal(go, inc=1, device_id={"leaf": leaf, "probe": along(flow, 0)}, device_id_type=MESH)

        @pl.when(q > h)
        def _():
            pl.semaphore_signal(go, inc=1, device_id={"leaf": mate, "probe": z}, device_id_type=MESH)

    @pl.when(q == 0)
    def _():
        pl.semaphore_wait(go, 2)

        @pl.loop(0, parts)
        def _(c):
            give_turned(c).start()

    @pl.when(is_hub)
    def _():
        for slot, k in enumerate(sides):
            give_probe(slot).wait_recv()
            ph, plo = split(got_probe[slot])
            probe_h[...] = ph
            probe_l[...] = plo
            near(near_other.at[slot])

        def pair(i, j):
            pairs[order.index((i, j))] = dot3((app_h[i], app_l[i]), (app_h[j], app_l[j]), CONTRACT_ROWS)

            @pl.loop(0, parts)
            def _(c):
                part_copy(i, j, c).start()

        for slot, k in enumerate(sides):
            for level in range(depth):
                give_sib(slot, level).wait_recv()
            far(got_sib.at[slot], near_other.at[slot], None, k)
            pair(min(k, h), max(k, h))
        pair(*sides)

    def late(c):
        @pl.when(is_hub)
        def _():
            give_turned(c).wait_recv()
            high, low = split(got_turned[rows_of(c), :])
            stacked = jnp.concatenate([high, low], axis=0)
            dot = functools.partial(lax.dot_general, dimension_numbers=PLAIN, preferred_element_type=jnp.float32)
            for j in range(1, n_probe):
                both = dot(stacked, app_h[j])
                pairs[order.index((0, j)), rows_of(c), :] = both[:chunk] + (dot(high, app_l[j]) + both[chunk:])
                part_copy(0, j, c).start()

    current = 1 - flow
    collects = z == along(current, h)
    position = along(current, a)

    def arrival(i, m, c):
        return remote(
            arrived.at[i, m, rows_of(c)], arrived.at[i, m, rows_of(c)],
            part_send.at[0, c], part_recv.at[i, m, c], mate, z,
        )

    per_slab = slab // chunk

    def holds(i):
        match = [j for j in range(n_probe) if (i, j) in seat]
        found = jnp.bool_(False)
        partner = position
        for j in match:
            found = found | (position == seat[i, j])
            if seat[i, j] != j:
                partner = jnp.where(position == seat[i, j], j, partner)
        return collects & found, along(current, partner)

    def kept(i, c):
        return (seat.get((i, h)) == i) & (position == i) & (c // per_slab == flow)

    def send_crossed(i, c, k):
        return remote(
            summed.at[i, rows_of(c), k * slab : (k + 1) * slab], crossed.at[rows_of(c)],
            crossed_send.at[i, c, k], crossed_recv.at[c], holds(i)[1] * fan + k, along(current, i),
        )

    def send_straight(i, c):
        return remote(
            summed.at[i, rows_of(c)], straight.at[rows_of(c % per_slab)],
            straight_send.at[i, c], straight_recv.at[c % per_slab],
            along(current, i) * fan + c // per_slab, holds(i)[1],
        )

    def collect(i, c):
        @pl.when(holds(i)[0])
        def _():
            for m in range(teams):
                arrival(i, m, c).wait_recv()
            value = arrived[i, 0, rows_of(c), :]
            for m in range(1, teams):
                value = value + arrived[i, m, rows_of(c), :]
            summed[i, rows_of(c), :] = value
            for k in range(fan):
                send_crossed(i, c, k).start()

            @pl.when(kept(i, c))
            def _():
                straight[rows_of(c % per_slab), :] = value

            @pl.when(jnp.logical_not(kept(i, c)))
            def _():
                send_straight(i, c).start()

    def collect_all(i, begin, end):
        @pl.loop(begin, end)
        def _(c):
            collect(i, c)

    @pl.loop(0, parts)
    def _(c):
        late(c)

    pl.semaphore_wait(ready, n_leaf - 1)
    for i in range(1, n_probe - 1):
        collect_all(i, 0, parts)
    collect_all(0, 0, parts)

    scale = 1.0 / (points * n_leaf)

    @pl.when(a == z)
    def _():
        shares[team] = diag_sum[...]

        @pl.loop(1, teams)
        def _(k):
            other = (team + k) % teams
            remote(diag_sum, shares.at[other], share_send, share_recv.at[other], mate, z).wait_recv()

        value = shares[0]
        for k in range(1, teams):
            value = value + shares[k]
        gram_ref[...] = value * scale

    @pl.when(a != z)
    def _():
        back = jnp.where(z < a, 0, 1)

        @pl.loop(0, parts)
        def _(c):
            remote(
                summed.at[0, rows_of(c), 0:slab], crossed.at[rows_of(c)],
                crossed_send.at[0, c, 0], crossed_recv.at[c], mate, z,
            ).wait_recv()

        stays = (along(1 - back, a) == 1) & (along(1 - back, z) == h) & (flow == back)

        @pl.loop(0, jnp.where(stays, 0, per_slab))
        def _(c):
            remote(
                summed.at[0, rows_of(c)], straight.at[rows_of(c)],
                straight_send.at[0, c], straight_recv.at[c], mate, z,
            ).wait_recv()

        gram_ref[...] = (straight[...] + crossed[...].T) * scale

    first_level.wait_send()
    upper_levels.wait_send()
    half_copy.wait_send()
    for level in range(1, depth):
        @pl.loop(0, 2 ** (level - 1))
        def _(k):
            to_group(level, k).wait_send()

    @pl.when(is_side)
    def _():
        give_probe(place).wait_send()

    @pl.when(q == 0)
    def _():
        @pl.loop(0, parts)
        def _(c):
            give_turned(c).wait_send()

    swap.wait_send()

    @pl.when(a != z)
    def _():
        share.wait_send()

    @pl.when(is_hub)
    def _():
        for i, j in order:

            @pl.loop(0, parts)
            def _(c):
                part_copy(i, j, c).wait_send()

    for i in range(n_probe - 1):

        @pl.when(holds(i)[0])
        def _():
            @pl.loop(0, parts)
            def _(c):
                for k in range(fan):
                    send_crossed(i, c, k).wait_send()

                @pl.when(jnp.logical_not(kept(i, c)))
                def _():
                    send_straight(i, c).wait_send()


def hub_local(n_leaf, n_probe, leaf_blocks, block_mask, row_factor_stack, column_factor_stack, probes):
    depth, points, rank = row_factor_stack.shape
    width = probes.shape[1]
    slab = n_probe * width // n_leaf
    fan = n_leaf // n_probe
    parts = 2 * width // slab
    teams = n_leaf // 2
    count = n_probe * (n_probe - 1) // 2
    f32, bf16 = jnp.float32, jnp.bfloat16
    dma = pltpu.SemaphoreType.DMA
    hbm = pl.BlockSpec(memory_space=pltpu.HBM)
    groups = 2 ** (depth - 1) - 1
    return pl.pallas_call(
        functools.partial(hub_kernel, n_leaf, n_probe, parts),
        out_shape=(
            pltpu.VMEM((points, width), f32),
            pltpu.VMEM((slab, width), f32),
        ),
        in_specs=[hbm] * 5,
        out_specs=(pl.BlockSpec(memory_space=pltpu.VMEM), pl.BlockSpec(memory_space=pltpu.VMEM)),
        scratch_shapes=[
            pltpu.SMEM(block_mask.shape, block_mask.dtype),
            pltpu.VMEM((points, points), f32),
            pltpu.VMEM((depth, points, rank), f32),
            pltpu.VMEM((depth, points, rank), f32),
            pltpu.VMEM((points, width), f32),
            pltpu.VMEM((points, width), bf16),
            pltpu.VMEM((points, width), bf16),
            pltpu.VMEM((points, points), bf16),
            pltpu.VMEM((points, points), bf16),
            pltpu.VMEM((points, depth * rank), bf16),
            pltpu.VMEM((points, depth * rank), bf16),
            pltpu.VMEM((depth, rank, width), f32),
            pltpu.VMEM((depth - 1, rank // 2, width), f32),
            pltpu.VMEM((depth - 1, rank // 2, width), f32),
            pltpu.VMEM((groups, rank // 2, width), f32),
            pltpu.VMEM((depth, rank, width), f32),
            pltpu.VMEM((depth * rank, width), bf16),
            pltpu.VMEM((depth * rank, width), bf16),
            pltpu.VMEM((n_probe, points, width), bf16),
            pltpu.VMEM((n_probe, points, width), bf16),
            pltpu.VMEM((2, points, width), f32),
            pltpu.VMEM((2, points, width), f32),
            pltpu.VMEM((2, depth, rank, width), f32),
            pltpu.VMEM((width, points), f32),
            pltpu.VMEM((width, points), f32),
            pltpu.VMEM((count, width, width), f32),
            pltpu.VMEM((n_probe - 1, teams, width, width), f32),
            pltpu.VMEM((n_probe - 1, width, width), f32),
            pltpu.VMEM((slab, width), f32),
            pltpu.VMEM((width, slab), f32),
            pltpu.VMEM((width, width), f32),
            pltpu.VMEM((slab, width), f32),
            pltpu.VMEM((slab, width), f32),
            pltpu.VMEM((teams, slab, width), f32),
            dma((5,)),
            dma((2,)),
            dma((2,)),
            dma((groups,)),
            dma((groups,)),
            dma,
            dma,
            dma,
            dma((2,)),
            dma((depth,)),
            dma((2, depth)),
            dma((parts,)),
            dma((parts,)),
            dma((count, parts)),
            dma((n_probe - 1, teams, parts)),
            dma((n_probe - 1, parts)),
            dma((slab * parts // width,)),
            dma((n_probe - 1, parts, fan)),
            dma((parts,)),
            dma,
            dma,
            dma,
            dma((teams,)),
            pltpu.SemaphoreType.REGULAR,
            pltpu.SemaphoreType.REGULAR,
        ],
        compiler_params=pltpu.CompilerParams(
            collective_id=0, has_side_effects=True, vmem_limit_bytes=56 * 2**20
        ),
    )(block_mask, leaf_blocks, row_factor_stack, column_factor_stack, probes)


def local(n_leaf, n_probe, *arrays):
    width = arrays[-1].shape[1]
    whole_lanes = (n_probe * width) % (128 * n_leaf) == 0
    if n_probe == 4 and n_leaf == 2 * n_probe and whole_lanes:
        return hub_local(n_leaf, n_probe, *arrays)
    return ring(n_leaf, n_probe, *arrays)


def solution(mesh):
    return jax.shard_map(
        functools.partial(local, mesh.shape["leaf"], mesh.shape["probe"]),
        mesh=mesh,
        in_specs=(
            P("leaf", None),
            P("leaf", None, None),
            P(None, "leaf", None),
            P(None, "leaf", None),
            P("leaf", "probe"),
        ),
        out_specs=(P("leaf", "probe"), P("leaf", "probe")),
        check_vma=False,
    )
```

```python
import functools

import jax
import jax.numpy as jnp
from jax import lax
from jax.experimental import pallas as pl
from jax.experimental.pallas import tpu as pltpu
from jax.sharding import PartitionSpec as P

MESH = pl.DeviceIdType.MESH
CONTRACT_ROWS = (((0,), (0,)), ((), ()))
PLAIN = (((1,), (0,)), ((), ()))


def split(value):
    high = value.astype(jnp.bfloat16)
    return high, (value - high.astype(jnp.float32)).astype(jnp.bfloat16)


def dot3(left, right, dims):
    (lh, ll), (rh, rl) = left, right
    dot = functools.partial(lax.dot_general, dimension_numbers=dims, preferred_element_type=jnp.float32)
    return dot(lh, rh) + (dot(lh, rl) + dot(ll, rh))


def ring_kernel(
    n_leaf, n_probe, pieces,
    mask, block_hbm, row_hbm, col_hbm, probe_hbm, app_hbm, gram_ref,
    block, row, col, probe, probe_h, probe_l, own, swap, sib_h, sib_l,
    app, app_h, app_l, got, part, shares, total, extra, turned, kept_h, kept_l,
    load_sem, out_sem, swap_send, swap_recv, right_send, right_recv, left_send, left_recv,
    share_send, share_recv, extra_send, extra_recv,
):
    depth, rank = row.shape[0], row.shape[2]
    points, width = app.shape
    side = mask.shape[1]
    span = points // side
    half = points // 2
    piece = half // pieces
    leaf, z = lax.axis_index("leaf"), lax.axis_index("probe")
    slab = n_probe * width // n_leaf
    fan = n_leaf // n_probe
    a, b = leaf // fan, leaf % fan
    last = n_probe - 1
    ends = n_probe > 2

    loads = [
        pltpu.make_async_copy(source, target, load_sem.at[i])
        for i, (source, target) in enumerate(
            ((probe_hbm, probe), (col_hbm, col), (block_hbm, block), (row_hbm, row))
        )
    ]
    loads[0].start()
    loads[1].start()

    barrier = pltpu.get_barrier_semaphore()

    @pl.loop(1, n_leaf)
    def _(k):
        pl.semaphore_signal(
            barrier, inc=1, device_id={"leaf": (leaf + k) % n_leaf, "probe": z}, device_id_type=MESH
        )

    @pl.when(z > 0)
    def _():
        pl.semaphore_signal(barrier, inc=1, device_id={"leaf": leaf, "probe": z - 1}, device_id_type=MESH)

    @pl.when(z < last)
    def _():
        pl.semaphore_signal(barrier, inc=1, device_id={"leaf": leaf, "probe": z + 1}, device_id_type=MESH)

    @pl.when(a != z)
    def _():
        @pl.loop(0, fan)
        def _(c):
            pl.semaphore_signal(
                barrier, inc=1, device_id={"leaf": z * fan + c, "probe": a}, device_id_type=MESH
            )

    loads[0].wait()
    ph, plo = split(probe[...])
    probe_h[...] = ph
    probe_l[...] = plo
    loads[1].wait()
    loads[2].start()
    loads[3].start()
    columns = jnp.concatenate([col[level] for level in range(depth)], axis=1)
    own[...] = dot3(split(columns), (probe_h[...], probe_l[...]), CONTRACT_ROWS).reshape(own.shape)

    peers = n_leaf - 1 + jnp.where(z > 0, 1, 0) + jnp.where(z < last, 1, 0) + jnp.where(a != z, fan, 0)
    pl.semaphore_wait(barrier, peers)

    def exchange(step):
        away = 2**step
        other = leaf + (1 - 2 * ((leaf // away) % 2)) * away
        start = sum(depth - s for s in range(step))
        return start, pltpu.make_async_remote_copy(
            src_ref=own.at[pl.ds(step, depth - step)],
            dst_ref=swap.at[pl.ds(start, depth - step)],
            send_sem=swap_send.at[step],
            recv_sem=swap_recv.at[step],
            device_id={"leaf": other, "probe": z},
            device_id_type=MESH,
        )

    def near(which):
        @pl.loop(0, side // 2)
        def _(i):
            line = which * (side // 2) + i
            rows = pl.ds(pl.multiple_of(line * span, span), span)
            strips = [
                block[rows, j * span : (j + 1) * span] * mask[0, line, j].astype(jnp.float32)
                for j in range(side)
            ]
            into = pl.ds(pl.multiple_of(i * span, span), span)
            kept_h[into, :], kept_l[into, :] = split(jnp.concatenate(strips, axis=1))

        app[which * half : (which + 1) * half, :] = dot3(
            (kept_h[...], kept_l[...]), (probe_h[...], probe_l[...]), PLAIN
        )

    for step in range(depth):
        start, copy = exchange(step)
        copy.start()
        if step == 0:
            loads[2].wait()
        for which in range(2):
            if step == min(which, depth - 1):
                near(which)
        copy.wait()
        sib_h[step * rank : (step + 1) * rank, :], sib_l[step * rank : (step + 1) * rank, :] = split(
            swap[start]
        )
        for level in range(step + 1, depth):
            own[level] = own[level] + swap[start + level - step]

    def ship(source, to, slot, begin, send, recv):
        rows = pl.ds(pl.multiple_of(begin, piece), piece)
        return pltpu.make_async_remote_copy(
            src_ref=source.at[rows] if source is app else source.at[slot, rows],
            dst_ref=got.at[slot, rows],
            send_sem=send.at[slot, begin // piece],
            recv_sem=recv.at[slot, begin // piece],
            device_id={"leaf": leaf, "probe": to},
            device_id_type=MESH,
        )

    def rightward(source, slot, begin):
        return ship(source, jnp.minimum(z + 1, last), slot, begin, right_send, right_recv)

    def leftward(source, slot, begin):
        return ship(source, jnp.maximum(z - 1, 0), slot, begin, left_send, left_recv)

    loads[3].wait()
    sends_right = (z < last - 1) if ends else (z < last)
    sends_left = (z > 1) if ends else (z > 0)

    def far(which):
        rows = slice(which * half, (which + 1) * half)
        factors = jnp.concatenate([row[level, rows, :] for level in range(depth)], axis=1)
        value = app[rows, :] + dot3(split(factors), (sib_h[...], sib_l[...]), PLAIN)
        app[rows, :] = value
        app_h[rows, :], app_l[rows, :] = split(value)

    far(0)

    @pl.when(sends_right)
    def _():
        @pl.loop(0, pieces)
        def _(c):
            rightward(app, z, c * piece).start()

    far(1)

    @pl.when(sends_left)
    def _():
        @pl.loop(0, pieces)
        def _(c):
            leftward(app, z, half + c * piece).start()

    if ends:
        @pl.loop(0, pieces)
        def _(c):
            @pl.when(z == 0)
            def _():
                rightward(app, z, half + c * piece).start()

            @pl.when(z == last)
            def _():
                leftward(app, z, c * piece).start()

    keep = pltpu.make_async_copy(app, app_hbm, out_sem)
    keep.start()

    def gram(slot, source, begin, fresh):
        into = pl.ds(pl.multiple_of(slot * width, width), width)
        rows = pl.ds(pl.multiple_of(begin, half), half)
        here = (app_h[rows, :], app_l[rows, :])
        there = here if source is None else split(source[slot, rows, :])
        value = dot3(there, here, CONTRACT_ROWS)
        part[into, :] = value if fresh else part[into, :] + value

    def share(k):
        to = (leaf + k) % n_leaf
        return pltpu.make_async_remote_copy(
            src_ref=part.at[pl.ds(pl.multiple_of(to * slab, slab), slab)],
            dst_ref=shares.at[k],
            send_sem=share_send.at[k],
            recv_sem=share_recv.at[k],
            device_id={"leaf": to, "probe": z},
            device_id_type=MESH,
        )

    def give(slot):
        @pl.loop(0, fan)
        def _(c):
            to = slot * fan + c

            @pl.when(to != leaf)
            def _():
                share((to - leaf + n_leaf) % n_leaf).start()

    part[...] = jnp.zeros_like(part)

    @pl.loop(0, 2)
    def _(h):
        gram(z, None, h * half, False)

    give(z)

    @pl.loop(1, n_probe)
    def _(d):
        from_left = (z - d >= 0) & ((z < last) | (d > 1) | (not ends))
        from_right = (z + d <= last) & ((z > 0) | (d > 1) | (not ends))
        low_slot, high_slot = jnp.maximum(z - d, 0), jnp.minimum(z + d, last)

        @pl.loop(0, pieces)
        def _(c):
            up, low = c * piece, half + c * piece

            @pl.when(from_left)
            def _():
                rightward(got, low_slot, up).wait_recv()

                @pl.when(z < last)
                def _():
                    rightward(got, low_slot, up).start()

            @pl.when(from_right)
            def _():
                leftward(got, high_slot, low).wait_recv()

                @pl.when(z > 0)
                def _():
                    leftward(got, high_slot, low).start()

        @pl.loop(0, 2)
        def _(h):
            @pl.when(jnp.where(h == 0, from_left, from_right))
            def _():
                slot = jnp.where(h == 0, low_slot, high_slot)
                gram(slot, got, h * half, False)
                whole = (d > 1) | jnp.where(h == 0, z != 1, z != last - 1) | (not ends)

                @pl.when(whole)
                def _():
                    give(slot)

    if ends:
        at_low, at_high = z == 1, z == last - 1

        @pl.loop(0, pieces)
        def _(c):
            @pl.when(at_low)
            def _():
                rightward(got, z - 1, half + c * piece).wait_recv()

            @pl.when(at_high)
            def _():
                leftward(got, z + 1, c * piece).wait_recv()

        @pl.loop(0, 2)
        def _(h):
            @pl.when(jnp.where(h == 0, at_high, at_low))
            def _():
                slot = jnp.where(h == 0, jnp.minimum(z + 1, last), jnp.maximum(z - 1, 0))
                gram(slot, got, h * half, False)
                give(slot)

    total[...] = part[pl.ds(pl.multiple_of(leaf * slab, slab), slab), :]

    def holds(slot):
        return (not ends) | (((z > 0) | (slot != 1)) & ((z < last) | (slot != last - 1)))

    @pl.when(holds(a))
    def _():
        @pl.loop(1, n_leaf)
        def _(k):
            share(k).wait_recv()
            total[...] = total[...] + shares[k]

    scale = 1.0 / (points * n_leaf)

    tile = extra.shape[1]

    def trade(c, at):
        return pltpu.make_async_remote_copy(
            src_ref=total if tile == width else total.at[:, pl.ds(pl.multiple_of(c * tile, tile), tile)],
            dst_ref=extra.at[pl.ds(pl.multiple_of(at * slab, slab), slab)],
            send_sem=extra_send.at[c],
            recv_sem=extra_recv.at[at],
            device_id={"leaf": z * fan + c, "probe": a},
            device_id_type=MESH,
        )

    @pl.when(a != z)
    def _():
        @pl.loop(0, fan)
        def _(c):
            trade(c, b).start()

        @pl.loop(0, fan)
        def _(c):
            trade(c, c).wait_recv()

        turned[...] = extra[...].T
        skip = 0 if tile == slab else pl.multiple_of(b * slab, slab)
        gram_ref[...] = (total[...] + turned[pl.ds(skip, slab), :]) * scale

        @pl.loop(0, fan)
        def _(c):
            trade(c, b).wait_send()

    @pl.when(a == z)
    def _():
        gram_ref[...] = total[...] * scale

    @pl.loop(0, pieces)
    def _(c):
        up, low = c * piece, half + c * piece

        @pl.when(sends_right)
        def _():
            rightward(app, z, up).wait_send()

        @pl.when(sends_left)
        def _():
            leftward(app, z, low).wait_send()

        if ends:

            @pl.when(z == 0)
            def _():
                rightward(app, z, low).wait_send()

            @pl.when(z == last)
            def _():
                leftward(app, z, up).wait_send()

        @pl.loop(1, n_probe)
        def _(d):
            @pl.when((z - d >= 0) & (z < last))
            def _():
                rightward(got, jnp.maximum(z - d, 0), up).wait_send()

            @pl.when((z + d <= last) & (z > 0))
            def _():
                leftward(got, jnp.minimum(z + d, last), low).wait_send()

    @pl.loop(1, n_leaf)
    def _(k):
        @pl.when(holds(((leaf + k) % n_leaf) // fan))
        def _():
            share(k).wait_send()

    keep.wait()


def ring(n_leaf, n_probe, leaf_blocks, block_mask, row_factor_stack, column_factor_stack, probes):
    depth, points, rank = row_factor_stack.shape
    width = probes.shape[1]
    slab = n_probe * width // n_leaf
    fan = n_leaf // n_probe
    pieces = 4
    tile = slab if slab % 128 == 0 else width
    f32, bf16 = jnp.float32, jnp.bfloat16
    dma = pltpu.SemaphoreType.DMA
    hbm = pl.BlockSpec(memory_space=pltpu.HBM)
    return pl.pallas_call(
        functools.partial(ring_kernel, n_leaf, n_probe, pieces),
        out_shape=(
            jax.ShapeDtypeStruct((points, width), f32),
            jax.ShapeDtypeStruct((slab, width), f32),
        ),
        in_specs=[pl.BlockSpec(memory_space=pltpu.SMEM), hbm, hbm, hbm, hbm],
        out_specs=(hbm, pl.BlockSpec(memory_space=pltpu.VMEM)),
        scratch_shapes=[
            pltpu.VMEM((points, points), f32),
            pltpu.VMEM((depth, points, rank), f32),
            pltpu.VMEM((depth, points, rank), f32),
            pltpu.VMEM((points, width), f32),
            pltpu.VMEM((points, width), bf16),
            pltpu.VMEM((points, width), bf16),
            pltpu.VMEM((depth, rank, width), f32),
            pltpu.VMEM((depth * (depth + 1) // 2, rank, width), f32),
            pltpu.VMEM((depth * rank, width), bf16),
            pltpu.VMEM((depth * rank, width), bf16),
            pltpu.VMEM((points, width), f32),
            pltpu.VMEM((points, width), bf16),
            pltpu.VMEM((points, width), bf16),
            pltpu.VMEM((n_probe, points, width), f32),
            pltpu.VMEM((n_probe * width, width), f32),
            pltpu.VMEM((n_leaf, slab, width), f32),
            pltpu.VMEM((slab, width), f32),
            pltpu.VMEM((width, tile), f32),
            pltpu.VMEM((tile, width), f32),
            pltpu.VMEM((points // 2, points), bf16),
            pltpu.VMEM((points // 2, points), bf16),
            dma((4,)),
            dma,
            dma((depth,)),
            dma((depth,)),
            dma((n_probe, 2 * pieces)),
            dma((n_probe, 2 * pieces)),
            dma((n_probe, 2 * pieces)),
            dma((n_probe, 2 * pieces)),
            dma((n_leaf,)),
            dma((n_leaf,)),
            dma((fan,)),
            dma((fan,)),
        ],
        compiler_params=pltpu.CompilerParams(
            collective_id=0, has_side_effects=True, vmem_limit_bytes=67043328
        ),
    )(block_mask, leaf_blocks, row_factor_stack, column_factor_stack, probes)


def hub_kernel(
    n_leaf, n_probe, parts,
    mask_hbm, block_hbm, row_hbm, col_hbm, probe_hbm, app, gram_ref,
    mask, block, row, col, probe, probe_h, probe_l, block_h, block_l, row_h, row_l,
    own, pair_in, pair_sum, group_in, sib, sib_h, sib_l, app_h, app_l, near_other,
    got_probe, got_sib, got_turned, turned, pairs, arrived, summed, straight, crossed, diag, diag_in, diag_sum, shares,
    load_sem, pair_send, pair_recv, group_send, group_recv, half_send, half_recv,
    probe_send, probe_recv, sib_send, sib_recv, turned_send, turned_recv,
    part_send, part_recv, straight_send, straight_recv, crossed_send, crossed_recv, swap_send, swap_recv, share_send, share_recv, ready, go,
):
    depth, rank = row.shape[0], row.shape[2]
    points, width = app.shape
    side = mask.shape[1]
    span = points // side
    half = points // 2
    leaf, z = lax.axis_index("leaf"), lax.axis_index("probe")
    slab = n_probe * width // n_leaf
    fan = n_leaf // n_probe
    chunk = width // parts
    last = n_probe - 1
    h = n_probe // 2
    teams = n_leaf // 2
    split_rank = rank // 2
    flow = leaf % 2
    team = leaf // 2
    mate = leaf + 1 - 2 * flow
    a, b = leaf // fan, leaf % fan

    def along(direction, position):
        return jnp.where(direction == 0, position, last - position)

    q = along(flow, z)
    is_hub = q == h
    hub = along(flow, h)

    def remote(src, dst, send, recv, to_leaf, to_z):
        return pltpu.make_async_remote_copy(
            src_ref=src, dst_ref=dst, send_sem=send, recv_sem=recv,
            device_id={"leaf": to_leaf, "probe": to_z}, device_id_type=MESH,
        )

    loads = [
        pltpu.make_async_copy(source, target, load_sem.at[i])
        for i, (source, target) in enumerate(
            ((probe_hbm, probe), (col_hbm, col), (block_hbm, block), (row_hbm, row), (mask_hbm, mask))
        )
    ]
    loads[0].start()
    loads[1].start()

    barrier = pltpu.get_barrier_semaphore()

    @pl.loop(1, n_leaf)
    def _(k):
        pl.semaphore_signal(
            barrier, inc=1, device_id={"leaf": (leaf + k) % n_leaf, "probe": z}, device_id_type=MESH
        )

    @pl.loop(0, n_probe)
    def _(k):
        @pl.when((k != z) & (jnp.abs(k - z) < last))
        def _():
            pl.semaphore_signal(barrier, inc=1, device_id={"leaf": leaf, "probe": k}, device_id_type=MESH)

    pl.semaphore_wait(barrier, n_leaf - 1 + last - jnp.where((z == 0) | (z == last), 1, 0))

    sides = [k for k in range(n_probe) if abs(k - h) == 1]
    distant = [k for k in range(n_probe) if abs(k - h) > 1]
    is_side = jnp.abs(q - h) == 1
    place = jnp.where(q > h, 1, 0)

    def give_probe(slot):
        return remote(probe_hbm, got_probe.at[slot], probe_send, probe_recv.at[slot], leaf, hub)

    @pl.when(is_side)
    def _():
        give_probe(place).start()

    loads[0].wait()
    ph, plo = split(probe[...])
    probe_h[...] = ph
    probe_l[...] = plo
    loads[1].wait()
    loads[4].start()
    loads[2].start()
    loads[3].start()
    columns = jnp.concatenate([col[level] for level in range(depth)], axis=1)
    own[...] = dot3(split(columns), (probe_h[...], probe_l[...]), CONTRACT_ROWS).reshape(own.shape)

    @pl.loop(1, n_leaf)
    def _(k):
        pl.semaphore_signal(
            ready, inc=1, device_id={"leaf": (leaf + k) % n_leaf, "probe": z}, device_id_type=MESH
        )

    first_level = remote(own.at[0], sib.at[0], pair_send.at[0], pair_recv.at[0], mate, z)
    upper_levels = remote(
        own.at[pl.ds(1, depth - 1), pl.ds(pl.multiple_of((1 - flow) * split_rank, split_rank), split_rank)],
        pair_in, pair_send.at[1], pair_recv.at[1], mate, z,
    )
    upper_levels.start()
    first_level.start()
    mine = pl.ds(pl.multiple_of(flow * split_rank, split_rank), split_rank)

    def to_group(level, k):
        members = 2 ** (level - 1)
        base = leaf - leaf % 2**level + (1 - 2 * ((leaf // 2**level) % 2)) * 2**level
        from_slot = members - 1 + (leaf % 2**level) // 2
        return remote(
            pair_sum.at[level - 1], group_in.at[from_slot],
            group_send.at[members - 1 + k], group_recv.at[from_slot], base + 2 * k + flow, z,
        )

    def from_group(level, k):
        members = 2 ** (level - 1)
        return remote(
            pair_sum.at[level - 1], group_in.at[members - 1 + k],
            group_send.at[members - 1 + k], group_recv.at[members - 1 + k], mate, z,
        )

    upper_levels.wait_recv()
    for level in range(1, depth):
        pair_sum[level - 1] = own[level, mine, :] + pair_in[level - 1]
    for level in reversed(range(1, depth)):
        @pl.loop(0, 2 ** (level - 1))
        def _(k):
            to_group(level, k).start()

    loads[4].wait()
    loads[2].wait()

    @pl.loop(0, side)
    def _(line):
        rows = pl.ds(pl.multiple_of(line * span, span), span)
        strips = [
            block[rows, j * span : (j + 1) * span] * mask[0, line, j].astype(jnp.float32)
            for j in range(side)
        ]
        block_h[rows, :], block_l[rows, :] = split(jnp.concatenate(strips, axis=1))

    def near(target):
        @pl.loop(0, 2)
        def _(i):
            rows = pl.ds(pl.multiple_of(i * half, half), half)
            target[rows, :] = dot3(
                (block_h[rows, :], block_l[rows, :]), (probe_h[...], probe_l[...]), PLAIN
            )

    near(app)
    loads[3].wait()
    for level in range(depth):
        row_h[:, level * rank : (level + 1) * rank], row_l[:, level * rank : (level + 1) * rank] = split(row[level])

    for level in range(1, depth):
        @pl.loop(0, 2 ** (level - 1))
        def _(k):
            from_group(level, k).wait_recv()

        begin = 2 ** (level - 1) - 1
        value = group_in[begin]
        for k in range(1, 2 ** (level - 1)):
            value = value + group_in[begin + k]
        sib[level, mine, :] = value

    half_copy = remote(
        sib.at[pl.ds(1, depth - 1), mine], sib.at[pl.ds(1, depth - 1), mine], half_send, half_recv, mate, z
    )
    half_copy.start()
    first_level.wait_recv()
    half_copy.wait_recv()

    def give_sib(slot, level):
        return remote(
            sib.at[level], got_sib.at[slot, level], sib_send.at[level], sib_recv.at[slot, level], leaf, hub
        )

    @pl.when(is_side)
    def _():
        for level in range(depth):
            give_sib(place, level).start()

    def far(source, base, target, slot):
        flat = source[...].reshape(depth * rank, width)
        sib_h[...], sib_l[...] = split(flat)

        @pl.loop(0, 2)
        def _(i):
            rows = pl.ds(pl.multiple_of(i * half, half), half)
            value = base[rows, :] + dot3((row_h[rows, :], row_l[rows, :]), (sib_h[...], sib_l[...]), PLAIN)
            if target is not None:
                target[rows, :] = value
            app_h[slot, rows, :], app_l[slot, rows, :] = split(value)

    far(sib, app, app, h)

    def rows_of(c):
        return pl.ds(pl.multiple_of(c * chunk, chunk), chunk)

    def give_turned(c):
        return remote(
            turned.at[rows_of(c)], got_turned.at[rows_of(c)], turned_send.at[c], turned_recv.at[c], leaf, hub
        )

    @pl.when(q == 0)
    def _():
        per = 128 // chunk
        for strip in range(width // 128):
            lanes = slice(strip * 128, (strip + 1) * 128)
            turned[lanes, :] = app[:, lanes].T

    diag[...] = dot3((app_h[h], app_l[h]), (app_h[h], app_l[h]), CONTRACT_ROWS)

    def slab_of(k):
        return pl.ds(pl.multiple_of(k * slab, slab), slab)

    swap = remote(diag.at[slab_of(1 - flow)], diag_in, swap_send, swap_recv, mate, z)
    swap.start()
    share = remote(diag_sum, shares.at[team], share_send, share_recv.at[team], z * fan + flow, z)

    def give_share():
        swap.wait_recv()
        diag_sum[...] = diag[slab_of(flow), :] + diag_in[...]

        @pl.when(a != z)
        def _():
            share.start()

    order = [(i, j) for j in range(n_probe) for i in range(j)]
    seat = {(i, j): i if j == i + 1 else j for i, j in order}

    def part_copy(i, j, c):
        pid = order.index((i, j))
        return remote(
            pairs.at[pid, rows_of(c)], arrived.at[i, team, rows_of(c)],
            part_send.at[pid, c], part_recv.at[i, team, c], along(flow, seat[i, j]) * fan + 1 - flow, z,
        )

    give_share()

    @pl.when(is_side)
    def _():
        for level in range(depth - 1):
            give_sib(place, level).wait_send()

        @pl.when(q < h)
        def _():
            pl.semaphore_signal(go, inc=1, device_id={"leaf": leaf, "probe": along(flow, 0)}, device_id_type=MESH)

        @pl.when(q > h)
        def _():
            pl.semaphore_signal(go, inc=1, device_id={"leaf": mate, "probe": z}, device_id_type=MESH)

        for level in range(depth - 1, depth):
            give_sib(place, level).wait_send()

    @pl.when(q == 0)
    def _():
        pl.semaphore_wait(go, 2)

        @pl.loop(0, parts)
        def _(c):
            give_turned(c).start()

    @pl.when(is_hub)
    def _():
        for slot, k in enumerate(sides):
            give_probe(slot).wait_recv()
            ph, plo = split(got_probe[slot])
            probe_h[...] = ph
            probe_l[...] = plo
            near(near_other.at[slot])

        def pair(i, j):
            pairs[order.index((i, j))] = dot3((app_h[i], app_l[i]), (app_h[j], app_l[j]), CONTRACT_ROWS)

            @pl.loop(0, parts)
            def _(c):
                part_copy(i, j, c).start()

        for slot, k in enumerate(sides):
            for level in range(depth):
                give_sib(slot, level).wait_recv()
            far(got_sib.at[slot], near_other.at[slot], None, k)
            pair(min(k, h), max(k, h))
        pair(*sides)

    def late(c):
        @pl.when(is_hub)
        def _():
            give_turned(c).wait_recv()
            high, low = split(got_turned[rows_of(c), :])
            stacked = jnp.concatenate([high, low], axis=0)
            dot = functools.partial(lax.dot_general, dimension_numbers=PLAIN, preferred_element_type=jnp.float32)
            for j in range(1, n_probe):
                both = dot(stacked, app_h[j])
                pairs[order.index((0, j)), rows_of(c), :] = both[:chunk] + (dot(high, app_l[j]) + both[chunk:])
                part_copy(0, j, c).start()

    current = 1 - flow
    collects = z == along(current, h)
    position = along(current, a)

    def arrival(i, m, c):
        return remote(
            arrived.at[i, m, rows_of(c)], arrived.at[i, m, rows_of(c)],
            part_send.at[0, c], part_recv.at[i, m, c], mate, z,
        )

    per_slab = slab // chunk

    def holds(i):
        match = [j for j in range(n_probe) if (i, j) in seat]
        found = jnp.bool_(False)
        partner = position
        for j in match:
            found = found | (position == seat[i, j])
            if seat[i, j] != j:
                partner = jnp.where(position == seat[i, j], j, partner)
        return collects & found, along(current, partner)

    def kept(i, c):
        return (seat.get((i, h)) == i) & (position == i) & (c // per_slab == flow)

    def send_crossed(i, c, k):
        return remote(
            summed.at[i, rows_of(c), k * slab : (k + 1) * slab], crossed.at[rows_of(c)],
            crossed_send.at[i, c, k], crossed_recv.at[c], holds(i)[1] * fan + k, along(current, i),
        )

    def send_straight(i, c):
        return remote(
            summed.at[i, rows_of(c)], straight.at[rows_of(c % per_slab)],
            straight_send.at[i, c], straight_recv.at[c % per_slab],
            along(current, i) * fan + c // per_slab, holds(i)[1],
        )

    def collect(i, c):
        @pl.when(holds(i)[0])
        def _():
            for m in range(teams):
                arrival(i, m, c).wait_recv()
            value = arrived[i, 0, rows_of(c), :]
            for m in range(1, teams):
                value = value + arrived[i, m, rows_of(c), :]
            summed[i, rows_of(c), :] = value
            for k in range(fan):
                send_crossed(i, c, k).start()

            @pl.when(kept(i, c))
            def _():
                straight[rows_of(c % per_slab), :] = value

            @pl.when(jnp.logical_not(kept(i, c)))
            def _():
                send_straight(i, c).start()

    def collect_all(i, begin, end):
        @pl.loop(begin, end)
        def _(c):
            collect(i, c)

    @pl.loop(0, parts)
    def _(c):
        late(c)

    pl.semaphore_wait(ready, n_leaf - 1)
    for i in range(1, n_probe - 1):
        collect_all(i, 0, parts)
    collect_all(0, 0, parts)

    scale = 1.0 / (points * n_leaf)

    @pl.when(a == z)
    def _():
        shares[team] = diag_sum[...]

        @pl.loop(1, teams)
        def _(k):
            other = (team + k) % teams
            remote(diag_sum, shares.at[other], share_send, share_recv.at[other], mate, z).wait_recv()

        value = shares[0]
        for k in range(1, teams):
            value = value + shares[k]
        gram_ref[...] = value * scale

    @pl.when(a != z)
    def _():
        back = jnp.where(z < a, 0, 1)

        @pl.loop(0, parts)
        def _(c):
            remote(
                summed.at[0, rows_of(c), 0:slab], crossed.at[rows_of(c)],
                crossed_send.at[0, c, 0], crossed_recv.at[c], mate, z,
            ).wait_recv()

        stays = (along(1 - back, a) == 1) & (along(1 - back, z) == h) & (flow == back)

        @pl.loop(0, jnp.where(stays, 0, per_slab))
        def _(c):
            remote(
                summed.at[0, rows_of(c)], straight.at[rows_of(c)],
                straight_send.at[0, c], straight_recv.at[c], mate, z,
            ).wait_recv()

        gram_ref[...] = (straight[...] + crossed[...].T) * scale

    first_level.wait_send()
    upper_levels.wait_send()
    half_copy.wait_send()
    for level in range(1, depth):
        @pl.loop(0, 2 ** (level - 1))
        def _(k):
            to_group(level, k).wait_send()

    @pl.when(is_side)
    def _():
        give_probe(place).wait_send()

    @pl.when(q == 0)
    def _():
        @pl.loop(0, parts)
        def _(c):
            give_turned(c).wait_send()

    swap.wait_send()

    @pl.when(a != z)
    def _():
        share.wait_send()

    @pl.when(is_hub)
    def _():
        for i, j in order:

            @pl.loop(0, parts)
            def _(c):
                part_copy(i, j, c).wait_send()

    for i in range(n_probe - 1):

        @pl.when(holds(i)[0])
        def _():
            @pl.loop(0, parts)
            def _(c):
                for k in range(fan):
                    send_crossed(i, c, k).wait_send()

                @pl.when(jnp.logical_not(kept(i, c)))
                def _():
                    send_straight(i, c).wait_send()


def hub_local(n_leaf, n_probe, leaf_blocks, block_mask, row_factor_stack, column_factor_stack, probes):
    depth, points, rank = row_factor_stack.shape
    width = probes.shape[1]
    slab = n_probe * width // n_leaf
    fan = n_leaf // n_probe
    parts = 2 * width // slab
    teams = n_leaf // 2
    count = n_probe * (n_probe - 1) // 2
    f32, bf16 = jnp.float32, jnp.bfloat16
    dma = pltpu.SemaphoreType.DMA
    hbm = pl.BlockSpec(memory_space=pltpu.HBM)
    groups = 2 ** (depth - 1) - 1
    return pl.pallas_call(
        functools.partial(hub_kernel, n_leaf, n_probe, parts),
        out_shape=(
            pltpu.VMEM((points, width), f32),
            pltpu.VMEM((slab, width), f32),
        ),
        in_specs=[hbm] * 5,
        out_specs=(pl.BlockSpec(memory_space=pltpu.VMEM), pl.BlockSpec(memory_space=pltpu.VMEM)),
        scratch_shapes=[
            pltpu.SMEM(block_mask.shape, block_mask.dtype),
            pltpu.VMEM((points, points), f32),
            pltpu.VMEM((depth, points, rank), f32),
            pltpu.VMEM((depth, points, rank), f32),
            pltpu.VMEM((points, width), f32),
            pltpu.VMEM((points, width), bf16),
            pltpu.VMEM((points, width), bf16),
            pltpu.VMEM((points, points), bf16),
            pltpu.VMEM((points, points), bf16),
            pltpu.VMEM((points, depth * rank), bf16),
            pltpu.VMEM((points, depth * rank), bf16),
            pltpu.VMEM((depth, rank, width), f32),
            pltpu.VMEM((depth - 1, rank // 2, width), f32),
            pltpu.VMEM((depth - 1, rank // 2, width), f32),
            pltpu.VMEM((groups, rank // 2, width), f32),
            pltpu.VMEM((depth, rank, width), f32),
            pltpu.VMEM((depth * rank, width), bf16),
            pltpu.VMEM((depth * rank, width), bf16),
            pltpu.VMEM((n_probe, points, width), bf16),
            pltpu.VMEM((n_probe, points, width), bf16),
            pltpu.VMEM((2, points, width), f32),
            pltpu.VMEM((2, points, width), f32),
            pltpu.VMEM((2, depth, rank, width), f32),
            pltpu.VMEM((width, points), f32),
            pltpu.VMEM((width, points), f32),
            pltpu.VMEM((count, width, width), f32),
            pltpu.VMEM((n_probe - 1, teams, width, width), f32),
            pltpu.VMEM((n_probe - 1, width, width), f32),
            pltpu.VMEM((slab, width), f32),
            pltpu.VMEM((width, slab), f32),
            pltpu.VMEM((width, width), f32),
            pltpu.VMEM((slab, width), f32),
            pltpu.VMEM((slab, width), f32),
            pltpu.VMEM((teams, slab, width), f32),
            dma((5,)),
            dma((2,)),
            dma((2,)),
            dma((groups,)),
            dma((groups,)),
            dma,
            dma,
            dma,
            dma((2,)),
            dma((depth,)),
            dma((2, depth)),
            dma((parts,)),
            dma((parts,)),
            dma((count, parts)),
            dma((n_probe - 1, teams, parts)),
            dma((n_probe - 1, parts)),
            dma((slab * parts // width,)),
            dma((n_probe - 1, parts, fan)),
            dma((parts,)),
            dma,
            dma,
            dma,
            dma((teams,)),
            pltpu.SemaphoreType.REGULAR,
            pltpu.SemaphoreType.REGULAR,
        ],
        compiler_params=pltpu.CompilerParams(
            collective_id=0, has_side_effects=True, vmem_limit_bytes=56 * 2**20
        ),
    )(block_mask, leaf_blocks, row_factor_stack, column_factor_stack, probes)


def local(n_leaf, n_probe, *arrays):
    width = arrays[-1].shape[1]
    whole_lanes = (n_probe * width) % (128 * n_leaf) == 0
    if n_probe == 4 and n_leaf == 2 * n_probe and whole_lanes:
        return hub_local(n_leaf, n_probe, *arrays)
    return ring(n_leaf, n_probe, *arrays)


def solution(mesh):
    return jax.shard_map(
        functools.partial(local, mesh.shape["leaf"], mesh.shape["probe"]),
        mesh=mesh,
        in_specs=(
            P("leaf", None),
            P("leaf", None, None),
            P(None, "leaf", None),
            P(None, "leaf", None),
            P("leaf", "probe"),
        ),
        out_specs=(P("leaf", "probe"), P("leaf", "probe")),
        check_vma=False,
    )
```

```python
import functools

import jax
import jax.numpy as jnp
from jax import lax
from jax.experimental import pallas as pl
from jax.experimental.pallas import tpu as pltpu
from jax.sharding import PartitionSpec as P

MESH = pl.DeviceIdType.MESH
CONTRACT_ROWS = (((0,), (0,)), ((), ()))
PLAIN = (((1,), (0,)), ((), ()))


def split(value):
    high = value.astype(jnp.bfloat16)
    return high, (value - high.astype(jnp.float32)).astype(jnp.bfloat16)


def dot3(left, right, dims):
    (lh, ll), (rh, rl) = left, right
    dot = functools.partial(lax.dot_general, dimension_numbers=dims, preferred_element_type=jnp.float32)
    return dot(lh, rh) + (dot(lh, rl) + dot(ll, rh))


def ring_kernel(
    n_leaf, n_probe, pieces,
    mask, block_hbm, row_hbm, col_hbm, probe_hbm, app_hbm, gram_ref,
    block, row, col, probe, probe_h, probe_l, own, swap, sib_h, sib_l,
    app, app_h, app_l, got, part, shares, total, extra, turned, kept_h, kept_l,
    load_sem, out_sem, swap_send, swap_recv, right_send, right_recv, left_send, left_recv,
    share_send, share_recv, extra_send, extra_recv,
):
    depth, rank = row.shape[0], row.shape[2]
    points, width = app.shape
    side = mask.shape[1]
    span = points // side
    half = points // 2
    piece = half // pieces
    leaf, z = lax.axis_index("leaf"), lax.axis_index("probe")
    slab = n_probe * width // n_leaf
    fan = n_leaf // n_probe
    a, b = leaf // fan, leaf % fan
    last = n_probe - 1
    ends = n_probe > 2

    loads = [
        pltpu.make_async_copy(source, target, load_sem.at[i])
        for i, (source, target) in enumerate(
            ((probe_hbm, probe), (col_hbm, col), (block_hbm, block), (row_hbm, row))
        )
    ]
    loads[0].start()
    loads[1].start()

    barrier = pltpu.get_barrier_semaphore()

    @pl.loop(1, n_leaf)
    def _(k):
        pl.semaphore_signal(
            barrier, inc=1, device_id={"leaf": (leaf + k) % n_leaf, "probe": z}, device_id_type=MESH
        )

    @pl.when(z > 0)
    def _():
        pl.semaphore_signal(barrier, inc=1, device_id={"leaf": leaf, "probe": z - 1}, device_id_type=MESH)

    @pl.when(z < last)
    def _():
        pl.semaphore_signal(barrier, inc=1, device_id={"leaf": leaf, "probe": z + 1}, device_id_type=MESH)

    @pl.when(a != z)
    def _():
        @pl.loop(0, fan)
        def _(c):
            pl.semaphore_signal(
                barrier, inc=1, device_id={"leaf": z * fan + c, "probe": a}, device_id_type=MESH
            )

    loads[0].wait()
    ph, plo = split(probe[...])
    probe_h[...] = ph
    probe_l[...] = plo
    loads[1].wait()
    loads[2].start()
    loads[3].start()
    columns = jnp.concatenate([col[level] for level in range(depth)], axis=1)
    own[...] = dot3(split(columns), (probe_h[...], probe_l[...]), CONTRACT_ROWS).reshape(own.shape)

    peers = n_leaf - 1 + jnp.where(z > 0, 1, 0) + jnp.where(z < last, 1, 0) + jnp.where(a != z, fan, 0)
    pl.semaphore_wait(barrier, peers)

    def exchange(step):
        away = 2**step
        other = leaf + (1 - 2 * ((leaf // away) % 2)) * away
        start = sum(depth - s for s in range(step))
        return start, pltpu.make_async_remote_copy(
            src_ref=own.at[pl.ds(step, depth - step)],
            dst_ref=swap.at[pl.ds(start, depth - step)],
            send_sem=swap_send.at[step],
            recv_sem=swap_recv.at[step],
            device_id={"leaf": other, "probe": z},
            device_id_type=MESH,
        )

    def near(which):
        @pl.loop(0, side // 2)
        def _(i):
            line = which * (side // 2) + i
            rows = pl.ds(pl.multiple_of(line * span, span), span)
            strips = [
                block[rows, j * span : (j + 1) * span] * mask[0, line, j].astype(jnp.float32)
                for j in range(side)
            ]
            into = pl.ds(pl.multiple_of(i * span, span), span)
            kept_h[into, :], kept_l[into, :] = split(jnp.concatenate(strips, axis=1))

        app[which * half : (which + 1) * half, :] = dot3(
            (kept_h[...], kept_l[...]), (probe_h[...], probe_l[...]), PLAIN
        )

    for step in range(depth):
        start, copy = exchange(step)
        copy.start()
        if step == 0:
            loads[2].wait()
        for which in range(2):
            if step == min(which, depth - 1):
                near(which)
        copy.wait()
        sib_h[step * rank : (step + 1) * rank, :], sib_l[step * rank : (step + 1) * rank, :] = split(
            swap[start]
        )
        for level in range(step + 1, depth):
            own[level] = own[level] + swap[start + level - step]

    def ship(source, to, slot, begin, send, recv):
        rows = pl.ds(pl.multiple_of(begin, piece), piece)
        return pltpu.make_async_remote_copy(
            src_ref=source.at[rows] if source is app else source.at[slot, rows],
            dst_ref=got.at[slot, rows],
            send_sem=send.at[slot, begin // piece],
            recv_sem=recv.at[slot, begin // piece],
            device_id={"leaf": leaf, "probe": to},
            device_id_type=MESH,
        )

    def rightward(source, slot, begin):
        return ship(source, jnp.minimum(z + 1, last), slot, begin, right_send, right_recv)

    def leftward(source, slot, begin):
        return ship(source, jnp.maximum(z - 1, 0), slot, begin, left_send, left_recv)

    loads[3].wait()
    sends_right = (z < last - 1) if ends else (z < last)
    sends_left = (z > 1) if ends else (z > 0)

    def far(which):
        rows = slice(which * half, (which + 1) * half)
        factors = jnp.concatenate([row[level, rows, :] for level in range(depth)], axis=1)
        value = app[rows, :] + dot3(split(factors), (sib_h[...], sib_l[...]), PLAIN)
        app[rows, :] = value
        app_h[rows, :], app_l[rows, :] = split(value)

    far(0)

    @pl.when(sends_right)
    def _():
        @pl.loop(0, pieces)
        def _(c):
            rightward(app, z, c * piece).start()

    far(1)

    @pl.when(sends_left)
    def _():
        @pl.loop(0, pieces)
        def _(c):
            leftward(app, z, half + c * piece).start()

    if ends:
        @pl.loop(0, pieces)
        def _(c):
            @pl.when(z == 0)
            def _():
                rightward(app, z, half + c * piece).start()

            @pl.when(z == last)
            def _():
                leftward(app, z, c * piece).start()

    keep = pltpu.make_async_copy(app, app_hbm, out_sem)
    keep.start()

    def gram(slot, source, begin, fresh):
        into = pl.ds(pl.multiple_of(slot * width, width), width)
        rows = pl.ds(pl.multiple_of(begin, half), half)
        here = (app_h[rows, :], app_l[rows, :])
        there = here if source is None else split(source[slot, rows, :])
        value = dot3(there, here, CONTRACT_ROWS)
        part[into, :] = value if fresh else part[into, :] + value

    def share(k):
        to = (leaf + k) % n_leaf
        return pltpu.make_async_remote_copy(
            src_ref=part.at[pl.ds(pl.multiple_of(to * slab, slab), slab)],
            dst_ref=shares.at[k],
            send_sem=share_send.at[k],
            recv_sem=share_recv.at[k],
            device_id={"leaf": to, "probe": z},
            device_id_type=MESH,
        )

    def give(slot):
        @pl.loop(0, fan)
        def _(c):
            to = slot * fan + c

            @pl.when(to != leaf)
            def _():
                share((to - leaf + n_leaf) % n_leaf).start()

    part[...] = jnp.zeros_like(part)

    @pl.loop(0, 2)
    def _(h):
        gram(z, None, h * half, False)

    give(z)

    @pl.loop(1, n_probe)
    def _(d):
        from_left = (z - d >= 0) & ((z < last) | (d > 1) | (not ends))
        from_right = (z + d <= last) & ((z > 0) | (d > 1) | (not ends))
        low_slot, high_slot = jnp.maximum(z - d, 0), jnp.minimum(z + d, last)

        @pl.loop(0, pieces)
        def _(c):
            up, low = c * piece, half + c * piece

            @pl.when(from_left)
            def _():
                rightward(got, low_slot, up).wait_recv()

                @pl.when(z < last)
                def _():
                    rightward(got, low_slot, up).start()

            @pl.when(from_right)
            def _():
                leftward(got, high_slot, low).wait_recv()

                @pl.when(z > 0)
                def _():
                    leftward(got, high_slot, low).start()

        @pl.loop(0, 2)
        def _(h):
            @pl.when(jnp.where(h == 0, from_left, from_right))
            def _():
                slot = jnp.where(h == 0, low_slot, high_slot)
                gram(slot, got, h * half, False)
                whole = (d > 1) | jnp.where(h == 0, z != 1, z != last - 1) | (not ends)

                @pl.when(whole)
                def _():
                    give(slot)

    if ends:
        at_low, at_high = z == 1, z == last - 1

        @pl.loop(0, pieces)
        def _(c):
            @pl.when(at_low)
            def _():
                rightward(got, z - 1, half + c * piece).wait_recv()

            @pl.when(at_high)
            def _():
                leftward(got, z + 1, c * piece).wait_recv()

        @pl.loop(0, 2)
        def _(h):
            @pl.when(jnp.where(h == 0, at_high, at_low))
            def _():
                slot = jnp.where(h == 0, jnp.minimum(z + 1, last), jnp.maximum(z - 1, 0))
                gram(slot, got, h * half, False)
                give(slot)

    total[...] = part[pl.ds(pl.multiple_of(leaf * slab, slab), slab), :]

    def holds(slot):
        return (not ends) | (((z > 0) | (slot != 1)) & ((z < last) | (slot != last - 1)))

    @pl.when(holds(a))
    def _():
        @pl.loop(1, n_leaf)
        def _(k):
            share(k).wait_recv()
            total[...] = total[...] + shares[k]

    scale = 1.0 / (points * n_leaf)

    tile = extra.shape[1]

    def trade(c, at):
        return pltpu.make_async_remote_copy(
            src_ref=total if tile == width else total.at[:, pl.ds(pl.multiple_of(c * tile, tile), tile)],
            dst_ref=extra.at[pl.ds(pl.multiple_of(at * slab, slab), slab)],
            send_sem=extra_send.at[c],
            recv_sem=extra_recv.at[at],
            device_id={"leaf": z * fan + c, "probe": a},
            device_id_type=MESH,
        )

    @pl.when(a != z)
    def _():
        @pl.loop(0, fan)
        def _(c):
            trade(c, b).start()

        @pl.loop(0, fan)
        def _(c):
            trade(c, c).wait_recv()

        turned[...] = extra[...].T
        skip = 0 if tile == slab else pl.multiple_of(b * slab, slab)
        gram_ref[...] = (total[...] + turned[pl.ds(skip, slab), :]) * scale

        @pl.loop(0, fan)
        def _(c):
            trade(c, b).wait_send()

    @pl.when(a == z)
    def _():
        gram_ref[...] = total[...] * scale

    @pl.loop(0, pieces)
    def _(c):
        up, low = c * piece, half + c * piece

        @pl.when(sends_right)
        def _():
            rightward(app, z, up).wait_send()

        @pl.when(sends_left)
        def _():
            leftward(app, z, low).wait_send()

        if ends:

            @pl.when(z == 0)
            def _():
                rightward(app, z, low).wait_send()

            @pl.when(z == last)
            def _():
                leftward(app, z, up).wait_send()

        @pl.loop(1, n_probe)
        def _(d):
            @pl.when((z - d >= 0) & (z < last))
            def _():
                rightward(got, jnp.maximum(z - d, 0), up).wait_send()

            @pl.when((z + d <= last) & (z > 0))
            def _():
                leftward(got, jnp.minimum(z + d, last), low).wait_send()

    @pl.loop(1, n_leaf)
    def _(k):
        @pl.when(holds(((leaf + k) % n_leaf) // fan))
        def _():
            share(k).wait_send()

    keep.wait()


def ring(n_leaf, n_probe, leaf_blocks, block_mask, row_factor_stack, column_factor_stack, probes):
    depth, points, rank = row_factor_stack.shape
    width = probes.shape[1]
    slab = n_probe * width // n_leaf
    fan = n_leaf // n_probe
    pieces = 4
    tile = slab if slab % 128 == 0 else width
    f32, bf16 = jnp.float32, jnp.bfloat16
    dma = pltpu.SemaphoreType.DMA
    hbm = pl.BlockSpec(memory_space=pltpu.HBM)
    return pl.pallas_call(
        functools.partial(ring_kernel, n_leaf, n_probe, pieces),
        out_shape=(
            jax.ShapeDtypeStruct((points, width), f32),
            jax.ShapeDtypeStruct((slab, width), f32),
        ),
        in_specs=[pl.BlockSpec(memory_space=pltpu.SMEM), hbm, hbm, hbm, hbm],
        out_specs=(hbm, pl.BlockSpec(memory_space=pltpu.VMEM)),
        scratch_shapes=[
            pltpu.VMEM((points, points), f32),
            pltpu.VMEM((depth, points, rank), f32),
            pltpu.VMEM((depth, points, rank), f32),
            pltpu.VMEM((points, width), f32),
            pltpu.VMEM((points, width), bf16),
            pltpu.VMEM((points, width), bf16),
            pltpu.VMEM((depth, rank, width), f32),
            pltpu.VMEM((depth * (depth + 1) // 2, rank, width), f32),
            pltpu.VMEM((depth * rank, width), bf16),
            pltpu.VMEM((depth * rank, width), bf16),
            pltpu.VMEM((points, width), f32),
            pltpu.VMEM((points, width), bf16),
            pltpu.VMEM((points, width), bf16),
            pltpu.VMEM((n_probe, points, width), f32),
            pltpu.VMEM((n_probe * width, width), f32),
            pltpu.VMEM((n_leaf, slab, width), f32),
            pltpu.VMEM((slab, width), f32),
            pltpu.VMEM((width, tile), f32),
            pltpu.VMEM((tile, width), f32),
            pltpu.VMEM((points // 2, points), bf16),
            pltpu.VMEM((points // 2, points), bf16),
            dma((4,)),
            dma,
            dma((depth,)),
            dma((depth,)),
            dma((n_probe, 2 * pieces)),
            dma((n_probe, 2 * pieces)),
            dma((n_probe, 2 * pieces)),
            dma((n_probe, 2 * pieces)),
            dma((n_leaf,)),
            dma((n_leaf,)),
            dma((fan,)),
            dma((fan,)),
        ],
        compiler_params=pltpu.CompilerParams(
            collective_id=0, has_side_effects=True, vmem_limit_bytes=67043328
        ),
    )(block_mask, leaf_blocks, row_factor_stack, column_factor_stack, probes)


def hub_kernel(
    n_leaf, n_probe, parts,
    mask_hbm, block_hbm, row_hbm, col_hbm, probe_hbm, app, gram_ref,
    mask, block, row, col, probe, probe_h, probe_l, block_h, block_l, row_h, row_l,
    own, pair_in, pair_sum, group_in, sib, sib_h, sib_l, app_h, app_l, near_other,
    got_probe, got_sib, got_turned, turned, pairs, arrived, summed, straight, crossed, diag, diag_in, diag_sum, shares,
    load_sem, pair_send, pair_recv, group_send, group_recv, half_send, half_recv,
    probe_send, probe_recv, sib_send, sib_recv, turned_send, turned_recv,
    part_send, part_recv, straight_send, straight_recv, crossed_send, crossed_recv, swap_send, swap_recv, share_send, share_recv, ready, go,
):
    depth, rank = row.shape[0], row.shape[2]
    points, width = app.shape
    side = mask.shape[1]
    span = points // side
    half = points // 2
    leaf, z = lax.axis_index("leaf"), lax.axis_index("probe")
    slab = n_probe * width // n_leaf
    fan = n_leaf // n_probe
    chunk = width // parts
    last = n_probe - 1
    h = n_probe // 2
    teams = n_leaf // 2
    split_rank = rank // 2
    flow = leaf % 2
    team = leaf // 2
    mate = leaf + 1 - 2 * flow
    a, b = leaf // fan, leaf % fan

    def along(direction, position):
        return jnp.where(direction == 0, position, last - position)

    q = along(flow, z)
    is_hub = q == h
    hub = along(flow, h)

    def remote(src, dst, send, recv, to_leaf, to_z):
        return pltpu.make_async_remote_copy(
            src_ref=src, dst_ref=dst, send_sem=send, recv_sem=recv,
            device_id={"leaf": to_leaf, "probe": to_z}, device_id_type=MESH,
        )

    loads = [
        pltpu.make_async_copy(source, target, load_sem.at[i])
        for i, (source, target) in enumerate(
            ((probe_hbm, probe), (col_hbm, col), (block_hbm, block), (row_hbm, row), (mask_hbm, mask))
        )
    ]
    loads[0].start()
    loads[1].start()

    barrier = pltpu.get_barrier_semaphore()

    @pl.loop(1, n_leaf)
    def _(k):
        pl.semaphore_signal(
            barrier, inc=1, device_id={"leaf": (leaf + k) % n_leaf, "probe": z}, device_id_type=MESH
        )

    @pl.loop(0, n_probe)
    def _(k):
        @pl.when((k != z) & (jnp.abs(k - z) < last))
        def _():
            pl.semaphore_signal(barrier, inc=1, device_id={"leaf": leaf, "probe": k}, device_id_type=MESH)

    pl.semaphore_wait(barrier, n_leaf - 1 + last - jnp.where((z == 0) | (z == last), 1, 0))

    sides = [k for k in range(n_probe) if abs(k - h) == 1]
    distant = [k for k in range(n_probe) if abs(k - h) > 1]
    is_side = jnp.abs(q - h) == 1
    place = jnp.where(q > h, 1, 0)

    def give_probe(slot):
        return remote(probe_hbm, got_probe.at[slot], probe_send, probe_recv.at[slot], leaf, hub)

    @pl.when(is_side)
    def _():
        give_probe(place).start()

    loads[0].wait()
    ph, plo = split(probe[...])
    probe_h[...] = ph
    probe_l[...] = plo
    loads[1].wait()
    loads[4].start()
    loads[2].start()
    loads[3].start()
    columns = jnp.concatenate([col[level] for level in range(depth)], axis=1)
    own[...] = dot3(split(columns), (probe_h[...], probe_l[...]), CONTRACT_ROWS).reshape(own.shape)

    @pl.loop(1, n_leaf)
    def _(k):
        pl.semaphore_signal(
            ready, inc=1, device_id={"leaf": (leaf + k) % n_leaf, "probe": z}, device_id_type=MESH
        )

    first_level = remote(own.at[0], sib.at[0], pair_send.at[0], pair_recv.at[0], mate, z)
    upper_levels = remote(
        own.at[pl.ds(1, depth - 1), pl.ds(pl.multiple_of((1 - flow) * split_rank, split_rank), split_rank)],
        pair_in, pair_send.at[1], pair_recv.at[1], mate, z,
    )
    upper_levels.start()
    first_level.start()
    mine = pl.ds(pl.multiple_of(flow * split_rank, split_rank), split_rank)

    def to_group(level, k):
        members = 2 ** (level - 1)
        base = leaf - leaf % 2**level + (1 - 2 * ((leaf // 2**level) % 2)) * 2**level
        from_slot = members - 1 + (leaf % 2**level) // 2
        return remote(
            pair_sum.at[level - 1], group_in.at[from_slot],
            group_send.at[members - 1 + k], group_recv.at[from_slot], base + 2 * k + flow, z,
        )

    def from_group(level, k):
        members = 2 ** (level - 1)
        return remote(
            pair_sum.at[level - 1], group_in.at[members - 1 + k],
            group_send.at[members - 1 + k], group_recv.at[members - 1 + k], mate, z,
        )

    upper_levels.wait_recv()
    for level in range(1, depth):
        pair_sum[level - 1] = own[level, mine, :] + pair_in[level - 1]
    for level in reversed(range(1, depth)):
        @pl.loop(0, 2 ** (level - 1))
        def _(k):
            to_group(level, k).start()

    loads[4].wait()
    loads[2].wait()

    @pl.loop(0, side)
    def _(line):
        rows = pl.ds(pl.multiple_of(line * span, span), span)
        strips = [
            block[rows, j * span : (j + 1) * span] * mask[0, line, j].astype(jnp.float32)
            for j in range(side)
        ]
        block_h[rows, :], block_l[rows, :] = split(jnp.concatenate(strips, axis=1))

    def near(target):
        @pl.loop(0, 2)
        def _(i):
            rows = pl.ds(pl.multiple_of(i * half, half), half)
            target[rows, :] = dot3(
                (block_h[rows, :], block_l[rows, :]), (probe_h[...], probe_l[...]), PLAIN
            )

    near(app)
    loads[3].wait()
    for level in range(depth):
        row_h[:, level * rank : (level + 1) * rank], row_l[:, level * rank : (level + 1) * rank] = split(row[level])

    for level in range(1, depth):
        @pl.loop(0, 2 ** (level - 1))
        def _(k):
            from_group(level, k).wait_recv()

        begin = 2 ** (level - 1) - 1
        value = group_in[begin]
        for k in range(1, 2 ** (level - 1)):
            value = value + group_in[begin + k]
        sib[level, mine, :] = value

    half_copy = remote(
        sib.at[pl.ds(1, depth - 1), mine], sib.at[pl.ds(1, depth - 1), mine], half_send, half_recv, mate, z
    )
    half_copy.start()
    first_level.wait_recv()
    half_copy.wait_recv()

    def give_sib(slot, level):
        return remote(
            sib.at[level], got_sib.at[slot, level], sib_send.at[level], sib_recv.at[slot, level], leaf, hub
        )

    @pl.when(is_side)
    def _():
        for level in range(depth):
            give_sib(place, level).start()

    def far(source, base, target, slot):
        flat = source[...].reshape(depth * rank, width)
        sib_h[...], sib_l[...] = split(flat)

        @pl.loop(0, 2)
        def _(i):
            rows = pl.ds(pl.multiple_of(i * half, half), half)
            value = base[rows, :] + dot3((row_h[rows, :], row_l[rows, :]), (sib_h[...], sib_l[...]), PLAIN)
            if target is not None:
                target[rows, :] = value
            app_h[slot, rows, :], app_l[slot, rows, :] = split(value)

    far(sib, app, app, h)

    def rows_of(c):
        return pl.ds(pl.multiple_of(c * chunk, chunk), chunk)

    def give_turned(c):
        return remote(
            turned.at[rows_of(c)], got_turned.at[rows_of(c)], turned_send.at[c], turned_recv.at[c], leaf, hub
        )

    @pl.when(q == 0)
    def _():
        per = 128 // chunk
        for strip in range(width // 128):
            lanes = slice(strip * 128, (strip + 1) * 128)
            turned[lanes, :] = app[:, lanes].T

    diag[...] = dot3((app_h[h], app_l[h]), (app_h[h], app_l[h]), CONTRACT_ROWS)

    def slab_of(k):
        return pl.ds(pl.multiple_of(k * slab, slab), slab)

    swap = remote(diag.at[slab_of(1 - flow)], diag_in, swap_send, swap_recv, mate, z)
    swap.start()
    share = remote(diag_sum, shares.at[team], share_send, share_recv.at[team], z * fan + flow, z)

    def give_share():
        swap.wait_recv()
        diag_sum[...] = diag[slab_of(flow), :] + diag_in[...]

        @pl.when(a != z)
        def _():
            share.start()

    order = [(i, j) for j in range(n_probe) for i in range(j)]
    seat = {(i, j): i if j == i + 1 else j for i, j in order}

    def part_copy(i, j, c):
        pid = order.index((i, j))
        return remote(
            pairs.at[pid, rows_of(c)], arrived.at[i, team, rows_of(c)],
            part_send.at[pid, c], part_recv.at[i, team, c], along(flow, seat[i, j]) * fan + 1 - flow, z,
        )

    give_share()

    @pl.when(is_side)
    def _():
        for level in range(depth - 1):
            give_sib(place, level).wait_send()

        @pl.when(q < h)
        def _():
            pl.semaphore_signal(go, inc=1, device_id={"leaf": leaf, "probe": along(flow, 0)}, device_id_type=MESH)

        @pl.when(q > h)
        def _():
            pl.semaphore_signal(go, inc=1, device_id={"leaf": mate, "probe": z}, device_id_type=MESH)

        for level in range(depth - 1, depth):
            give_sib(place, level).wait_send()

    @pl.when(q == 0)
    def _():
        pl.semaphore_wait(go, 2)

        @pl.loop(0, parts)
        def _(c):
            give_turned(c).start()

    @pl.when(is_hub)
    def _():
        for slot, k in enumerate(sides):
            give_probe(slot).wait_recv()
            ph, plo = split(got_probe[slot])
            probe_h[...] = ph
            probe_l[...] = plo
            near(near_other.at[slot])

        def pair(i, j):
            pairs[order.index((i, j))] = dot3((app_h[i], app_l[i]), (app_h[j], app_l[j]), CONTRACT_ROWS)

            @pl.loop(0, parts)
            def _(c):
                part_copy(i, j, c).start()

        for slot, k in enumerate(sides):
            for level in range(depth):
                give_sib(slot, level).wait_recv()
            far(got_sib.at[slot], near_other.at[slot], None, k)
            if slot == 1:
                pair(*sides)
            pair(min(k, h), max(k, h))

    def late(c):
        @pl.when(is_hub)
        def _():
            give_turned(c).wait_recv()
            high, low = split(got_turned[rows_of(c), :])
            stacked = jnp.concatenate([high, low], axis=0)
            dot = functools.partial(lax.dot_general, dimension_numbers=PLAIN, preferred_element_type=jnp.float32)
            for j in range(1, n_probe):
                both = dot(stacked, app_h[j])
                pairs[order.index((0, j)), rows_of(c), :] = both[:chunk] + (dot(high, app_l[j]) + both[chunk:])
                part_copy(0, j, c).start()

    current = 1 - flow
    collects = z == along(current, h)
    position = along(current, a)

    def arrival(i, m, c):
        return remote(
            arrived.at[i, m, rows_of(c)], arrived.at[i, m, rows_of(c)],
            part_send.at[0, c], part_recv.at[i, m, c], mate, z,
        )

    per_slab = slab // chunk

    def holds(i):
        match = [j for j in range(n_probe) if (i, j) in seat]
        found = jnp.bool_(False)
        partner = position
        for j in match:
            found = found | (position == seat[i, j])
            if seat[i, j] != j:
                partner = jnp.where(position == seat[i, j], j, partner)
        return collects & found, along(current, partner)

    def kept(i, c):
        return (seat.get((i, h)) == i) & (position == i) & (c // per_slab == flow)

    def send_crossed(i, c, k):
        return remote(
            summed.at[i, rows_of(c), k * slab : (k + 1) * slab], crossed.at[rows_of(c)],
            crossed_send.at[i, c, k], crossed_recv.at[c], holds(i)[1] * fan + k, along(current, i),
        )

    def send_straight(i, c):
        return remote(
            summed.at[i, rows_of(c)], straight.at[rows_of(c % per_slab)],
            straight_send.at[i, c], straight_recv.at[c % per_slab],
            along(current, i) * fan + c // per_slab, holds(i)[1],
        )

    def collect(i, c):
        @pl.when(holds(i)[0])
        def _():
            for m in range(teams):
                arrival(i, m, c).wait_recv()
            value = arrived[i, 0, rows_of(c), :]
            for m in range(1, teams):
                value = value + arrived[i, m, rows_of(c), :]
            summed[i, rows_of(c), :] = value
            for k in range(fan):
                send_crossed(i, c, k).start()

            @pl.when(kept(i, c))
            def _():
                straight[rows_of(c % per_slab), :] = value

            @pl.when(jnp.logical_not(kept(i, c)))
            def _():
                send_straight(i, c).start()

    def collect_all(i, begin, end):
        @pl.loop(begin, end)
        def _(c):
            collect(i, c)

    @pl.loop(0, parts)
    def _(c):
        late(c)

    pl.semaphore_wait(ready, n_leaf - 1)
    collect_all(1, 0, parts)
    collect_all(0, 0, 1)
    for i in range(2, n_probe - 1):
        collect_all(i, 0, parts)
    collect_all(0, 1, parts)

    scale = 1.0 / (points * n_leaf)

    @pl.when(a == z)
    def _():
        shares[team] = diag_sum[...]

        @pl.loop(1, teams)
        def _(k):
            other = (team + k) % teams
            remote(diag_sum, shares.at[other], share_send, share_recv.at[other], mate, z).wait_recv()

        value = shares[0]
        for k in range(1, teams):
            value = value + shares[k]
        gram_ref[...] = value * scale

    @pl.when(a != z)
    def _():
        back = jnp.where(z < a, 0, 1)

        @pl.loop(0, parts)
        def _(c):
            remote(
                summed.at[0, rows_of(c), 0:slab], crossed.at[rows_of(c)],
                crossed_send.at[0, c, 0], crossed_recv.at[c], mate, z,
            ).wait_recv()

        stays = (along(1 - back, a) == 1) & (along(1 - back, z) == h) & (flow == back)

        @pl.loop(0, jnp.where(stays, 0, per_slab))
        def _(c):
            remote(
                summed.at[0, rows_of(c)], straight.at[rows_of(c)],
                straight_send.at[0, c], straight_recv.at[c], mate, z,
            ).wait_recv()

        gram_ref[...] = (straight[...] + crossed[...].T) * scale

    first_level.wait_send()
    upper_levels.wait_send()
    half_copy.wait_send()
    for level in range(1, depth):
        @pl.loop(0, 2 ** (level - 1))
        def _(k):
            to_group(level, k).wait_send()

    @pl.when(is_side)
    def _():
        give_probe(place).wait_send()

    @pl.when(q == 0)
    def _():
        @pl.loop(0, parts)
        def _(c):
            give_turned(c).wait_send()

    swap.wait_send()

    @pl.when(a != z)
    def _():
        share.wait_send()

    @pl.when(is_hub)
    def _():
        for i, j in order:

            @pl.loop(0, parts)
            def _(c):
                part_copy(i, j, c).wait_send()

    for i in range(n_probe - 1):

        @pl.when(holds(i)[0])
        def _():
            @pl.loop(0, parts)
            def _(c):
                for k in range(fan):
                    send_crossed(i, c, k).wait_send()

                @pl.when(jnp.logical_not(kept(i, c)))
                def _():
                    send_straight(i, c).wait_send()


def hub_local(n_leaf, n_probe, leaf_blocks, block_mask, row_factor_stack, column_factor_stack, probes):
    depth, points, rank = row_factor_stack.shape
    width = probes.shape[1]
    slab = n_probe * width // n_leaf
    fan = n_leaf // n_probe
    parts = 2 * width // slab
    teams = n_leaf // 2
    count = n_probe * (n_probe - 1) // 2
    f32, bf16 = jnp.float32, jnp.bfloat16
    dma = pltpu.SemaphoreType.DMA
    hbm = pl.BlockSpec(memory_space=pltpu.HBM)
    groups = 2 ** (depth - 1) - 1
    return pl.pallas_call(
        functools.partial(hub_kernel, n_leaf, n_probe, parts),
        out_shape=(
            pltpu.VMEM((points, width), f32),
            pltpu.VMEM((slab, width), f32),
        ),
        in_specs=[hbm] * 5,
        out_specs=(pl.BlockSpec(memory_space=pltpu.VMEM), pl.BlockSpec(memory_space=pltpu.VMEM)),
        scratch_shapes=[
            pltpu.SMEM(block_mask.shape, block_mask.dtype),
            pltpu.VMEM((points, points), f32),
            pltpu.VMEM((depth, points, rank), f32),
            pltpu.VMEM((depth, points, rank), f32),
            pltpu.VMEM((points, width), f32),
            pltpu.VMEM((points, width), bf16),
            pltpu.VMEM((points, width), bf16),
            pltpu.VMEM((points, points), bf16),
            pltpu.VMEM((points, points), bf16),
            pltpu.VMEM((points, depth * rank), bf16),
            pltpu.VMEM((points, depth * rank), bf16),
            pltpu.VMEM((depth, rank, width), f32),
            pltpu.VMEM((depth - 1, rank // 2, width), f32),
            pltpu.VMEM((depth - 1, rank // 2, width), f32),
            pltpu.VMEM((groups, rank // 2, width), f32),
            pltpu.VMEM((depth, rank, width), f32),
            pltpu.VMEM((depth * rank, width), bf16),
            pltpu.VMEM((depth * rank, width), bf16),
            pltpu.VMEM((n_probe, points, width), bf16),
            pltpu.VMEM((n_probe, points, width), bf16),
            pltpu.VMEM((2, points, width), f32),
            pltpu.VMEM((2, points, width), f32),
            pltpu.VMEM((2, depth, rank, width), f32),
            pltpu.VMEM((width, points), f32),
            pltpu.VMEM((width, points), f32),
            pltpu.VMEM((count, width, width), f32),
            pltpu.VMEM((n_probe - 1, teams, width, width), f32),
            pltpu.VMEM((n_probe - 1, width, width), f32),
            pltpu.VMEM((slab, width), f32),
            pltpu.VMEM((width, slab), f32),
            pltpu.VMEM((width, width), f32),
            pltpu.VMEM((slab, width), f32),
            pltpu.VMEM((slab, width), f32),
            pltpu.VMEM((teams, slab, width), f32),
            dma((5,)),
            dma((2,)),
            dma((2,)),
            dma((groups,)),
            dma((groups,)),
            dma,
            dma,
            dma,
            dma((2,)),
            dma((depth,)),
            dma((2, depth)),
            dma((parts,)),
            dma((parts,)),
            dma((count, parts)),
            dma((n_probe - 1, teams, parts)),
            dma((n_probe - 1, parts)),
            dma((slab * parts // width,)),
            dma((n_probe - 1, parts, fan)),
            dma((parts,)),
            dma,
            dma,
            dma,
            dma((teams,)),
            pltpu.SemaphoreType.REGULAR,
            pltpu.SemaphoreType.REGULAR,
        ],
        compiler_params=pltpu.CompilerParams(
            collective_id=0, has_side_effects=True, vmem_limit_bytes=56 * 2**20
        ),
    )(block_mask, leaf_blocks, row_factor_stack, column_factor_stack, probes)


def local(n_leaf, n_probe, *arrays):
    width = arrays[-1].shape[1]
    whole_lanes = (n_probe * width) % (128 * n_leaf) == 0
    if n_probe == 4 and n_leaf == 2 * n_probe and whole_lanes:
        return hub_local(n_leaf, n_probe, *arrays)
    return ring(n_leaf, n_probe, *arrays)


def solution(mesh):
    return jax.shard_map(
        functools.partial(local, mesh.shape["leaf"], mesh.shape["probe"]),
        mesh=mesh,
        in_specs=(
            P("leaf", None),
            P("leaf", None, None),
            P(None, "leaf", None),
            P(None, "leaf", None),
            P("leaf", "probe"),
        ),
        out_specs=(P("leaf", "probe"), P("leaf", "probe")),
        check_vma=False,
    )
```
